32 devices in a mesh: case: 4 (over z), span: 2 (over x), vert: 4 (over y, core).
Axes of the slice: x: 2, y: 2, z: 4, core: 2. Of those that a mesh axis runs over, the one named last changes fastest.
Arguments:
- state: float32 [8, 4, 16, 32, 512], P('case', None, 'span', 'vert'), may hold values from -3 to 4.5
- turbine_x: int32 [8, 6], P('case'), may hold values from 128 to 511
- turbine_y: int32 [8, 6], P('case'), may hold values from 0 to 15
- yaw_index: int32 [8], P('case'), may hold values from 0 to 7
Outputs:
- final_state: float32 [8, 4, 16, 32, 512], P('case', None, 'span', 'vert')
The draws below stay inside these ranges and needn't reach their ends.
All inputs are finite; a program needn't handle non-finite values.
Results may differ from the reference program's by a relative error of at most 0.0003.
Values sent between devices are 32-bit elements; how exact they have to be, the bound alone decides.
No kernel may reach another device: no remote copies, remote signals or barrier semaphores. Data moves between devices by JAX's collectives and lax.ppermute only.
A program may use at most 64 MiB of HBM per device.

```python
import jax
import jax.numpy as jnp
from jax import lax

X = 512
FIELDS = 4
STEPS = 3
NT = 6
DISK = 8
DOM = 8
NY = 16
NZ = 32


def draw_state(key, part):
    shape = (DOM, FIELDS, NY, NZ, X)
    noise = 0.75 * jax.random.normal(key, shape, jnp.float32)
    noise = jnp.clip(noise, -3.0, 3.0)
    offset = jnp.array([0.0, 1.5, 0.0, 0.0], jnp.float32)[None, :, None, None, None]
    return noise + offset


def touch_ends(result, key, least, top_value):
    longest = result.shape.index(max(result.shape))
    spots = []
    for shift in (0, 1):
        where = [jax.random.randint(jax.random.fold_in(key, axis), (), 0, length) for axis, length in enumerate(result.shape)]
        where[longest] = (where[longest] + shift) % result.shape[longest]
        spots.append(tuple(where))
    return result.at[spots[0]].set(least).at[spots[1]].set(top_value)


def setup_inputs(seed: int = 0) -> dict:
    keys = jax.random.split(jax.random.key(seed), 5)
    return {
        "state": draw_state(jax.random.fold_in(keys[4], 71), 0),
        "turbine_x": touch_ends(jax.random.randint(keys[1], (DOM, NT), X // 4, X), jax.random.fold_in(keys[1], 1), X // 4, X - 1).astype(jnp.int32),
        "turbine_y": touch_ends(jax.random.randint(keys[2], (DOM, NT), 0, NY), jax.random.fold_in(keys[2], 1), 0, NY - 1).astype(jnp.int32),
        "yaw_index": touch_ends(jax.random.randint(keys[3], (DOM,), 0, 8), jax.random.fold_in(keys[3], 1), 0, 7).astype(jnp.int32),
    }


U_MEAN = 1.0
VISC = 0.04
THRUST = 0.75
TIME_STEP = 0.1
YAW_STEP = 0.15

def tendency(center, east, west, north, south, upper, lower, weight, cos_yaw, sin_yaw):
    grad_x = (east - west) * 0.5
    grad_y = (north - south) * 0.5
    grad_z = (upper - lower) * 0.5
    laplace = east + west + north + south + upper + lower - 6.0 * center
    vel_u = center[..., 1, :, :, :]
    vel_v = center[..., 2, :, :, :]
    vel_w = center[..., 3, :, :, :]
    dux = grad_x[..., 1, :, :, :]
    dvy = grad_y[..., 2, :, :, :]
    dwz = grad_z[..., 3, :, :, :]
    duy = grad_y[..., 1, :, :, :]
    duz = grad_z[..., 1, :, :, :]
    strain = dux * dux + dvy * dvy + dwz * dwz + duy * duy + duz * duz
    viscous = VISC * jnp.sqrt(1.0 + strain)
    speed = U_MEAN + vel_u
    flow = -(jnp.expand_dims(speed, -4) * grad_x + jnp.expand_dims(vel_v, -4) * grad_y + jnp.expand_dims(vel_w, -4) * grad_z)
    flow = flow + jnp.expand_dims(viscous, -4) * laplace
    normal = speed * cos_yaw + vel_v * sin_yaw
    thrust = THRUST * normal * jnp.abs(normal) * weight
    extra = jnp.stack([-(dux + dvy + dwz), -grad_x[..., 0, :, :, :] - thrust * cos_yaw, -grad_y[..., 0, :, :, :] - thrust * sin_yaw, -grad_z[..., 0, :, :, :]], axis=-4)
    return flow + extra

def neighbours(fields):
    east = jnp.roll(fields, -1, axis=3)
    west = jnp.roll(fields, 1, axis=3)
    north = jnp.roll(fields, -1, axis=1)
    south = jnp.roll(fields, 1, axis=1)
    padded = jnp.pad(fields, ((0, 0), (0, 0), (1, 1), (0, 0)))
    return (east, west, north, south, padded[:, :, 2:, :], padded[:, :, :-2, :])

def domain_step(fields, tx_row, ty_row, yaw, domain):
    along_x = jnp.arange(X, dtype=jnp.int32)
    along_y = jnp.arange(NY, dtype=jnp.int32)
    along_z = jnp.arange(NZ, dtype=jnp.int32)
    hit_x = (along_x[None, :] == tx_row[:, None]).astype(jnp.float32)
    hit_y = ((along_y[None, :] - ty_row[:, None]) % NY < DISK).astype(jnp.float32)
    plane = jnp.dot(hit_y.T, hit_x, precision=lax.Precision.HIGHEST)
    lower_half = (along_z < NZ // 2).astype(jnp.float32)
    active = (domain > 0).astype(jnp.float32)
    weight = plane[:, None, :] * lower_half[None, :, None] * active
    angle = (yaw.astype(jnp.float32) - 3.5) * YAW_STEP
    cos_yaw = jnp.cos(angle)
    sin_yaw = jnp.sin(angle)

    def rate(values):
        return tendency(values, *neighbours(values), weight, cos_yaw, sin_yaw)
    first = rate(fields)
    middle = fields + TIME_STEP * first
    second = rate(middle)
    return fields + 0.5 * TIME_STEP * (first + second)

def reference(state, turbine_x, turbine_y, yaw_index):
    width = X // 4
    ramp = 0.5 * (1.0 - jnp.cos(jnp.pi * (jnp.arange(width, dtype=jnp.float32) + 1.0) / width))
    domains = jnp.arange(DOM, dtype=jnp.int32)
    for step in range(STEPS):
        state = lax.map(lambda items: domain_step(*items), (state, turbine_x, turbine_y, yaw_index, domains))
        front = state[..., :width]
        source = front[0:1]
        front = front + ramp * (source - front)
        state = jnp.concatenate([front, state[..., width:]], axis=4)
    return state
```

```python
import functools

import jax
import jax.numpy as jnp
from jax import lax
from jax.experimental import pallas as pl
from jax.experimental.pallas import tpu as pltpu
from jax.sharding import PartitionSpec as P

STEPS = 3
DISK = 8
LANES = 128
HALO = 2 * STEPS

U_MEAN = 1.0
VISC = 0.04
THRUST = 0.75
TIME_STEP = 0.1
YAW_STEP = 0.15

ROW0 = 8
STRIP = 16


def flat(block):
    f, y, z, x = block.shape
    t = x // LANES
    return block.reshape(f, y, z, t, LANES).transpose(0, 1, 3, 2, 4).reshape(f * y * t * z, LANES)


def unflat(rows, f, y, z, x):
    t = x // LANES
    lead = rows.shape[:-2]
    n = len(lead)
    a = rows.reshape(*lead, f, y, t, z, LANES)
    a = jnp.swapaxes(a, n + 2, n + 3)
    return a.reshape(*lead, f, y, z, x)


def pack_kernel(dims, src_ref, out_ref):
    fields, ry, rz, tiles = dims
    lane = lax.broadcasted_iota(jnp.int32, (rz, LANES), 1)
    for f in range(fields):
        strip = jnp.zeros((rz, LANES), jnp.float32)
        for y in range(ry):
            row = (f * ry + y) * tiles * rz
            out_ref[pl.ds((f * (ry + 1) + y) * rz, rz), :] = src_ref[pl.ds(row, rz), :]
            after = src_ref[pl.ds(row + rz, rz), :]
            before = src_ref[pl.ds(row + (tiles - 1) * rz, rz), :]
            both = jnp.where(lane < LANES // 2, after, before)
            both = pltpu.roll(both, (HALO + STRIP * y) % LANES, 1)
            here = (lane >= STRIP * y) & (lane < STRIP * y + 2 * HALO)
            strip = jnp.where(here, both, strip)
        out_ref[pl.ds((f * (ry + 1) + ry) * rz, rz), :] = strip


def main_kernel(
    dims, ints, reals, own, got, in_own, in_got, out_own, out_got, p_own, p_in, p_out, ramp_ref,
    mine_ref, send_ref, q, m, pq, pm, tmp, wgt,
):
    fields, ry, rz, tiles, nt = dims
    ext = rz + 2 * HALO
    total_y = 2 * ry
    groups = total_y // 8
    dlo, dhi, even, gate, y_off = (ints[i] for i in range(5))
    cos_yaw, sin_yaw, active = (reals[i] for i in range(3))
    lane = lax.broadcasted_iota(jnp.int32, (8, LANES), 1)
    sub = lax.broadcasted_iota(jnp.int32, (8, LANES), 0)
    first_lane = lane == 0
    last_lane = lane == LANES - 1

    def put(dst, f, t, z, group, value):
        dst[f, t, z, pl.ds(ROW0 + 8 * group, 8), :] = value
        if group == 0:
            dst[f, t, z, pl.ds(ROW0 + total_y, 1), :] = value[0:1]
        if group == groups - 1:
            dst[f, t, z, pl.ds(ROW0 - 1, 1), :] = value[7:8]

    def fill(src, half, z_src, z_dst, count):
        def one(f, carry):
            for t in range(tiles):
                for k in range(count):
                    for g in range(ry // 8):
                        start = ((f * ry + 8 * g) * tiles + t) * rz + z_src + k
                        value = src[pl.ds(start, 8, stride=tiles * rz), :]
                        put(q, f, t, z_dst + k, half * (ry // 8) + g, value)
            return carry

        lax.fori_loop(0, fields, one, 0)

    def fill_fringe(src, half, z_src, z_dst, count):
        def one(f, carry):
            base = (half * fields + f) * (ry + 1) * rz
            strip = src[pl.ds(base + ry * rz, rz), :]
            for y in range(ry):
                tmp[pl.ds(y * rz, rz), :] = pltpu.roll(strip, (-(HALO + STRIP * y)) % LANES, 1)
            for k in range(count):
                for g in range(ry // 8):
                    start = base + 8 * g * rz + z_src + k
                    group = half * (ry // 8) + g
                    put(pq, f, 0, z_dst + k, group, src[pl.ds(start, 8, stride=rz), :])
                    value = tmp[pl.ds(8 * g * rz + z_src + k, 8, stride=rz), :]
                    put(pq, f, 1, z_dst + k, group, value)
            return carry

        lax.fori_loop(0, fields, one, 0)

    for half, src in enumerate((own, got)):
        fill(src, half, 0, HALO, rz)
    for half in range(2):
        fill_fringe(p_own, half, 0, HALO, rz)

    @pl.when(even == 1)
    def _():
        fill(out_own, 0, rz - HALO, 0, HALO)
        fill(out_got, 1, rz - HALO, 0, HALO)
        fill(in_own, 0, 0, HALO + rz, HALO)
        fill(in_got, 1, 0, HALO + rz, HALO)
        for half in range(2):
            fill_fringe(p_out, half, rz - HALO, 0, HALO)
            fill_fringe(p_in, half, 0, HALO + rz, HALO)

    @pl.when(even == 0)
    def _():
        fill(in_own, 0, rz - HALO, 0, HALO)
        fill(in_got, 1, rz - HALO, 0, HALO)
        fill(out_own, 0, 0, HALO + rz, HALO)
        fill(out_got, 1, 0, HALO + rz, HALO)
        for half in range(2):
            fill_fringe(p_in, half, rz - HALO, 0, HALO)
            fill_fringe(p_out, half, 0, HALO + rz, HALO)

    zero = jnp.zeros((ROW0 * 2 + total_y, LANES), jnp.float32)
    for ref, width in ((m, tiles), (pm, 2), (q, tiles), (pq, 2)):
        for z in (HALO - 1, HALO + rz):
            outside = (z < dlo) | (z >= dhi)

            def clear(ref=ref, width=width, z=z):
                for f in range(fields):
                    for t in range(width):
                        ref[f, t, z] = zero

            pl.when(outside)(clear)

    for t in range(1, tiles):
        for g in range(groups):
            acc = jnp.zeros((8, LANES), jnp.float32)
            y = y_off + 8 * g + sub
            for k in range(nt):
                hit = lax.rem(y - ints[5 + nt + k] + 2 * total_y, total_y) < DISK
                hit = hit & (lane + t * LANES == ints[5 + k])
                acc = acc + jnp.where(hit, 1.0, 0.0)
            acc = acc * active
            wgt[0, 0, t, g] = jnp.zeros((8, LANES), jnp.float32)
            wgt[0, 1, t, g] = jnp.zeros((8, LANES), jnp.float32)
            wgt[1, 0, t, g] = acc * (THRUST * cos_yaw)
            wgt[1, 1, t, g] = acc * (THRUST * sin_yaw)

    ramp = ramp_ref[...]

    def stage(src, base, dst, width, k, is_domain):
        second = k % 2 == 0
        dt = 0.5 * TIME_STEP if second else TIME_STEP
        half = 0.5 * dt
        root = dt ** 0.5
        cos_n = cos_yaw * (root / half)
        sin_n = sin_yaw * (root / half)

        def row(z, carry):
            if is_domain:
                on = jnp.where(z < gate, 1, 0)
            for g in range(groups):
                here = pl.ds(ROW0 + 8 * g, 8)
                north_rows = pl.ds(ROW0 + 8 * g + 1, 8)
                south_rows = pl.ds(ROW0 + 8 * g - 1, 8)

                def load(t):
                    c = [src[f, t % width, z, here, :] for f in range(fields)]
                    left = [pltpu.roll(a, LANES - 1, 1) for a in c]
                    right = [pltpu.roll(a, 1, 1) for a in c]
                    return c, left, right

                loaded = {}
                for t in (-1, 0):
                    loaded[t % width] = load(t)
                for t in range(width):
                    if (t + 1) % width not in loaded:
                        loaded[(t + 1) % width] = load(t + 1)
                    c, left, right = loaded[t]
                    left_next = loaded[(t + 1) % width][1]
                    right_prev = loaded[(t - 1) % width][2]
                    east = [jnp.where(last_lane, b, a) for a, b in zip(left, left_next)]
                    west = [jnp.where(first_lane, b, a) for a, b in zip(right, right_prev)]
                    gx, gy, gz, lap = [], [], [], []
                    for f in range(fields):
                        north = src[f, t, z, north_rows, :]
                        south = src[f, t, z, south_rows, :]
                        upper = src[f, t, z + 1, here, :]
                        lower = src[f, t, z - 1, here, :]
                        gx.append(east[f] - west[f])
                        gy.append(north - south)
                        gz.append(upper - lower)
                        around = ((east[f] + west[f]) + (north + south)) + (upper + lower)
                        lap.append(around - 6.0 * c[f])
                    speed = -half * U_MEAN - half * c[1]
                    vel_v = -half * c[2]
                    vel_w = -half * c[3]
                    strain = gx[1] * gx[1] + gy[2] * gy[2] + gz[3] * gz[3]
                    strain = strain + gy[1] * gy[1] + gz[1] * gz[1] + 4.0
                    viscous = (0.5 * VISC * dt) * (strain * lax.rsqrt(strain))
                    rate = [
                        speed * gx[f] + vel_v * gy[f] + vel_w * gz[f] + viscous * lap[f]
                        for f in range(fields)
                    ]
                    rate[0] = rate[0] - half * (gx[1] + gy[2] + gz[3])
                    rate[1] = rate[1] - half * gx[0]
                    rate[2] = rate[2] - half * gy[0]
                    rate[3] = rate[3] - half * gz[0]
                    if is_domain and t > 0:
                        normal = speed * cos_n + vel_v * sin_n
                        thrust = normal * jnp.abs(normal)
                        rate[1] = rate[1] + thrust * wgt[on, 0, t, g]
                        rate[2] = rate[2] + thrust * wgt[on, 1, t, g]
                    for f in range(fields):
                        if second:
                            old = base[f, t, z, here, :]
                            new = 0.5 * (old + c[f]) + rate[f]
                            if is_domain and t == 0:
                                new = new + ramp * (pq[f, 0, z, here, :] - new)
                        else:
                            new = c[f] + rate[f]
                        if is_domain and k == HALO:
                            out = mine_ref if g < groups // 2 else send_ref
                            y = 8 * (g % (groups // 2))
                            start = ((f * ry + y) * tiles + t) * rz + z - HALO
                            out[pl.ds(start, 8, stride=tiles * rz), :] = new
                        else:
                            put(dst, f, t, z, g, new)
            return carry

        lax.fori_loop(jnp.maximum(k, dlo), jnp.minimum(ext - k, dhi), row, 0)

    for step in range(STEPS):
        k = 2 * step + 1
        stage(pq, None, pm, 2, k, False)
        stage(pm, pq, pq, 2, k + 1, False)
        stage(q, None, m, tiles, k, True)
        stage(m, q, q, tiles, k + 1, True)


def join_kernel(ints, mine_ref, got_ref, out_ref):
    out_ref[ints[0]] = mine_ref[...]
    out_ref[1 - ints[0]] = got_ref[...]


def swaps(size):
    inner = [(i, i ^ 1) for i in range(size)]
    outer = [(i, i + 1 if i % 2 else i - 1) for i in range(size)]
    outer = [(i, j) for i, j in outer if 0 <= j < size]
    return inner, outer


def spread(value, axis):
    size = lax.axis_size(axis)
    at = lax.axis_index(axis)
    gap = size // 2
    while gap:
        pairs = [(i, i + gap) for i in range(0, size, 2 * gap)]
        moved = lax.ppermute(value, axis, pairs)
        value = jnp.where(at % (2 * gap) == gap, moved, value)
        gap //= 2
    return value


def body(state, turbine_x, turbine_y, yaw_index):
    slots, fields, ry, rz, x = state.shape
    tiles = x // LANES
    nt = turbine_x.shape[1]
    case_at, span_at, vert_at = (lax.axis_index(a) for a in ("case", "span", "vert"))
    total_z = rz * lax.axis_size("vert")
    rows = fields * ry * tiles * rz
    inner, outer = swaps(lax.axis_size("vert"))
    across = [(0, 1), (1, 0)]

    own = flat(lax.dynamic_index_in_dim(state, span_at, 0, False))
    away = flat(lax.dynamic_index_in_dim(state, 1 - span_at, 0, False))
    got = lax.ppermute(away, "span", across)
    fringe = pl.pallas_call(
        functools.partial(pack_kernel, (fields, ry, rz, tiles)),
        out_shape=jax.ShapeDtypeStruct((fields * (ry + 1) * rz, LANES), jnp.float32),
        name="pack",
    )(flat(state[0]))
    in_own = lax.ppermute(own, "vert", inner)
    out_own = lax.ppermute(own, "vert", outer)
    fringe = spread(fringe, "case")
    fringe_got = lax.ppermute(fringe, "span", across)
    fringe = jnp.concatenate([fringe, fringe_got])
    in_got = lax.ppermute(got, "vert", inner)
    out_got = lax.ppermute(got, "vert", outer)
    fringe_in = lax.ppermute(fringe, "vert", inner)
    fringe_out = lax.ppermute(fringe, "vert", outer)

    domain = case_at * slots + span_at
    tx = lax.dynamic_index_in_dim(turbine_x, span_at, 0, False)
    ty = lax.dynamic_index_in_dim(turbine_y, span_at, 0, False)
    yaw = lax.dynamic_index_in_dim(yaw_index, span_at, 0, False)
    z0 = vert_at * rz
    ints = jnp.stack(
        [
            jnp.maximum(HALO - z0, 0),
            jnp.minimum(HALO + total_z - z0, rz + 2 * HALO),
            1 - vert_at % 2,
            HALO + total_z // 2 - z0,
            span_at * ry,
        ]
    ).astype(jnp.int32)
    ints = jnp.concatenate([ints, tx, ty])
    angle = (yaw.astype(jnp.float32) - 3.5) * YAW_STEP
    reals = jnp.stack([jnp.cos(angle), jnp.sin(angle), (domain > 0).astype(jnp.float32)])
    width = x // 4
    ramp = 0.5 * (1.0 - jnp.cos(jnp.pi * (jnp.arange(width, dtype=jnp.float32) + 1.0) / width))
    ramp = jnp.broadcast_to(ramp[None], (8, width))

    smem = pl.BlockSpec(memory_space=pltpu.SMEM)
    vmem = pl.BlockSpec(memory_space=pltpu.VMEM)
    ext = rz + 2 * HALO
    store = 2 * ROW0 + 2 * ry
    mine, send = pl.pallas_call(
        functools.partial(main_kernel, (fields, ry, rz, tiles, nt)),
        out_shape=[jax.ShapeDtypeStruct((rows, LANES), jnp.float32)] * 2,
        in_specs=[smem, smem] + [vmem] * 10,
        out_specs=[vmem, vmem],
        scratch_shapes=[
            pltpu.VMEM((fields, tiles, ext, store, LANES), jnp.float32),
            pltpu.VMEM((fields, tiles, ext, store, LANES), jnp.float32),
            pltpu.VMEM((fields, 2, ext, store, LANES), jnp.float32),
            pltpu.VMEM((fields, 2, ext, store, LANES), jnp.float32),
            pltpu.VMEM((ry * rz, LANES), jnp.float32),
            pltpu.VMEM((2, 2, tiles, 2 * ry // 8, 8, LANES), jnp.float32),
        ],
        name="steps",
    )(ints, reals, own, got, in_own, in_got, out_own, out_got, fringe, fringe_in, fringe_out, ramp)
    back = lax.ppermute(send, "span", across)
    out = pl.pallas_call(
        join_kernel,
        out_shape=jax.ShapeDtypeStruct((slots, rows, LANES), jnp.float32),
        in_specs=[smem, vmem, vmem],
        out_specs=vmem,
        name="join",
    )(span_at[None].astype(jnp.int32), mine, back)
    return unflat(out, fields, ry, rz, x)


def extended_2(shard, sides, width):
    for axis, dim in sides:
        size, length = (lax.axis_size(axis), shard.shape[dim])
        up = [(i, (i + 1) % size) for i in range(size)]
        down = [(j, i) for i, j in up]
        last = lax.slice_in_dim(shard, length - width, length, axis=dim)
        leading = lax.slice_in_dim(shard, 0, width, axis=dim)
        before = lax.ppermute(last, axis, up)
        after = lax.ppermute(leading, axis, down)
        shard = jnp.concatenate([before, shard, after], axis=dim)
    return shard


def entering(part, axis, combine, identity):
    place = lax.axis_index(axis)
    gathered = jax.tree.map(lambda a: lax.all_gather(a, axis), part)
    state = jax.tree.map(lambda a, e: jnp.zeros_like(a) + jnp.asarray(e, a.dtype), part, identity)

    def one(step, state):
        return combine(
            state, jax.tree.map(lambda a: lax.dynamic_index_in_dim(a, step, 0, False), gathered)
        )

    return lax.fori_loop(0, place, one, state)


def tendency(center, east, west, north, south, upper, lower, weight, cos_yaw, sin_yaw):
    grad_x = (east - west) * 0.5
    grad_y = (north - south) * 0.5
    grad_z = (upper - lower) * 0.5
    laplace = east + west + north + south + upper + lower - 6.0 * center
    vel_u = center[..., 1, :, :, :]
    vel_v = center[..., 2, :, :, :]
    vel_w = center[..., 3, :, :, :]
    dux = grad_x[..., 1, :, :, :]
    dvy = grad_y[..., 2, :, :, :]
    dwz = grad_z[..., 3, :, :, :]
    duy = grad_y[..., 1, :, :, :]
    duz = grad_z[..., 1, :, :, :]
    strain = dux * dux + dvy * dvy + dwz * dwz + duy * duy + duz * duz
    viscous = VISC * jnp.sqrt(1.0 + strain)
    speed = U_MEAN + vel_u
    flow = -(
        jnp.expand_dims(speed, -4) * grad_x
        + jnp.expand_dims(vel_v, -4) * grad_y
        + jnp.expand_dims(vel_w, -4) * grad_z
    )
    flow = flow + jnp.expand_dims(viscous, -4) * laplace
    normal = speed * cos_yaw + vel_v * sin_yaw
    thrust = THRUST * normal * jnp.abs(normal) * weight
    extra = jnp.stack(
        [
            -(dux + dvy + dwz),
            -grad_x[..., 0, :, :, :] - thrust * cos_yaw,
            -grad_y[..., 0, :, :, :] - thrust * sin_yaw,
            -grad_z[..., 0, :, :, :],
        ],
        axis=-4,
    )
    return flow + extra


def extended(fields):
    padded = extended_2(fields, (("span", 2), ("vert", 3)), 1)
    vert_at = lax.axis_index("vert")
    bottom = jnp.where(vert_at == 0, 0.0, padded[:, :, :, :1, :])
    summit = jnp.where(vert_at == lax.axis_size("vert") - 1, 0.0, padded[:, :, :, -1:, :])
    padded = jnp.concatenate([bottom, padded[:, :, :, 1:-1, :], summit], axis=3)
    return padded


def stencil(fields, padded, weight, cos_yaw, sin_yaw):
    east = jnp.roll(fields, -1, axis=4)
    west = jnp.roll(fields, 1, axis=4)
    north = padded[:, :, 2:, 1:-1, :]
    south = padded[:, :, :-2, 1:-1, :]
    upper = padded[:, :, 1:-1, 2:, :]
    lower = padded[:, :, 1:-1, :-2, :]
    return tendency(fields, east, west, north, south, upper, lower, weight, cos_yaw, sin_yaw)


def rate(fields, weight, cos_yaw, sin_yaw):
    return stencil(fields, extended(fields), weight, cos_yaw, sin_yaw)


def make_weight(turbine_x, turbine_y, along_y, along_z, total_y, total_z, active, length):
    along_x = jnp.arange(length, dtype=jnp.int32)
    hit_x = (along_x[None, None, :] == turbine_x[:, :, None]).astype(jnp.float32)
    hit_y = ((along_y[None, None, :] - turbine_y[:, :, None]) % total_y < DISK).astype(jnp.float32)
    plane = jnp.einsum("dky,dkx->dyx", hit_y, hit_x, precision=lax.Precision.HIGHEST)
    lower_half = (along_z < total_z // 2).astype(jnp.float32)
    return plane[:, :, None, :] * lower_half[None, None, :, None] * active[:, None, None, None]


def first_held(earlier, later):
    keep = earlier[1] > 0.0
    return (jnp.where(keep, earlier[0], later[0]), jnp.maximum(earlier[1], later[1]))


def body_general(state, turbine_x, turbine_y, yaw_index):
    slots = state.shape[0]
    rows_y = state.shape[2]
    rows_z = state.shape[3]
    total_y = rows_y * lax.axis_size("span")
    total_z = rows_z * lax.axis_size("vert")
    domain = lax.axis_index("case") * slots + jnp.arange(slots, dtype=jnp.int32)
    active = (domain > 0).astype(jnp.float32)
    along_y = lax.axis_index("span") * rows_y + jnp.arange(rows_y, dtype=jnp.int32)
    along_z = lax.axis_index("vert") * rows_z + jnp.arange(rows_z, dtype=jnp.int32)
    weight = make_weight(turbine_x, turbine_y, along_y, along_z, total_y, total_z, active, state.shape[4])
    angle = (yaw_index.astype(jnp.float32) - 3.5) * YAW_STEP
    cos_yaw = jnp.cos(angle)[:, None, None, None]
    sin_yaw = jnp.sin(angle)[:, None, None, None]
    width = state.shape[4] // 4
    ramp = 0.5 * (1.0 - jnp.cos(jnp.pi * (jnp.arange(width, dtype=jnp.float32) + 1.0) / width))
    case_at = lax.axis_index("case")
    for step in range(STEPS):
        first = rate(state, weight, cos_yaw, sin_yaw)
        middle = state + TIME_STEP * first
        second = rate(middle, weight, cos_yaw, sin_yaw)
        state = state + 0.5 * TIME_STEP * (first + second)
        front = state[..., :width]
        own_fringe = front[0]
        marker = jnp.ones((), jnp.float32)
        blank = (jnp.zeros_like(own_fringe), jnp.zeros((), jnp.float32))
        passed = entering((own_fringe, marker), "case", first_held, blank)
        source = jnp.where(case_at == 0, own_fringe, passed[0])
        front = front + ramp * (source[None] - front)
        state = jnp.concatenate([front, state[..., width:]], axis=4)
    return state


def body_any(state, turbine_x, turbine_y, yaw_index):
    slots, _, ry, rz, x = state.shape
    fits = lax.axis_size("span") == 2 and slots == 2 and lax.axis_size("vert") % 2 == 0
    fits = fits and ry == 8 and rz % 8 == 0 and x == 4 * LANES
    chosen = body if fits else body_general
    return chosen(state, turbine_x, turbine_y, yaw_index)


def solution(mesh):
    return jax.shard_map(
        body_any,
        mesh=mesh,
        in_specs=(
            P("case", None, "span", "vert", None),
            P("case", None),
            P("case", None),
            P("case"),
        ),
        out_specs=P("case", None, "span", "vert", None),
        check_vma=False,
    )
```

```python
import functools

import jax
import jax.numpy as jnp
from jax import lax
from jax.experimental import pallas as pl
from jax.experimental.pallas import tpu as pltpu
from jax.sharding import PartitionSpec as P

STEPS = 3
DISK = 8
LANES = 128
HALO = 2 * STEPS

U_MEAN = 1.0
VISC = 0.04
THRUST = 0.75
TIME_STEP = 0.1
YAW_STEP = 0.15
HALF = 0.5 * TIME_STEP
SCALES = (HALF * HALF, HALF, HALF, HALF)

ROW0 = 8
STRIP = 16


def flat(blocks):
    y, z, x = blocks.shape[-3:]
    a = blocks.reshape(-1, z, x // LANES, LANES)
    return jnp.swapaxes(a, 1, 2).reshape(-1, LANES)


def unflat(rows, shape):
    y, z, x = shape[-3:]
    a = rows.reshape(-1, x // LANES, z, LANES)
    return jnp.swapaxes(a, 1, 2).reshape(shape)


def away_kernel(dims, state_ref, near_ref, far_ref, block, sem):
    fields, ry, rz, tiles = dims
    size = fields * ry * tiles * rz
    slot = 1 - lax.axis_index("span")
    even = lax.axis_index("vert") % 2 == 0
    start = pl.multiple_of(slot * size, 8)
    copy = pltpu.make_async_copy(state_ref.at[pl.ds(start, size)], block, sem)
    copy.start()
    copy.wait()
    near = jnp.where(even, 0, rz - HALO)
    far = jnp.where(even, HALO, 0)
    for ref, low, count in ((near_ref, near, HALO), (far_ref, far, rz - HALO)):
        for f in range(fields):
            for t in range(tiles):
                for k in range(count):
                    row = (f * ry * tiles + t) * rz + low + k
                    value = block[pl.ds(row, ry, stride=tiles * rz), :]
                    ref[pl.ds(((f * tiles + t) * count + k) * ry, ry), :] = value


def own_kernel(dims, state_ref, after_ref, own_ref, near_ref, fringe_ref, block, first, sems):
    del after_ref
    fields, ry, rz, tiles = dims
    size = fields * ry * tiles * rz
    slot = lax.axis_index("span")
    even = lax.axis_index("vert") % 2 == 0
    start = pl.multiple_of(slot * size, 8)
    copy_first = pltpu.make_async_copy(state_ref.at[pl.ds(0, size)], first, sems.at[0])
    copy_own = pltpu.make_async_copy(state_ref.at[pl.ds(start, size)], block, sems.at[1])
    copy_first.start()
    copy_own.start()
    copy_first.wait()
    lane = lax.broadcasted_iota(jnp.int32, (ry, LANES), 1)
    for f in range(fields):
        strip = jnp.zeros((ry, LANES), jnp.float32)
        for z in range(rz):
            row = f * ry * tiles * rz + z
            step = tiles * rz
            place = f * (rz + 1) + z
            fringe_ref[pl.ds(place * ry, ry), :] = first[pl.ds(row, ry, stride=step), :]
            after = first[pl.ds(row + rz, ry, stride=step), :]
            before = first[pl.ds(row + (tiles - 1) * rz, ry, stride=step), :]
            both = jnp.where(lane < LANES // 2, after, before)
            both = pltpu.roll(both, (HALO + STRIP * z) % LANES, 1)
            here = (lane >= STRIP * z) & (lane < STRIP * z + 2 * HALO)
            strip = jnp.where(here, both, strip)
        fringe_ref[pl.ds((f * (rz + 1) + rz) * ry, ry), :] = strip
    copy_own.wait()
    for f in range(fields):
        for t in range(tiles):
            for z in range(rz):
                row = (f * ry * tiles + t) * rz + z
                value = block[pl.ds(row, ry, stride=tiles * rz), :]
                own_ref[pl.ds(((f * tiles + t) * rz + z) * ry, ry), :] = value
    near = jnp.where(even, 0, rz - HALO)
    for c in range(fields * tiles):
        for k in range(HALO):
            row = pl.multiple_of((c * rz + near + k) * ry, 8)
            near_ref[pl.ds((c * HALO + k) * ry, ry), :] = own_ref[pl.ds(row, ry), :]


def main_kernel(
    dims, xs, ys, yaws, own, got_near, got_far, out_own, out_got, in_own, in_near, in_far,
    p_own, p_got, p_out_own, p_out_got, p_in_own, p_in_got,
    mine_ref, send_ref, q, m, pq, pm, wgt, sides0, sides1,
):
    fields, ry, rz, tiles, nt, slots = dims
    ext = rz + 2 * HALO
    rows = ext + 2
    total_y = 2 * ry
    total_z = rz * lax.axis_size("vert")
    store = 2 * ROW0 + total_y
    groups = total_y // 8
    slot = lax.axis_index("span")
    vert_at = lax.axis_index("vert")
    z0 = vert_at * rz
    even = vert_at % 2 == 0
    dlo = jnp.maximum(HALO - z0, 0)
    dhi = jnp.minimum(HALO + total_z - z0, ext)
    gate = HALO + total_z // 2 - z0
    y_off = slot * ry
    one = 1 + jnp.minimum(vert_at, 0)
    active = jnp.where(lax.axis_index("case") * slots + slot > 0, 1.0, 0.0)
    lane = lax.broadcasted_iota(jnp.int32, (8, LANES), 1)
    sub = lax.broadcasted_iota(jnp.int32, (8, LANES), 0)
    first_lane = lane == 0
    last_lane = lane == LANES - 1
    angle = (jnp.full((8, LANES), yaws[slot], jnp.int32).astype(jnp.float32) - 3.5) * YAW_STEP
    cos_yaw = jnp.cos(angle)
    sin_yaw = jnp.sin(angle)
    ramp = 0.5 * (1.0 - jnp.cos(jnp.pi * (lane.astype(jnp.float32) + 1.0) / LANES))

    def put(dst, width, f, t, z, group, value):
        start = pl.multiple_of(((f * width + t) * rows + z + 1) * store, 8)
        dst[pl.ds(start + (ROW0 + 8 * group), 8), :] = value
        if group == 0:
            dst[pl.ds(start + (ROW0 + total_y), 1), :] = value[0:1]
        if group == groups - 1:
            dst[pl.ds(start + (ROW0 - 1), 1), :] = value[7:8]

    def scale_of(f):
        return jnp.where(f == 0, SCALES[0], SCALES[1])

    def fill(parts):
        def one_field(f, carry):
            for src, held, taken, half, z_dst, count in parts:
                for t in range(tiles):
                    for k in range(count):
                        row = pl.multiple_of(((f * tiles + t) * held + taken + k) * ry, 8)
                        for g in range(ry // 8):
                            value = scale_of(f) * src[pl.ds(row + 8 * g, 8), :]
                            put(q, tiles, f, t, z_dst + k, half * (ry // 8) + g, value)
            return carry

        lax.fori_loop(0, fields, one_field, 0)

    def fill_fringe(parts):
        def one_field(f, carry):
            for src, taken, half, z_dst, count in parts:
                base = f * (rz + 1)
                strip = scale_of(f) * src[pl.ds(pl.multiple_of((base + rz) * ry, 8), ry), :]
                for k in range(count):
                    z = taken + k
                    row = pl.multiple_of((base + z) * ry, 8)
                    put(pq, 2, f, 0, z_dst + k, half, scale_of(f) * src[pl.ds(row, ry), :])
                    value = pltpu.roll(strip, 2 * LANES - HALO - STRIP * z, 1)
                    put(pq, 2, f, 1, z_dst + k, half, value)
            return carry

        lax.fori_loop(0, fields, one_field, 0)

    def pick(a, b):
        return jnp.where(even, a, b)

    above = HALO + rz
    rest = rz - HALO
    fill(
        (
            (own, rz, 0, 0, HALO, rz),
            (in_own, rz, pick(0, rest), 0, pick(above, 0), HALO),
            (out_own, HALO, 0, 0, pick(0, above), HALO),
        )
    )
    fill(
        (
            (got_near, HALO, 0, 1, HALO + pick(0, rest), HALO),
            (got_far, rest, 0, 1, HALO + pick(HALO, 0), rest),
            (out_got, HALO, 0, 1, pick(0, above), HALO),
            (in_near, HALO, pick(0, rest), 1, pick(above + rest, 0), HALO - rest),
            (in_far, rest, 0, 1, pick(above, HALO - rest), rest),
        )
    )
    fill_fringe(
        (
            (p_own, 0, 0, HALO, rz),
            (p_got, 0, 1, HALO, rz),
            (p_out_own, pick(rest, 0), 0, pick(0, above), HALO),
            (p_out_got, pick(rest, 0), 1, pick(0, above), HALO),
            (p_in_own, pick(0, rest), 0, pick(above, 0), HALO),
            (p_in_got, pick(0, rest), 1, pick(above, 0), HALO),
        )
    )

    zero = jnp.zeros((store, LANES), jnp.float32)
    for ref, width in ((m, tiles), (pm, 2), (q, tiles), (pq, 2)):
        for z in (HALO - 1, HALO + rz):
            outside = (z < dlo) | (z >= dhi)

            def clear(ref=ref, width=width, z=z):
                for f in range(fields):
                    for t in range(width):
                        ref[pl.ds(((f * width + t) * rows + z + 1) * store, store), :] = zero

            pl.when(outside)(clear)

    for t in range(1, tiles):
        for g in range(groups):
            acc = jnp.zeros((8, LANES), jnp.float32)
            y = y_off + 8 * g + sub
            for k in range(nt):
                hit = lax.rem(y - ys[slot, k] + 2 * total_y, total_y) < DISK
                hit = hit & (lane + t * LANES == xs[slot, k])
                acc = acc + jnp.where(hit, 1.0, 0.0)
            acc = acc * active
            wgt[0, 0, t, g] = jnp.zeros((8, LANES), jnp.float32)
            wgt[0, 1, t, g] = jnp.zeros((8, LANES), jnp.float32)
            wgt[1, 0, t, g] = acc * (2.0 * THRUST * cos_yaw)
            wgt[1, 1, t, g] = acc * (2.0 * THRUST * sin_yaw)

    def stage(src, base, dst, width, k, is_domain):
        second = k % 2 == 0

        def at(ref, f, t, g, z, dy=0):
            start = ((f * width + t % width) * rows + z + 1) * store + ROW0 + 8 * g
            start = start + dy * one if dy else pl.multiple_of(start, 8)
            return ref[pl.ds(start, 8), :]

        def beside(f, t, g, side):
            return pl.ds((((f * 2 + side) * width + t) * groups + g) * 8, 8)

        def shift(z, into, t, g):
            for f in range(fields):
                c = at(src, f, t, g, z)
                after = at(src, f, t + 1, g, z)
                before = at(src, f, t - 1, g, z)
                east = pltpu.roll(jnp.where(first_lane, after, c), LANES - 1, 1)
                west = pltpu.roll(jnp.where(last_lane, before, c), 1, 1)
                into[beside(f, t, g, 0), :] = east
                into[beside(f, t, g, 1), :] = west

        def row(z, sides, following):
            if is_domain:
                on = jnp.where(z < gate, 1, 0)
            for t in range(width):
                for g in range(groups):
                    shift(z + 1, following, t, g)
                    c = [at(src, f, t, g, z) for f in range(fields)]
                    gx, gy, gz, lap = [], [], [], []
                    for f in range(fields):
                        east = sides[beside(f, t, g, 0), :]
                        west = sides[beside(f, t, g, 1), :]
                        north = at(src, f, t, g, z, dy=1)
                        south = at(src, f, t, g, z, dy=-1)
                        upper = at(src, f, t, g, z + 1)
                        lower = at(src, f, t, g, z - 1)
                        gx.append(east - west)
                        gy.append(north - south)
                        gz.append(upper - lower)
                        around = ((east + west) + (north + south)) + (upper + lower)
                        lap.append(around - 6.0 * c[f])
                    speed = c[1] + HALF * U_MEAN
                    strain = gx[1] * gx[1] + gy[2] * gy[2] + gz[3] * gz[3]
                    strain = strain + gy[1] * gy[1] + gz[1] * gz[1] + 4.0 * HALF * HALF
                    viscous = VISC * (strain * lax.rsqrt(strain))
                    rate = [
                        viscous * lap[f] - (speed * gx[f] + c[2] * gy[f] + c[3] * gz[f])
                        for f in range(fields)
                    ]
                    rate[0] = rate[0] - HALF * HALF * (gx[1] + gy[2] + gz[3])
                    rate[1] = rate[1] - gx[0]
                    rate[2] = rate[2] - gy[0]
                    rate[3] = rate[3] - gz[0]
                    if is_domain and t > 0:
                        normal = speed * cos_yaw + c[2] * sin_yaw
                        thrust = normal * jnp.abs(normal)
                        rate[1] = rate[1] - thrust * wgt[on, 0, t, g]
                        rate[2] = rate[2] - thrust * wgt[on, 1, t, g]
                    for f in range(fields):
                        if second:
                            new = 0.5 * ((at(base, f, t, g, z) + c[f]) + rate[f])
                            if is_domain and t == 0:
                                start = pl.multiple_of((f * 2 * rows + z + 1) * store, 8)
                                new = new + ramp * (pq[pl.ds(start + (ROW0 + 8 * g), 8), :] - new)
                        else:
                            new = c[f] + rate[f]
                        if is_domain and k == HALO:
                            out = mine_ref if g < groups // 2 else send_ref
                            start = ((f * tiles + t) * rz + z - HALO) * ry + 8 * (g % (groups // 2))
                            new = new * (1.0 / SCALES[f])
                            out[pl.ds(pl.multiple_of(start, 8), 8), :] = new
                        else:
                            put(dst, width, f, t, z, g, new)
        first = jnp.maximum(k, dlo)
        count = jnp.minimum(ext - k, dhi) - first
        first = first - jnp.where(dhi < ext, count & 1, 0)
        for t in range(width):
            for g in range(groups):
                shift(first, sides0, t, g)

        def pair(i, carry):
            z = first + 2 * i
            row(z, sides0, sides1)
            row(z + 1, sides1, sides0)
            return carry

        lax.fori_loop(0, (count + 1) // 2, pair, 0)

    for step in range(STEPS):
        k = 2 * step + 1
        stage(pq, None, pm, 2, k, False)
        stage(pm, pq, pq, 2, k + 1, False)
        stage(q, None, m, tiles, k, True)
        stage(m, q, q, tiles, k + 1, True)


def place_kernel(dims, other, *refs):
    fields, ry, rz, tiles = dims
    src, out_ref, block, sems = refs[0], refs[-3], refs[-2], refs[-1]
    size = ry * tiles * rz
    slot = lax.axis_index("span")
    slot = 1 - slot if other else slot
    copies = []
    for f in range(fields):
        for y in range(ry):
            for t in range(tiles):
                value = src[pl.ds((f * tiles + t) * rz * ry + y, rz, stride=ry), :]
                block[pl.ds(((f * ry + y) * tiles + t) * rz, rz), :] = value
        start = pl.multiple_of((slot * fields + f) * size, 8)
        part = block.at[pl.ds(f * size, size)]
        copies.append(pltpu.make_async_copy(part, out_ref.at[pl.ds(start, size)], sems.at[f]))
        copies[-1].start()
    for copy in copies:
        copy.wait()


def swaps(size):
    inner = [(i, i ^ 1) for i in range(size)]
    outer = [(i, i + 1 if i % 2 else i - 1) for i in range(size)]
    outer = [(i, j) for i, j in outer if 0 <= j < size]
    return inner, outer


def spread(value, axis):
    size = lax.axis_size(axis)
    at = lax.axis_index(axis)
    gap = size // 2
    while gap:
        pairs = [(i, i + gap) for i in range(0, size, 2 * gap)]
        moved = lax.ppermute(value, axis, pairs)
        value = jnp.where(at % (2 * gap) == gap, moved, value)
        gap //= 2
    return value


def body(state, turbine_x, turbine_y, yaw_index):
    slots, fields, ry, rz, x = state.shape
    tiles = x // LANES
    nt = turbine_x.shape[1]
    count = fields * ry * tiles * rz
    near_count = count // rz * HALO
    fringe_count = fields * (rz + 1) * ry
    dims = (fields, ry, rz, tiles)
    inner, outer = swaps(lax.axis_size("vert"))
    across = [(0, 1), (1, 0)]
    smem = pl.BlockSpec(memory_space=pltpu.SMEM)
    vmem = pl.BlockSpec(memory_space=pltpu.VMEM)
    hbm = pl.BlockSpec(memory_space=pl.ANY)
    whole = flat(state)

    def rows_of(n):
        return jax.ShapeDtypeStruct((n, LANES), jnp.float32)

    def block_of(n):
        return pltpu.VMEM((n, LANES), jnp.float32)

    away_near, away_far = pl.pallas_call(
        functools.partial(away_kernel, dims),
        out_shape=[rows_of(near_count), rows_of(count - near_count)],
        in_specs=[hbm],
        out_specs=[vmem, vmem],
        scratch_shapes=[block_of(count), pltpu.SemaphoreType.DMA],
        name="away",
    )(whole)
    got_near = lax.ppermute(away_near, "span", across)
    got_far = lax.ppermute(away_far, "span", across)
    own, near, fringe = pl.pallas_call(
        functools.partial(own_kernel, dims),
        out_shape=[rows_of(count), rows_of(near_count), rows_of(fringe_count)],
        in_specs=[hbm, hbm],
        out_specs=[vmem, vmem, vmem],
        scratch_shapes=[block_of(count), block_of(count), pltpu.SemaphoreType.DMA((2,))],
        name="own",
    )(whole, away_far)
    out_own = lax.ppermute(near, "vert", outer)
    in_own = lax.ppermute(own, "vert", inner)
    fringe = spread(fringe, "case")
    fringe_got = lax.ppermute(fringe, "span", across)
    out_got = lax.ppermute(got_near, "vert", outer)
    in_near = lax.ppermute(got_near, "vert", inner)
    in_far = lax.ppermute(got_far, "vert", inner)
    fringes = [fringe, fringe_got]
    fringes += [lax.ppermute(a, "vert", outer) for a in (fringe, fringe_got)]
    fringes += [lax.ppermute(a, "vert", inner) for a in (fringe, fringe_got)]

    ext = rz + 2 * HALO
    store = 2 * ROW0 + 2 * ry
    mine, send = pl.pallas_call(
        functools.partial(main_kernel, (fields, ry, rz, tiles, nt, slots)),
        out_shape=[rows_of(count)] * 2,
        in_specs=[smem] * 3 + [vmem] * 14,
        out_specs=[vmem, vmem],
        scratch_shapes=[block_of(fields * w * (ext + 2) * store) for w in (tiles, tiles, 2, 2)]
        + [pltpu.VMEM((2, 2, tiles, 2 * ry // 8, 8, LANES), jnp.float32)]
        + [block_of(fields * 2 * tiles * 2 * ry)] * 2,
        compiler_params=pltpu.CompilerParams(

        ),
        name="steps",
    )(
        turbine_x, turbine_y, yaw_index, own, got_near, got_far, out_own, out_got, in_own, in_near, in_far,
        *fringes,
    )
    back = lax.ppermute(send, "span", across)

    def place(other, block, *earlier):
        return pl.pallas_call(
            functools.partial(place_kernel, dims, other),
            out_shape=rows_of(slots * count),
            in_specs=[vmem] + [hbm] * len(earlier),
            out_specs=hbm,
            scratch_shapes=[block_of(count), pltpu.SemaphoreType.DMA((fields,))],
            input_output_aliases={1: 0} if earlier else {},
            name="place",
        )(block, *earlier)

    return unflat(place(True, back, place(False, mine)), state.shape)


def extended_2(shard, sides, width):
    for axis, dim in sides:
        size, length = (lax.axis_size(axis), shard.shape[dim])
        up = [(i, (i + 1) % size) for i in range(size)]
        down = [(j, i) for i, j in up]
        last = lax.slice_in_dim(shard, length - width, length, axis=dim)
        leading = lax.slice_in_dim(shard, 0, width, axis=dim)
        before = lax.ppermute(last, axis, up)
        after = lax.ppermute(leading, axis, down)
        shard = jnp.concatenate([before, shard, after], axis=dim)
    return shard


def entering(part, axis, combine, identity):
    place = lax.axis_index(axis)
    gathered = jax.tree.map(lambda a: lax.all_gather(a, axis), part)
    state = jax.tree.map(lambda a, e: jnp.zeros_like(a) + jnp.asarray(e, a.dtype), part, identity)

    def one(step, state):
        return combine(
            state, jax.tree.map(lambda a: lax.dynamic_index_in_dim(a, step, 0, False), gathered)
        )

    return lax.fori_loop(0, place, one, state)


def tendency(center, east, west, north, south, upper, lower, weight, cos_yaw, sin_yaw):
    grad_x = (east - west) * 0.5
    grad_y = (north - south) * 0.5
    grad_z = (upper - lower) * 0.5
    laplace = east + west + north + south + upper + lower - 6.0 * center
    vel_u = center[..., 1, :, :, :]
    vel_v = center[..., 2, :, :, :]
    vel_w = center[..., 3, :, :, :]
    dux = grad_x[..., 1, :, :, :]
    dvy = grad_y[..., 2, :, :, :]
    dwz = grad_z[..., 3, :, :, :]
    duy = grad_y[..., 1, :, :, :]
    duz = grad_z[..., 1, :, :, :]
    strain = dux * dux + dvy * dvy + dwz * dwz + duy * duy + duz * duz
    viscous = VISC * jnp.sqrt(1.0 + strain)
    speed = U_MEAN + vel_u
    flow = -(
        jnp.expand_dims(speed, -4) * grad_x
        + jnp.expand_dims(vel_v, -4) * grad_y
        + jnp.expand_dims(vel_w, -4) * grad_z
    )
    flow = flow + jnp.expand_dims(viscous, -4) * laplace
    normal = speed * cos_yaw + vel_v * sin_yaw
    thrust = THRUST * normal * jnp.abs(normal) * weight
    extra = jnp.stack(
        [
            -(dux + dvy + dwz),
            -grad_x[..., 0, :, :, :] - thrust * cos_yaw,
            -grad_y[..., 0, :, :, :] - thrust * sin_yaw,
            -grad_z[..., 0, :, :, :],
        ],
        axis=-4,
    )
    return flow + extra


def extended(fields):
    padded = extended_2(fields, (("span", 2), ("vert", 3)), 1)
    vert_at = lax.axis_index("vert")
    bottom = jnp.where(vert_at == 0, 0.0, padded[:, :, :, :1, :])
    summit = jnp.where(vert_at == lax.axis_size("vert") - 1, 0.0, padded[:, :, :, -1:, :])
    padded = jnp.concatenate([bottom, padded[:, :, :, 1:-1, :], summit], axis=3)
    return padded


def stencil(fields, padded, weight, cos_yaw, sin_yaw):
    east = jnp.roll(fields, -1, axis=4)
    west = jnp.roll(fields, 1, axis=4)
    north = padded[:, :, 2:, 1:-1, :]
    south = padded[:, :, :-2, 1:-1, :]
    upper = padded[:, :, 1:-1, 2:, :]
    lower = padded[:, :, 1:-1, :-2, :]
    return tendency(fields, east, west, north, south, upper, lower, weight, cos_yaw, sin_yaw)


def rate(fields, weight, cos_yaw, sin_yaw):
    return stencil(fields, extended(fields), weight, cos_yaw, sin_yaw)


def make_weight(turbine_x, turbine_y, along_y, along_z, total_y, total_z, active, length):
    along_x = jnp.arange(length, dtype=jnp.int32)
    hit_x = (along_x[None, None, :] == turbine_x[:, :, None]).astype(jnp.float32)
    hit_y = ((along_y[None, None, :] - turbine_y[:, :, None]) % total_y < DISK).astype(jnp.float32)
    plane = jnp.einsum("dky,dkx->dyx", hit_y, hit_x, precision=lax.Precision.HIGHEST)
    lower_half = (along_z < total_z // 2).astype(jnp.float32)
    return plane[:, :, None, :] * lower_half[None, None, :, None] * active[:, None, None, None]


def first_held(earlier, later):
    keep = earlier[1] > 0.0
    return (jnp.where(keep, earlier[0], later[0]), jnp.maximum(earlier[1], later[1]))


def body_general(state, turbine_x, turbine_y, yaw_index):
    slots = state.shape[0]
    rows_y = state.shape[2]
    rows_z = state.shape[3]
    total_y = rows_y * lax.axis_size("span")
    total_z = rows_z * lax.axis_size("vert")
    domain = lax.axis_index("case") * slots + jnp.arange(slots, dtype=jnp.int32)
    active = (domain > 0).astype(jnp.float32)
    along_y = lax.axis_index("span") * rows_y + jnp.arange(rows_y, dtype=jnp.int32)
    along_z = lax.axis_index("vert") * rows_z + jnp.arange(rows_z, dtype=jnp.int32)
    weight = make_weight(turbine_x, turbine_y, along_y, along_z, total_y, total_z, active, state.shape[4])
    angle = (yaw_index.astype(jnp.float32) - 3.5) * YAW_STEP
    cos_yaw = jnp.cos(angle)[:, None, None, None]
    sin_yaw = jnp.sin(angle)[:, None, None, None]
    width = state.shape[4] // 4
    ramp = 0.5 * (1.0 - jnp.cos(jnp.pi * (jnp.arange(width, dtype=jnp.float32) + 1.0) / width))
    case_at = lax.axis_index("case")
    for step in range(STEPS):
        first = rate(state, weight, cos_yaw, sin_yaw)
        middle = state + TIME_STEP * first
        second = rate(middle, weight, cos_yaw, sin_yaw)
        state = state + 0.5 * TIME_STEP * (first + second)
        front = state[..., :width]
        own_fringe = front[0]
        marker = jnp.ones((), jnp.float32)
        blank = (jnp.zeros_like(own_fringe), jnp.zeros((), jnp.float32))
        passed = entering((own_fringe, marker), "case", first_held, blank)
        source = jnp.where(case_at == 0, own_fringe, passed[0])
        front = front + ramp * (source[None] - front)
        state = jnp.concatenate([front, state[..., width:]], axis=4)
    return state


def body_any(state, turbine_x, turbine_y, yaw_index):
    slots, _, ry, rz, x = state.shape
    fits = lax.axis_size("span") == 2 and slots == 2 and lax.axis_size("vert") % 2 == 0
    fits = fits and ry == 8 and rz % 8 == 0 and x == 4 * LANES
    chosen = body if fits else body_general
    return chosen(state, turbine_x, turbine_y, yaw_index)


def solution(mesh):
    return jax.shard_map(
        body_any,
        mesh=mesh,
        in_specs=(
            P("case", None, "span", "vert", None),
            P("case", None),
            P("case", None),
            P("case"),
        ),
        out_specs=P("case", None, "span", "vert", None),
        check_vma=False,
    )
```

```python
import functools

import jax
import jax.numpy as jnp
from jax import lax
from jax.experimental import pallas as pl
from jax.experimental.pallas import tpu as pltpu
from jax.sharding import PartitionSpec as P

STEPS = 3
DISK = 8
LANES = 128
HALO = 2 * STEPS

U_MEAN = 1.0
VISC = 0.04
THRUST = 0.75
TIME_STEP = 0.1
YAW_STEP = 0.15
HALF = 0.5 * TIME_STEP
SCALES = (HALF * HALF, HALF, HALF, HALF)

ROW0 = 8
STRIP = 16


def flat(blocks):
    _, z, x = blocks.shape[-3:]
    a = blocks.reshape(-1, z, x // LANES, LANES)
    return jnp.swapaxes(a, 1, 2).reshape(-1, LANES)


def unflat(rows, shape):
    _, z, x = shape[-3:]
    a = rows.reshape(-1, x // LANES, z, LANES)
    return jnp.swapaxes(a, 1, 2).reshape(shape)


def away_kernel(dims, state_ref, near_ref, far_ref, block, sem):
    fields, ry, rz, tiles = dims
    size = fields * ry * tiles * rz
    slot = 1 - lax.axis_index("span")
    even = lax.axis_index("vert") % 2 == 0
    start = pl.multiple_of(slot * size, 8)
    copy = pltpu.make_async_copy(state_ref.at[pl.ds(start, size)], block, sem)
    copy.start()
    copy.wait()
    near = jnp.where(even, 0, rz - HALO)
    far = jnp.where(even, HALO, 0)
    for ref, low, count in ((near_ref, near, HALO), (far_ref, far, rz - HALO)):
        for f in range(fields):
            for t in range(tiles):
                for k in range(count):
                    row = (f * ry * tiles + t) * rz + low + k
                    value = block[pl.ds(row, ry, stride=tiles * rz), :]
                    ref[pl.ds(((f * tiles + t) * count + k) * ry, ry), :] = value


def own_kernel(dims, state_ref, after_ref, own_ref, near_ref, fringe_ref, block, first, sems):
    del after_ref
    fields, ry, rz, tiles = dims
    size = fields * ry * tiles * rz
    slot = lax.axis_index("span")
    even = lax.axis_index("vert") % 2 == 0
    start = pl.multiple_of(slot * size, 8)
    copy_first = pltpu.make_async_copy(state_ref.at[pl.ds(0, size)], first, sems.at[0])
    copy_own = pltpu.make_async_copy(state_ref.at[pl.ds(start, size)], block, sems.at[1])
    copy_first.start()
    copy_own.start()
    copy_first.wait()
    lane = lax.broadcasted_iota(jnp.int32, (ry, LANES), 1)
    for f in range(fields):
        strip = jnp.zeros((ry, LANES), jnp.float32)
        for z in range(rz):
            row = f * ry * tiles * rz + z
            step = tiles * rz
            place = f * (rz + 1) + z
            fringe_ref[pl.ds(place * ry, ry), :] = first[pl.ds(row, ry, stride=step), :]
            after = first[pl.ds(row + rz, ry, stride=step), :]
            before = first[pl.ds(row + (tiles - 1) * rz, ry, stride=step), :]
            both = jnp.where(lane < LANES // 2, after, before)
            both = pltpu.roll(both, (HALO + STRIP * z) % LANES, 1)
            here = (lane >= STRIP * z) & (lane < STRIP * z + 2 * HALO)
            strip = jnp.where(here, both, strip)
        fringe_ref[pl.ds((f * (rz + 1) + rz) * ry, ry), :] = strip
    copy_own.wait()
    for f in range(fields):
        for t in range(tiles):
            for z in range(rz):
                row = (f * ry * tiles + t) * rz + z
                value = block[pl.ds(row, ry, stride=tiles * rz), :]
                own_ref[pl.ds(((f * tiles + t) * rz + z) * ry, ry), :] = value
    near = jnp.where(even, 0, rz - HALO)
    for c in range(fields * tiles):
        for k in range(HALO):
            row = pl.multiple_of((c * rz + near + k) * ry, 8)
            near_ref[pl.ds((c * HALO + k) * ry, ry), :] = own_ref[pl.ds(row, ry), :]


def main_kernel(
    dims, xs, ys, yaws, own, got_near, got_far, out_own, out_got, in_own, in_near, in_far,
    p_own, p_got, p_out_own, p_out_got, p_in_own, p_in_got,
    mine_ref, send_ref, q, m, pq, pm, wgt, sides0, sides1,
):
    fields, ry, rz, tiles, nt, slots = dims
    ext = rz + 2 * HALO
    rows = ext + 2
    total_y = 2 * ry
    total_z = rz * lax.axis_size("vert")
    store = 2 * ROW0 + total_y
    groups = total_y // 8
    slot = lax.axis_index("span")
    vert_at = lax.axis_index("vert")
    z0 = vert_at * rz
    even = vert_at % 2 == 0
    dlo = jnp.maximum(HALO - z0, 0)
    dhi = jnp.minimum(HALO + total_z - z0, ext)
    gate = HALO + total_z // 2 - z0
    y_off = slot * ry
    one = 1 + jnp.minimum(vert_at, 0)
    active = jnp.where(lax.axis_index("case") * slots + slot > 0, 1.0, 0.0)
    lane = lax.broadcasted_iota(jnp.int32, (8, LANES), 1)
    sub = lax.broadcasted_iota(jnp.int32, (8, LANES), 0)
    first_lane = lane == 0
    last_lane = lane == LANES - 1
    angle = (jnp.full((8, LANES), yaws[slot], jnp.int32).astype(jnp.float32) - 3.5) * YAW_STEP
    cos_yaw = jnp.cos(angle)
    sin_yaw = jnp.sin(angle)
    ramp = 0.5 * (1.0 - jnp.cos(jnp.pi * (lane.astype(jnp.float32) + 1.0) / LANES))

    def put(dst, width, f, t, z, group, value):
        start = pl.multiple_of(((f * width + t) * rows + z + 1) * store, 8)
        dst[pl.ds(start + (ROW0 + 8 * group), 8), :] = value
        if group == 0:
            dst[pl.ds(start + (ROW0 + total_y), 1), :] = value[0:1]
        if group == groups - 1:
            dst[pl.ds(start + (ROW0 - 1), 1), :] = value[7:8]

    def scale_of(f):
        return jnp.where(f == 0, SCALES[0], SCALES[1])

    def fill(parts):
        def one_field(f, carry):
            for src, held, taken, half, z_dst, count in parts:
                for t in range(tiles):
                    for k in range(count):
                        row = pl.multiple_of(((f * tiles + t) * held + taken + k) * ry, 8)
                        for g in range(ry // 8):
                            value = scale_of(f) * src[pl.ds(row + 8 * g, 8), :]
                            put(q, tiles, f, t, z_dst + k, half * (ry // 8) + g, value)
            return carry

        lax.fori_loop(0, fields, one_field, 0)

    def fill_fringe(parts):
        def one_field(f, carry):
            for src, taken, half, z_dst, count in parts:
                base = f * (rz + 1)
                strip = scale_of(f) * src[pl.ds(pl.multiple_of((base + rz) * ry, 8), ry), :]
                for k in range(count):
                    z = taken + k
                    row = pl.multiple_of((base + z) * ry, 8)
                    put(pq, 2, f, 0, z_dst + k, half, scale_of(f) * src[pl.ds(row, ry), :])
                    value = pltpu.roll(strip, 2 * LANES - HALO - STRIP * z, 1)
                    put(pq, 2, f, 1, z_dst + k, half, value)
            return carry

        lax.fori_loop(0, fields, one_field, 0)

    def pick(a, b):
        return jnp.where(even, a, b)

    above = HALO + rz
    rest = rz - HALO
    fill(
        (
            (own, rz, 0, 0, HALO, rz),
            (in_own, rz, pick(0, rest), 0, pick(above, 0), HALO),
            (out_own, HALO, 0, 0, pick(0, above), HALO),
        )
    )
    fill(
        (
            (got_near, HALO, 0, 1, HALO + pick(0, rest), HALO),
            (got_far, rest, 0, 1, HALO + pick(HALO, 0), rest),
            (out_got, HALO, 0, 1, pick(0, above), HALO),
            (in_near, HALO, pick(0, rest), 1, pick(above + rest, 0), HALO - rest),
            (in_far, rest, 0, 1, pick(above, HALO - rest), rest),
        )
    )
    fill_fringe(
        (
            (p_own, 0, 0, HALO, rz),
            (p_got, 0, 1, HALO, rz),
            (p_out_own, pick(rest, 0), 0, pick(0, above), HALO),
            (p_out_got, pick(rest, 0), 1, pick(0, above), HALO),
            (p_in_own, pick(0, rest), 0, pick(above, 0), HALO),
            (p_in_got, pick(0, rest), 1, pick(above, 0), HALO),
        )
    )

    zero = jnp.zeros((store, LANES), jnp.float32)
    for ref, width in ((m, tiles), (pm, 2), (q, tiles), (pq, 2)):
        for z in (HALO - 1, HALO + rz):
            outside = (z < dlo) | (z >= dhi)

            def clear(ref=ref, width=width, z=z):
                for f in range(fields):
                    for t in range(width):
                        ref[pl.ds(((f * width + t) * rows + z + 1) * store, store), :] = zero

            pl.when(outside)(clear)

    for t in range(1, tiles):
        for g in range(groups):
            acc = jnp.zeros((8, LANES), jnp.float32)
            y = y_off + 8 * g + sub
            for k in range(nt):
                hit = lax.rem(y - ys[slot, k] + 2 * total_y, total_y) < DISK
                hit = hit & (lane + t * LANES == xs[slot, k])
                acc = acc + jnp.where(hit, 1.0, 0.0)
            acc = acc * active
            wgt[0, 0, t, g] = jnp.zeros((8, LANES), jnp.float32)
            wgt[0, 1, t, g] = jnp.zeros((8, LANES), jnp.float32)
            wgt[1, 0, t, g] = acc * (2.0 * THRUST * cos_yaw)
            wgt[1, 1, t, g] = acc * (2.0 * THRUST * sin_yaw)

    def stage(src, base, dst, width, k, is_domain):
        second = k % 2 == 0

        def at(ref, f, t, g, z, dy=0):
            start = ((f * width + t % width) * rows + z + 1) * store + ROW0 + 8 * g
            start = start + dy * one if dy else pl.multiple_of(start, 8)
            return ref[pl.ds(start, 8), :]

        def beside(f, t, g, side):
            return pl.ds((((f * 2 + side) * width + t) * groups + g) * 8, 8)

        def shift(z, into, t, g):
            for f in range(fields):
                c = at(src, f, t, g, z)
                after = at(src, f, t + 1, g, z)
                before = at(src, f, t - 1, g, z)
                east = pltpu.roll(jnp.where(first_lane, after, c), LANES - 1, 1)
                west = pltpu.roll(jnp.where(last_lane, before, c), 1, 1)
                into[beside(f, t, g, 0), :] = east
                into[beside(f, t, g, 1), :] = west

        def row(z, sides, following):
            if is_domain:
                on = jnp.where(z < gate, 1, 0)
            for t in range(width):
                for g in range(groups):
                    shift(z + 1, following, t, g)
                    c = [at(src, f, t, g, z) for f in range(fields)]
                    gx, gy, gz, lap = [], [], [], []
                    for f in range(fields):
                        east = sides[beside(f, t, g, 0), :]
                        west = sides[beside(f, t, g, 1), :]
                        north = at(src, f, t, g, z, dy=1)
                        south = at(src, f, t, g, z, dy=-1)
                        upper = at(src, f, t, g, z + 1)
                        lower = at(src, f, t, g, z - 1)
                        gx.append(east - west)
                        gy.append(north - south)
                        gz.append(upper - lower)
                        around = ((east + west) + (north + south)) + (upper + lower)
                        lap.append(around - 6.0 * c[f])
                    speed = c[1] + HALF * U_MEAN
                    strain = gx[1] * gx[1] + gy[2] * gy[2] + gz[3] * gz[3]
                    strain = strain + gy[1] * gy[1] + gz[1] * gz[1] + 4.0 * HALF * HALF
                    viscous = VISC * (strain * lax.rsqrt(strain))
                    rate = [
                        viscous * lap[f] - (speed * gx[f] + c[2] * gy[f] + c[3] * gz[f])
                        for f in range(fields)
                    ]
                    rate[0] = rate[0] - HALF * HALF * (gx[1] + gy[2] + gz[3])
                    rate[1] = rate[1] - gx[0]
                    rate[2] = rate[2] - gy[0]
                    rate[3] = rate[3] - gz[0]
                    if is_domain and t > 0:
                        normal = speed * cos_yaw + c[2] * sin_yaw
                        thrust = normal * jnp.abs(normal)
                        rate[1] = rate[1] - thrust * wgt[on, 0, t, g]
                        rate[2] = rate[2] - thrust * wgt[on, 1, t, g]
                    for f in range(fields):
                        if second:
                            new = 0.5 * ((at(base, f, t, g, z) + c[f]) + rate[f])
                            if is_domain and t == 0:
                                start = pl.multiple_of((f * 2 * rows + z + 1) * store, 8)
                                new = new + ramp * (pq[pl.ds(start + (ROW0 + 8 * g), 8), :] - new)
                        else:
                            new = c[f] + rate[f]
                        if is_domain and k == HALO:
                            out = mine_ref if g < groups // 2 else send_ref
                            start = ((f * tiles + t) * rz + z - HALO) * ry + 8 * (g % (groups // 2))
                            new = new * (1.0 / SCALES[f])
                            out[pl.ds(pl.multiple_of(start, 8), 8), :] = new
                        else:
                            put(dst, width, f, t, z, g, new)

        first = jnp.maximum(k, dlo)
        count = jnp.minimum(ext - k, dhi) - first
        first = first - jnp.where(dhi < ext, count & 1, 0)
        for t in range(width):
            for g in range(groups):
                shift(first, sides0, t, g)

        def pair(i, carry):
            z = first + 2 * i
            row(z, sides0, sides1)
            row(z + 1, sides1, sides0)
            return carry

        lax.fori_loop(0, (count + 1) // 2, pair, 0)

    for step in range(STEPS):
        k = 2 * step + 1
        stage(pq, None, pm, 2, k, False)
        stage(pm, pq, pq, 2, k + 1, False)
        stage(q, None, m, tiles, k, True)
        stage(m, q, q, tiles, k + 1, True)


def place_kernel(dims, other, *refs):
    fields, ry, rz, tiles = dims
    src, out_ref, block, sems = refs[0], refs[-3], refs[-2], refs[-1]
    size = ry * tiles * rz
    slot = lax.axis_index("span")
    slot = 1 - slot if other else slot
    copies = []
    for f in range(fields):
        for y in range(ry):
            for t in range(tiles):
                value = src[pl.ds((f * tiles + t) * rz * ry + y, rz, stride=ry), :]
                block[pl.ds(((f * ry + y) * tiles + t) * rz, rz), :] = value
        start = pl.multiple_of((slot * fields + f) * size, 8)
        part = block.at[pl.ds(f * size, size)]
        copies.append(pltpu.make_async_copy(part, out_ref.at[pl.ds(start, size)], sems.at[f]))
        copies[-1].start()
    for copy in copies:
        copy.wait()


def swaps(size):
    inner = [(i, i ^ 1) for i in range(size)]
    outer = [(i, i + 1 if i % 2 else i - 1) for i in range(size)]
    outer = [(i, j) for i, j in outer if 0 <= j < size]
    return inner, outer


def spread(value, axis):
    size = lax.axis_size(axis)
    at = lax.axis_index(axis)
    gap = size // 2
    while gap:
        pairs = [(i, i + gap) for i in range(0, size, 2 * gap)]
        moved = lax.ppermute(value, axis, pairs)
        value = jnp.where(at % (2 * gap) == gap, moved, value)
        gap //= 2
    return value


def body(state, turbine_x, turbine_y, yaw_index):
    slots, fields, ry, rz, x = state.shape
    tiles = x // LANES
    nt = turbine_x.shape[1]
    count = fields * ry * tiles * rz
    near_count = count // rz * HALO
    fringe_count = fields * (rz + 1) * ry
    dims = (fields, ry, rz, tiles)
    inner, outer = swaps(lax.axis_size("vert"))
    across = [(0, 1), (1, 0)]
    smem = pl.BlockSpec(memory_space=pltpu.SMEM)
    vmem = pl.BlockSpec(memory_space=pltpu.VMEM)
    hbm = pl.BlockSpec(memory_space=pl.ANY)
    whole = flat(state)

    def rows_of(n):
        return jax.ShapeDtypeStruct((n, LANES), jnp.float32)

    def block_of(n):
        return pltpu.VMEM((n, LANES), jnp.float32)

    away_near, away_far = pl.pallas_call(
        functools.partial(away_kernel, dims),
        out_shape=[rows_of(near_count), rows_of(count - near_count)],
        in_specs=[hbm],
        out_specs=[vmem, vmem],
        scratch_shapes=[block_of(count), pltpu.SemaphoreType.DMA],
        compiler_params=pltpu.CompilerParams(vmem_limit_bytes=8 << 20),
        name="away",
    )(whole)
    got_near = lax.ppermute(away_near, "span", across)
    got_far = lax.ppermute(away_far, "span", across)
    own, near, fringe = pl.pallas_call(
        functools.partial(own_kernel, dims),
        out_shape=[rows_of(count), rows_of(near_count), rows_of(fringe_count)],
        in_specs=[hbm, hbm],
        out_specs=[vmem, vmem, vmem],
        scratch_shapes=[block_of(count), block_of(count), pltpu.SemaphoreType.DMA((2,))],
        compiler_params=pltpu.CompilerParams(vmem_limit_bytes=8 << 20),
        name="own",
    )(whole, away_far)
    out_own = lax.ppermute(near, "vert", outer)
    in_own = lax.ppermute(own, "vert", inner)
    fringe = spread(fringe, "case")
    fringe_got = lax.ppermute(fringe, "span", across)
    out_got = lax.ppermute(got_near, "vert", outer)
    in_near = lax.ppermute(got_near, "vert", inner)
    in_far = lax.ppermute(got_far, "vert", inner)
    fringes = [fringe, fringe_got]
    for pairs in (outer, inner):
        for a in (fringe, fringe_got):
            fringes.append(lax.ppermute(a, "vert", pairs))

    ext = rz + 2 * HALO
    store = 2 * ROW0 + 2 * ry
    mine, send = pl.pallas_call(
        functools.partial(main_kernel, (fields, ry, rz, tiles, nt, slots)),
        out_shape=[rows_of(count)] * 2,
        in_specs=[smem] * 3 + [vmem] * 14,
        out_specs=[vmem, vmem],
        scratch_shapes=[block_of(fields * w * (ext + 2) * store) for w in (tiles, tiles, 2, 2)]
        + [pltpu.VMEM((2, 2, tiles, 2 * ry // 8, 8, LANES), jnp.float32)]
        + [block_of(fields * 2 * tiles * 2 * ry)] * 2,
        compiler_params=pltpu.CompilerParams(vmem_limit_bytes=32 << 20),
        name="steps",
    )(
        turbine_x, turbine_y, yaw_index, own, got_near, got_far, out_own, out_got, in_own, in_near, in_far,
        *fringes,
    )
    back = lax.ppermute(send, "span", across)

    def place(other, block, *earlier):
        return pl.pallas_call(
            functools.partial(place_kernel, dims, other),
            out_shape=rows_of(slots * count),
            in_specs=[vmem] + [hbm] * len(earlier),
            out_specs=hbm,
            scratch_shapes=[block_of(count), pltpu.SemaphoreType.DMA((fields,))],
            input_output_aliases={1: 0} if earlier else {},
            compiler_params=pltpu.CompilerParams(vmem_limit_bytes=8 << 20),
            name="place",
        )(block, *earlier)

    return unflat(place(True, back, place(False, mine)), state.shape)


def extended_2(shard, sides, width):
    for axis, dim in sides:
        size, length = (lax.axis_size(axis), shard.shape[dim])
        up = [(i, (i + 1) % size) for i in range(size)]
        down = [(j, i) for i, j in up]
        last = lax.slice_in_dim(shard, length - width, length, axis=dim)
        leading = lax.slice_in_dim(shard, 0, width, axis=dim)
        before = lax.ppermute(last, axis, up)
        after = lax.ppermute(leading, axis, down)
        shard = jnp.concatenate([before, shard, after], axis=dim)
    return shard


def entering(part, axis, combine, identity):
    place = lax.axis_index(axis)
    gathered = jax.tree.map(lambda a: lax.all_gather(a, axis), part)
    state = jax.tree.map(lambda a, e: jnp.zeros_like(a) + jnp.asarray(e, a.dtype), part, identity)

    def one(step, state):
        return combine(
            state, jax.tree.map(lambda a: lax.dynamic_index_in_dim(a, step, 0, False), gathered)
        )

    return lax.fori_loop(0, place, one, state)


def tendency(center, east, west, north, south, upper, lower, weight, cos_yaw, sin_yaw):
    grad_x = (east - west) * 0.5
    grad_y = (north - south) * 0.5
    grad_z = (upper - lower) * 0.5
    laplace = east + west + north + south + upper + lower - 6.0 * center
    vel_u = center[..., 1, :, :, :]
    vel_v = center[..., 2, :, :, :]
    vel_w = center[..., 3, :, :, :]
    dux = grad_x[..., 1, :, :, :]
    dvy = grad_y[..., 2, :, :, :]
    dwz = grad_z[..., 3, :, :, :]
    duy = grad_y[..., 1, :, :, :]
    duz = grad_z[..., 1, :, :, :]
    strain = dux * dux + dvy * dvy + dwz * dwz + duy * duy + duz * duz
    viscous = VISC * jnp.sqrt(1.0 + strain)
    speed = U_MEAN + vel_u
    flow = -(
        jnp.expand_dims(speed, -4) * grad_x
        + jnp.expand_dims(vel_v, -4) * grad_y
        + jnp.expand_dims(vel_w, -4) * grad_z
    )
    flow = flow + jnp.expand_dims(viscous, -4) * laplace
    normal = speed * cos_yaw + vel_v * sin_yaw
    thrust = THRUST * normal * jnp.abs(normal) * weight
    extra = jnp.stack(
        [
            -(dux + dvy + dwz),
            -grad_x[..., 0, :, :, :] - thrust * cos_yaw,
            -grad_y[..., 0, :, :, :] - thrust * sin_yaw,
            -grad_z[..., 0, :, :, :],
        ],
        axis=-4,
    )
    return flow + extra


def extended(fields):
    padded = extended_2(fields, (("span", 2), ("vert", 3)), 1)
    vert_at = lax.axis_index("vert")
    bottom = jnp.where(vert_at == 0, 0.0, padded[:, :, :, :1, :])
    summit = jnp.where(vert_at == lax.axis_size("vert") - 1, 0.0, padded[:, :, :, -1:, :])
    padded = jnp.concatenate([bottom, padded[:, :, :, 1:-1, :], summit], axis=3)
    return padded


def stencil(fields, padded, weight, cos_yaw, sin_yaw):
    east = jnp.roll(fields, -1, axis=4)
    west = jnp.roll(fields, 1, axis=4)
    north = padded[:, :, 2:, 1:-1, :]
    south = padded[:, :, :-2, 1:-1, :]
    upper = padded[:, :, 1:-1, 2:, :]
    lower = padded[:, :, 1:-1, :-2, :]
    return tendency(fields, east, west, north, south, upper, lower, weight, cos_yaw, sin_yaw)


def rate(fields, weight, cos_yaw, sin_yaw):
    return stencil(fields, extended(fields), weight, cos_yaw, sin_yaw)


def make_weight(turbine_x, turbine_y, along_y, along_z, total_y, total_z, active, length):
    along_x = jnp.arange(length, dtype=jnp.int32)
    hit_x = (along_x[None, None, :] == turbine_x[:, :, None]).astype(jnp.float32)
    hit_y = ((along_y[None, None, :] - turbine_y[:, :, None]) % total_y < DISK).astype(jnp.float32)
    plane = jnp.einsum("dky,dkx->dyx", hit_y, hit_x, precision=lax.Precision.HIGHEST)
    lower_half = (along_z < total_z // 2).astype(jnp.float32)
    return plane[:, :, None, :] * lower_half[None, None, :, None] * active[:, None, None, None]


def first_held(earlier, later):
    keep = earlier[1] > 0.0
    return (jnp.where(keep, earlier[0], later[0]), jnp.maximum(earlier[1], later[1]))


def body_general(state, turbine_x, turbine_y, yaw_index):
    slots = state.shape[0]
    rows_y = state.shape[2]
    rows_z = state.shape[3]
    total_y = rows_y * lax.axis_size("span")
    total_z = rows_z * lax.axis_size("vert")
    domain = lax.axis_index("case") * slots + jnp.arange(slots, dtype=jnp.int32)
    active = (domain > 0).astype(jnp.float32)
    along_y = lax.axis_index("span") * rows_y + jnp.arange(rows_y, dtype=jnp.int32)
    along_z = lax.axis_index("vert") * rows_z + jnp.arange(rows_z, dtype=jnp.int32)
    weight = make_weight(turbine_x, turbine_y, along_y, along_z, total_y, total_z, active, state.shape[4])
    angle = (yaw_index.astype(jnp.float32) - 3.5) * YAW_STEP
    cos_yaw = jnp.cos(angle)[:, None, None, None]
    sin_yaw = jnp.sin(angle)[:, None, None, None]
    width = state.shape[4] // 4
    ramp = 0.5 * (1.0 - jnp.cos(jnp.pi * (jnp.arange(width, dtype=jnp.float32) + 1.0) / width))
    case_at = lax.axis_index("case")
    for _ in range(STEPS):
        first = rate(state, weight, cos_yaw, sin_yaw)
        middle = state + TIME_STEP * first
        second = rate(middle, weight, cos_yaw, sin_yaw)
        state = state + 0.5 * TIME_STEP * (first + second)
        front = state[..., :width]
        own_fringe = front[0]
        marker = jnp.ones((), jnp.float32)
        blank = (jnp.zeros_like(own_fringe), jnp.zeros((), jnp.float32))
        passed = entering((own_fringe, marker), "case", first_held, blank)
        source = jnp.where(case_at == 0, own_fringe, passed[0])
        front = front + ramp * (source[None] - front)
        state = jnp.concatenate([front, state[..., width:]], axis=4)
    return state


def body_any(state, turbine_x, turbine_y, yaw_index):
    slots, _, ry, rz, x = state.shape
    fits = lax.axis_size("span") == 2 and slots == 2 and lax.axis_size("vert") % 2 == 0
    fits = fits and ry == 8 and rz % 8 == 0 and x == 4 * LANES
    chosen = body if fits else body_general
    return chosen(state, turbine_x, turbine_y, yaw_index)


def solution(mesh):
    return jax.shard_map(
        body_any,
        mesh=mesh,
        in_specs=(
            P("case", None, "span", "vert", None),
            P("case", None),
            P("case", None),
            P("case"),
        ),
        out_specs=P("case", None, "span", "vert", None),
        check_vma=False,
    )
```

```python
import functools

import jax
import jax.numpy as jnp
from jax import lax
from jax.experimental import pallas as pl
from jax.experimental.pallas import tpu as pltpu
from jax.sharding import PartitionSpec as P


STEPS = 3
DISK = 8
LANES = 128
HALO = 2 * STEPS

U_MEAN = 1.0
VISC = 0.04
THRUST = 0.75
TIME_STEP = 0.1
YAW_STEP = 0.15
HALF = 0.5 * TIME_STEP
SCALES = (HALF * HALF, HALF, HALF, HALF)

ROW0 = 8
STRIP = 16


def flat(blocks):
    _, z, x = blocks.shape[-3:]
    a = blocks.reshape(-1, z, x // LANES, LANES)
    return jnp.swapaxes(a, 1, 2).reshape(-1, LANES)


def unflat(rows, shape):
    _, z, x = shape[-3:]
    a = rows.reshape(-1, x // LANES, z, LANES)
    return jnp.swapaxes(a, 1, 2).reshape(shape)


def away_kernel(dims, state_ref, near_ref, far_ref, fringe_ref, block, sems):
    fields, ry, rz, tiles = dims
    part = ry * tiles * rz
    step = tiles * rz
    slot = 1 - lax.axis_index("span")
    even = lax.axis_index("vert") % 2 == 0
    copies = []
    for f in range(fields):
        for other in range(2):
            source = (slot * fields + f if other else f) * part
            rows = state_ref.at[pl.ds(pl.multiple_of(source, 8), part)]
            copies.append(pltpu.make_async_copy(rows, block.at[f, other], sems.at[f, other]))
            copies[-1].start()
    near = jnp.where(even, 0, rz - HALO)
    far = jnp.where(even, HALO, 0)
    lane = lax.broadcasted_iota(jnp.int32, (ry, LANES), 1)
    for f in range(fields):
        copies[2 * f].wait()
        first = block.at[f, 0]
        strip = jnp.zeros((ry, LANES), jnp.float32)
        for z in range(rz):
            place = f * (rz + 1) + z
            fringe_ref[pl.ds(place * ry, ry), :] = first[pl.ds(z, ry, stride=step), :]
            after = first[pl.ds(z + rz, ry, stride=step), :]
            before = first[pl.ds(z + (tiles - 1) * rz, ry, stride=step), :]
            both = jnp.where(lane < LANES // 2, after, before)
            both = pltpu.roll(both, (HALO + STRIP * z) % LANES, 1)
            here = (lane >= STRIP * z) & (lane < STRIP * z + 2 * HALO)
            strip = jnp.where(here, both, strip)
        fringe_ref[pl.ds((f * (rz + 1) + rz) * ry, ry), :] = strip
        copies[2 * f + 1].wait()
        other = block.at[f, 1]
        for ref, low, count in ((near_ref, near, HALO), (far_ref, far, rz - HALO)):
            for t in range(tiles):
                for k in range(count):
                    value = other[pl.ds(t * rz + low + k, ry, stride=step), :]
                    ref[pl.ds(((f * tiles + t) * count + k) * ry, ry), :] = value


def own_kernel(dims, state_ref, after_ref, own_ref, near_ref):
    del after_ref
    fields, ry, rz, tiles = dims
    size = fields * ry * tiles * rz
    start = lax.axis_index("span") * size
    even = lax.axis_index("vert") % 2 == 0
    near = jnp.where(even, 0, rz - HALO)
    for f in range(fields):
        for t in range(tiles):
            for z in range(rz):
                row = start + (f * ry * tiles + t) * rz + z
                value = state_ref[pl.ds(row, ry, stride=tiles * rz), :]
                own_ref[pl.ds(((f * tiles + t) * rz + z) * ry, ry), :] = value
    for c in range(fields * tiles):
        for k in range(HALO):
            row = pl.multiple_of((c * rz + near + k) * ry, 8)
            near_ref[pl.ds((c * HALO + k) * ry, ry), :] = own_ref[pl.ds(row, ry), :]


def main_kernel(
    dims, xs, ys, yaws, own, got_near, got_far, out_own, out_got, in_own, in_near, in_far,
    p_own, p_got, p_out_own, p_out_got, p_in_own, p_in_got,
    mine_ref, send_ref, q, m, pq, pm, wgt, sides0, sides1,
):
    fields, ry, rz, tiles, nt, slots = dims
    ext = rz + 2 * HALO
    rows = ext + 2
    total_y = 2 * ry
    total_z = rz * lax.axis_size("vert")
    store = 2 * ROW0 + total_y
    groups = total_y // 8
    slot = lax.axis_index("span")
    vert_at = lax.axis_index("vert")
    z0 = vert_at * rz
    even = vert_at % 2 == 0
    dlo = jnp.maximum(HALO - z0, 0)
    dhi = jnp.minimum(HALO + total_z - z0, ext)
    gate = HALO + total_z // 2 - z0
    y_off = slot * ry
    one = 1 + jnp.minimum(vert_at, 0)
    active = jnp.where(lax.axis_index("case") * slots + slot > 0, 1.0, 0.0)
    lane = lax.broadcasted_iota(jnp.int32, (8, LANES), 1)
    sub = lax.broadcasted_iota(jnp.int32, (8, LANES), 0)
    first_lane = lane == 0
    last_lane = lane == LANES - 1
    angle = (jnp.full((8, LANES), yaws[slot], jnp.int32).astype(jnp.float32) - 3.5) * YAW_STEP
    cos_yaw = jnp.cos(angle)
    sin_yaw = jnp.sin(angle)
    ramp = 0.5 * (1.0 - jnp.cos(jnp.pi * (lane.astype(jnp.float32) + 1.0) / LANES))

    def put(dst, width, f, t, z, group, value):
        start = pl.multiple_of(((f * width + t) * rows + z + 1) * store, 8)
        dst[pl.ds(start + (ROW0 + 8 * group), 8), :] = value
        if group == 0:
            dst[pl.ds(start + (ROW0 + total_y), 1), :] = value[0:1]
        if group == groups - 1:
            dst[pl.ds(start + (ROW0 - 1), 1), :] = value[7:8]

    def scale_of(f):
        return jnp.where(f == 0, SCALES[0], SCALES[1])

    def fill(parts):
        def one_field(f, carry):
            for src, held, taken, half, z_dst, count in parts:
                for t in range(tiles):
                    for k in range(count):
                        row = pl.multiple_of(((f * tiles + t) * held + taken + k) * ry, 8)
                        for g in range(ry // 8):
                            value = scale_of(f) * src[pl.ds(row + 8 * g, 8), :]
                            put(q, tiles, f, t, z_dst + k, half * (ry // 8) + g, value)
            return carry

        lax.fori_loop(0, fields, one_field, 0)

    def fill_fringe(parts):
        def one_field(f, carry):
            for src, taken, half, z_dst, count in parts:
                base = f * (rz + 1)
                strip = scale_of(f) * src[pl.ds(pl.multiple_of((base + rz) * ry, 8), ry), :]
                for k in range(count):
                    z = taken + k
                    row = pl.multiple_of((base + z) * ry, 8)
                    put(pq, 2, f, 0, z_dst + k, half, scale_of(f) * src[pl.ds(row, ry), :])
                    value = pltpu.roll(strip, 2 * LANES - HALO - STRIP * z, 1)
                    put(pq, 2, f, 1, z_dst + k, half, value)
            return carry

        lax.fori_loop(0, fields, one_field, 0)

    def pick(a, b):
        return jnp.where(even, a, b)

    above = HALO + rz
    rest = rz - HALO
    fill(
        (
            (own, rz, 0, 0, HALO, rz),
            (in_own, rz, pick(0, rest), 0, pick(above, 0), HALO),
            (out_own, HALO, 0, 0, pick(0, above), HALO),
        )
    )
    fill(
        (
            (got_near, HALO, 0, 1, HALO + pick(0, rest), HALO),
            (got_far, rest, 0, 1, HALO + pick(HALO, 0), rest),
            (out_got, HALO, 0, 1, pick(0, above), HALO),
            (in_near, HALO, pick(0, rest), 1, pick(above + rest, 0), HALO - rest),
            (in_far, rest, 0, 1, pick(above, HALO - rest), rest),
        )
    )
    fill_fringe(
        (
            (p_own, 0, 0, HALO, rz),
            (p_got, 0, 1, HALO, rz),
            (p_out_own, pick(rest, 0), 0, pick(0, above), HALO),
            (p_out_got, pick(rest, 0), 1, pick(0, above), HALO),
            (p_in_own, pick(0, rest), 0, pick(above, 0), HALO),
            (p_in_got, pick(0, rest), 1, pick(above, 0), HALO),
        )
    )

    zero = jnp.zeros((store, LANES), jnp.float32)
    for ref, width in ((m, tiles), (pm, 2), (q, tiles), (pq, 2)):
        for z in (HALO - 1, HALO + rz):
            outside = (z < dlo) | (z >= dhi)

            def clear(ref=ref, width=width, z=z):
                for f in range(fields):
                    for t in range(width):
                        ref[pl.ds(((f * width + t) * rows + z + 1) * store, store), :] = zero

            pl.when(outside)(clear)

    for t in range(1, tiles):
        for g in range(groups):
            acc = jnp.zeros((8, LANES), jnp.float32)
            y = y_off + 8 * g + sub
            for k in range(nt):
                hit = lax.rem(y - ys[slot, k] + 2 * total_y, total_y) < DISK
                hit = hit & (lane + t * LANES == xs[slot, k])
                acc = acc + jnp.where(hit, 1.0, 0.0)
            acc = acc * active
            wgt[0, 0, t, g] = jnp.zeros((8, LANES), jnp.float32)
            wgt[0, 1, t, g] = jnp.zeros((8, LANES), jnp.float32)
            wgt[1, 0, t, g] = acc * (2.0 * THRUST * cos_yaw)
            wgt[1, 1, t, g] = acc * (2.0 * THRUST * sin_yaw)

    def stage(src, base, dst, width, k, is_domain):
        second = k % 2 == 0

        def at(ref, f, t, g, z, dy=0):
            start = ((f * width + t % width) * rows + z + 1) * store + ROW0 + 8 * g
            start = start + dy * one if dy else pl.multiple_of(start, 8)
            return ref[pl.ds(start, 8), :]

        def beside(f, t, g, side):
            return pl.ds((((f * 2 + side) * width + t) * groups + g) * 8, 8)

        def shift(z, into, t, g):
            for f in range(fields):
                c = at(src, f, t, g, z)
                after = at(src, f, t + 1, g, z)
                before = at(src, f, t - 1, g, z)
                east = pltpu.roll(jnp.where(first_lane, after, c), LANES - 1, 1)
                west = pltpu.roll(jnp.where(last_lane, before, c), 1, 1)
                into[beside(f, t, g, 0), :] = east
                into[beside(f, t, g, 1), :] = west

        def row(z, sides, following):
            if is_domain:
                on = jnp.where(z < gate, 1, 0)
            for t in range(width):
                for g in range(groups):
                    shift(z + 1, following, t, g)
                    c = [at(src, f, t, g, z) for f in range(fields)]
                    gx, gy, gz, lap = [], [], [], []
                    for f in range(fields):
                        east = sides[beside(f, t, g, 0), :]
                        west = sides[beside(f, t, g, 1), :]
                        north = at(src, f, t, g, z, dy=1)
                        south = at(src, f, t, g, z, dy=-1)
                        upper = at(src, f, t, g, z + 1)
                        lower = at(src, f, t, g, z - 1)
                        gx.append(east - west)
                        gy.append(north - south)
                        gz.append(upper - lower)
                        around = ((east + west) + (north + south)) + (upper + lower)
                        lap.append(around - 6.0 * c[f])
                    speed = c[1] + HALF * U_MEAN
                    strain = gx[1] * gx[1] + gy[2] * gy[2] + gz[3] * gz[3]
                    strain = strain + gy[1] * gy[1] + gz[1] * gz[1] + 4.0 * HALF * HALF
                    viscous = VISC * (strain * lax.rsqrt(strain))
                    rate = [
                        viscous * lap[f] - (speed * gx[f] + c[2] * gy[f] + c[3] * gz[f])
                        for f in range(fields)
                    ]
                    rate[0] = rate[0] - HALF * HALF * (gx[1] + gy[2] + gz[3])
                    rate[1] = rate[1] - gx[0]
                    rate[2] = rate[2] - gy[0]
                    rate[3] = rate[3] - gz[0]
                    if is_domain and t > 0:
                        normal = speed * cos_yaw + c[2] * sin_yaw
                        thrust = normal * jnp.abs(normal)
                        rate[1] = rate[1] - thrust * wgt[on, 0, t, g]
                        rate[2] = rate[2] - thrust * wgt[on, 1, t, g]
                    for f in range(fields):
                        if second:
                            new = 0.5 * ((at(base, f, t, g, z) + c[f]) + rate[f])
                            if is_domain and t == 0:
                                start = pl.multiple_of((f * 2 * rows + z + 1) * store, 8)
                                new = new + ramp * (pq[pl.ds(start + (ROW0 + 8 * g), 8), :] - new)
                        else:
                            new = c[f] + rate[f]
                        if is_domain and k == HALO:
                            out = mine_ref if g < groups // 2 else send_ref
                            start = ((f * tiles + t) * rz + z - HALO) * ry + 8 * (g % (groups // 2))
                            new = new * (1.0 / SCALES[f])
                            out[pl.ds(pl.multiple_of(start, 8), 8), :] = new
                        else:
                            put(dst, width, f, t, z, g, new)

        first = jnp.maximum(k, dlo)
        count = jnp.minimum(ext - k, dhi) - first
        first = first - jnp.where(dhi < ext, count & 1, 0)
        for t in range(width):
            for g in range(groups):
                shift(first, sides0, t, g)

        def pair(i, carry):
            z = first + 2 * i
            row(z, sides0, sides1)
            row(z + 1, sides1, sides0)
            return carry

        lax.fori_loop(0, (count + 1) // 2, pair, 0)

    for step in range(STEPS):
        k = 2 * step + 1
        stage(pq, None, pm, 2, k, False)
        stage(pm, pq, pq, 2, k + 1, False)
        stage(q, None, m, tiles, k, True)
        stage(m, q, q, tiles, k + 1, True)


def place_kernel(dims, other, *refs):
    fields, ry, rz, tiles = dims
    src, out_ref, block, sems = refs[0], refs[-3], refs[-2], refs[-1]
    size = ry * tiles * rz
    slot = lax.axis_index("span")
    slot = 1 - slot if other else slot
    copies = []
    for f in range(fields):
        for y in range(ry):
            for t in range(tiles):
                value = src[pl.ds((f * tiles + t) * rz * ry + y, rz, stride=ry), :]
                block[pl.ds(((f * ry + y) * tiles + t) * rz, rz), :] = value
        start = pl.multiple_of((slot * fields + f) * size, 8)
        part = block.at[pl.ds(f * size, size)]
        copies.append(pltpu.make_async_copy(part, out_ref.at[pl.ds(start, size)], sems.at[f]))
        copies[-1].start()
    for copy in copies:
        copy.wait()


def swaps(size):
    inner = [(i, i ^ 1) for i in range(size)]
    outer = [(i, i + 1 if i % 2 else i - 1) for i in range(size)]
    outer = [(i, j) for i, j in outer if 0 <= j < size]
    return inner, outer


def spread(value, axis):
    size = lax.axis_size(axis)
    at = lax.axis_index(axis)
    gap = size // 2
    while gap:
        pairs = [(i, i + gap) for i in range(0, size, 2 * gap)]
        moved = lax.ppermute(value, axis, pairs)
        value = jnp.where(at % (2 * gap) == gap, moved, value)
        gap //= 2
    return value


def body(state, turbine_x, turbine_y, yaw_index):
    slots, fields, ry, rz, x = state.shape
    tiles = x // LANES
    nt = turbine_x.shape[1]
    count = fields * ry * tiles * rz
    near_count = count // rz * HALO
    fringe_count = fields * (rz + 1) * ry
    dims = (fields, ry, rz, tiles)
    inner, outer = swaps(lax.axis_size("vert"))
    across = [(0, 1), (1, 0)]
    smem = pl.BlockSpec(memory_space=pltpu.SMEM)
    vmem = pl.BlockSpec(memory_space=pltpu.VMEM)
    hbm = pl.BlockSpec(memory_space=pl.ANY)
    whole = flat(state)

    def rows_of(n):
        return jax.ShapeDtypeStruct((n, LANES), jnp.float32)

    def block_of(n):
        return pltpu.VMEM((n, LANES), jnp.float32)

    away_near, away_far, fringe = pl.pallas_call(
        functools.partial(away_kernel, dims),
        out_shape=[rows_of(near_count), rows_of(count - near_count), rows_of(fringe_count)],
        in_specs=[pl.BlockSpec(memory_space=pltpu.HBM)],
        out_specs=[vmem] * 3,
        scratch_shapes=[
            pltpu.VMEM((fields, 2, count // fields, LANES), jnp.float32),
            pltpu.SemaphoreType.DMA((fields, 2)),
        ],
        compiler_params=pltpu.CompilerParams(vmem_limit_bytes=8 << 20),
        name="away",
    )(whole)
    got_near = lax.ppermute(away_near, "span", across)
    got_far = lax.ppermute(away_far, "span", across)
    own, near = pl.pallas_call(
        functools.partial(own_kernel, dims),
        out_shape=[rows_of(count), rows_of(near_count)],
        in_specs=[vmem, hbm],
        out_specs=[vmem] * 2,
        compiler_params=pltpu.CompilerParams(vmem_limit_bytes=8 << 20),
        name="own",
    )(whole, away_far)
    out_own = lax.ppermute(near, "vert", outer)
    in_own = lax.ppermute(own, "vert", inner)
    fringe = spread(fringe, "case")
    fringe_got = lax.ppermute(fringe, "span", across)
    out_got = lax.ppermute(got_near, "vert", outer)
    in_near = lax.ppermute(got_near, "vert", inner)
    in_far = lax.ppermute(got_far, "vert", inner)
    fringes = [fringe, fringe_got]
    for pairs in (outer, inner):
        for a in (fringe, fringe_got):
            fringes.append(lax.ppermute(a, "vert", pairs))

    ext = rz + 2 * HALO
    store = 2 * ROW0 + 2 * ry
    mine, send = pl.pallas_call(
        functools.partial(main_kernel, (fields, ry, rz, tiles, nt, slots)),
        out_shape=[rows_of(count)] * 2,
        in_specs=[smem] * 3 + [vmem] * 14,
        out_specs=[vmem, vmem],
        scratch_shapes=[block_of(fields * w * (ext + 2) * store) for w in (tiles, tiles, 2, 2)]
        + [pltpu.VMEM((2, 2, tiles, 2 * ry // 8, 8, LANES), jnp.float32)]
        + [block_of(fields * 2 * tiles * 2 * ry)] * 2,
        compiler_params=pltpu.CompilerParams(vmem_limit_bytes=32 << 20),
        name="steps",
    )(
        turbine_x, turbine_y, yaw_index, own, got_near, got_far, out_own, out_got, in_own, in_near, in_far,
        *fringes,
    )
    back = lax.ppermute(send, "span", across)

    def place(other, block, *earlier):
        return pl.pallas_call(
            functools.partial(place_kernel, dims, other),
            out_shape=rows_of(slots * count),
            in_specs=[vmem] + [hbm] * len(earlier),
            out_specs=hbm,
            scratch_shapes=[block_of(count), pltpu.SemaphoreType.DMA((fields,))],
            input_output_aliases={1: 0} if earlier else {},
            compiler_params=pltpu.CompilerParams(vmem_limit_bytes=8 << 20),
            name="place",
        )(block, *earlier)

    return unflat(place(True, back, place(False, mine)), state.shape)


def extended_2(shard, sides, width):
    for axis, dim in sides:
        size, length = (lax.axis_size(axis), shard.shape[dim])
        up = [(i, (i + 1) % size) for i in range(size)]
        down = [(j, i) for i, j in up]
        last = lax.slice_in_dim(shard, length - width, length, axis=dim)
        leading = lax.slice_in_dim(shard, 0, width, axis=dim)
        before = lax.ppermute(last, axis, up)
        after = lax.ppermute(leading, axis, down)
        shard = jnp.concatenate([before, shard, after], axis=dim)
    return shard


def entering(part, axis, combine, identity):
    place = lax.axis_index(axis)
    gathered = jax.tree.map(lambda a: lax.all_gather(a, axis), part)
    state = jax.tree.map(lambda a, e: jnp.zeros_like(a) + jnp.asarray(e, a.dtype), part, identity)

    def one(step, state):
        return combine(
            state, jax.tree.map(lambda a: lax.dynamic_index_in_dim(a, step, 0, False), gathered)
        )

    return lax.fori_loop(0, place, one, state)


def tendency(center, east, west, north, south, upper, lower, weight, cos_yaw, sin_yaw):
    grad_x = (east - west) * 0.5
    grad_y = (north - south) * 0.5
    grad_z = (upper - lower) * 0.5
    laplace = east + west + north + south + upper + lower - 6.0 * center
    vel_u = center[..., 1, :, :, :]
    vel_v = center[..., 2, :, :, :]
    vel_w = center[..., 3, :, :, :]
    dux = grad_x[..., 1, :, :, :]
    dvy = grad_y[..., 2, :, :, :]
    dwz = grad_z[..., 3, :, :, :]
    duy = grad_y[..., 1, :, :, :]
    duz = grad_z[..., 1, :, :, :]
    strain = dux * dux + dvy * dvy + dwz * dwz + duy * duy + duz * duz
    viscous = VISC * jnp.sqrt(1.0 + strain)
    speed = U_MEAN + vel_u
    flow = -(
        jnp.expand_dims(speed, -4) * grad_x
        + jnp.expand_dims(vel_v, -4) * grad_y
        + jnp.expand_dims(vel_w, -4) * grad_z
    )
    flow = flow + jnp.expand_dims(viscous, -4) * laplace
    normal = speed * cos_yaw + vel_v * sin_yaw
    thrust = THRUST * normal * jnp.abs(normal) * weight
    extra = jnp.stack(
        [
            -(dux + dvy + dwz),
            -grad_x[..., 0, :, :, :] - thrust * cos_yaw,
            -grad_y[..., 0, :, :, :] - thrust * sin_yaw,
            -grad_z[..., 0, :, :, :],
        ],
        axis=-4,
    )
    return flow + extra


def extended(fields):
    padded = extended_2(fields, (("span", 2), ("vert", 3)), 1)
    vert_at = lax.axis_index("vert")
    bottom = jnp.where(vert_at == 0, 0.0, padded[:, :, :, :1, :])
    summit = jnp.where(vert_at == lax.axis_size("vert") - 1, 0.0, padded[:, :, :, -1:, :])
    padded = jnp.concatenate([bottom, padded[:, :, :, 1:-1, :], summit], axis=3)
    return padded


def stencil(fields, padded, weight, cos_yaw, sin_yaw):
    east = jnp.roll(fields, -1, axis=4)
    west = jnp.roll(fields, 1, axis=4)
    north = padded[:, :, 2:, 1:-1, :]
    south = padded[:, :, :-2, 1:-1, :]
    upper = padded[:, :, 1:-1, 2:, :]
    lower = padded[:, :, 1:-1, :-2, :]
    return tendency(fields, east, west, north, south, upper, lower, weight, cos_yaw, sin_yaw)


def rate(fields, weight, cos_yaw, sin_yaw):
    return stencil(fields, extended(fields), weight, cos_yaw, sin_yaw)


def make_weight(turbine_x, turbine_y, along_y, along_z, total_y, total_z, active, length):
    along_x = jnp.arange(length, dtype=jnp.int32)
    hit_x = (along_x[None, None, :] == turbine_x[:, :, None]).astype(jnp.float32)
    hit_y = ((along_y[None, None, :] - turbine_y[:, :, None]) % total_y < DISK).astype(jnp.float32)
    plane = jnp.einsum("dky,dkx->dyx", hit_y, hit_x, precision=lax.Precision.HIGHEST)
    lower_half = (along_z < total_z // 2).astype(jnp.float32)
    return plane[:, :, None, :] * lower_half[None, None, :, None] * active[:, None, None, None]


def first_held(earlier, later):
    keep = earlier[1] > 0.0
    return (jnp.where(keep, earlier[0], later[0]), jnp.maximum(earlier[1], later[1]))


def body_general(state, turbine_x, turbine_y, yaw_index):
    slots = state.shape[0]
    rows_y = state.shape[2]
    rows_z = state.shape[3]
    total_y = rows_y * lax.axis_size("span")
    total_z = rows_z * lax.axis_size("vert")
    domain = lax.axis_index("case") * slots + jnp.arange(slots, dtype=jnp.int32)
    active = (domain > 0).astype(jnp.float32)
    along_y = lax.axis_index("span") * rows_y + jnp.arange(rows_y, dtype=jnp.int32)
    along_z = lax.axis_index("vert") * rows_z + jnp.arange(rows_z, dtype=jnp.int32)
    weight = make_weight(turbine_x, turbine_y, along_y, along_z, total_y, total_z, active, state.shape[4])
    angle = (yaw_index.astype(jnp.float32) - 3.5) * YAW_STEP
    cos_yaw = jnp.cos(angle)[:, None, None, None]
    sin_yaw = jnp.sin(angle)[:, None, None, None]
    width = state.shape[4] // 4
    ramp = 0.5 * (1.0 - jnp.cos(jnp.pi * (jnp.arange(width, dtype=jnp.float32) + 1.0) / width))
    case_at = lax.axis_index("case")
    for _ in range(STEPS):
        first = rate(state, weight, cos_yaw, sin_yaw)
        middle = state + TIME_STEP * first
        second = rate(middle, weight, cos_yaw, sin_yaw)
        state = state + 0.5 * TIME_STEP * (first + second)
        front = state[..., :width]
        own_fringe = front[0]
        marker = jnp.ones((), jnp.float32)
        blank = (jnp.zeros_like(own_fringe), jnp.zeros((), jnp.float32))
        passed = entering((own_fringe, marker), "case", first_held, blank)
        source = jnp.where(case_at == 0, own_fringe, passed[0])
        front = front + ramp * (source[None] - front)
        state = jnp.concatenate([front, state[..., width:]], axis=4)
    return state


def body_any(state, turbine_x, turbine_y, yaw_index):
    slots, _, ry, rz, x = state.shape
    fits = lax.axis_size("span") == 2 and slots == 2 and lax.axis_size("vert") % 2 == 0
    fits = fits and ry == 8 and rz % 8 == 0 and x == 4 * LANES
    chosen = body if fits else body_general
    return chosen(state, turbine_x, turbine_y, yaw_index)


def solution(mesh):
    return jax.shard_map(
        body_any,
        mesh=mesh,
        in_specs=(
            P("case", None, "span", "vert", None),
            P("case", None),
            P("case", None),
            P("case"),
        ),
        out_specs=P("case", None, "span", "vert", None),
        check_vma=False,
    )
```

```python
import functools

import jax
import jax.numpy as jnp
from jax import lax
from jax.experimental import pallas as pl
from jax.experimental.pallas import tpu as pltpu
from jax.sharding import PartitionSpec as P


STEPS = 3
DISK = 8
LANES = 128
HALO = 2 * STEPS

U_MEAN = 1.0
VISC = 0.04
THRUST = 0.75
TIME_STEP = 0.1
YAW_STEP = 0.15
HALF = 0.5 * TIME_STEP
SCALES = (HALF * HALF, HALF, HALF, HALF)

ROW0 = 8
STRIP = 16


def flat(blocks):
    _, z, x = blocks.shape[-3:]
    a = blocks.reshape(-1, z, x // LANES, LANES)
    return jnp.swapaxes(a, 1, 2).reshape(-1, LANES)


def unflat(rows, shape):
    _, z, x = shape[-3:]
    a = rows.reshape(-1, x // LANES, z, LANES)
    return jnp.swapaxes(a, 1, 2).reshape(shape)


def away_kernel(dims, state_ref, near_ref, far_ref):
    fields, ry, rz, tiles = dims
    part = ry * tiles * rz
    slot = 1 - lax.axis_index("span")
    even = lax.axis_index("vert") % 2 == 0
    near = jnp.where(even, 0, rz - HALO)
    far = jnp.where(even, HALO, 0)
    for f in range(fields):
        base = (slot * fields + f) * part
        for ref, low, count in ((near_ref, near, HALO), (far_ref, far, rz - HALO)):
            for t in range(tiles):
                for k in range(count):
                    value = state_ref[pl.ds(base + t * rz + low + k, ry, stride=tiles * rz), :]
                    ref[pl.ds(((f * tiles + t) * count + k) * ry, ry), :] = value


def fringe_kernel(dims, held_ref, fringe_ref):
    fields, ry, rz, tiles = dims
    step = tiles * rz
    lane = lax.broadcasted_iota(jnp.int32, (ry, LANES), 1)
    for f in range(fields):
        base = f * ry * step
        strip = jnp.zeros((ry, LANES), jnp.float32)
        for z in range(rz):
            place = f * (rz + 1) + z
            row = base + z
            fringe_ref[pl.ds(place * ry, ry), :] = held_ref[pl.ds(row, ry, stride=step), :]
            after = held_ref[pl.ds(row + rz, ry, stride=step), :]
            before = held_ref[pl.ds(row + (tiles - 1) * rz, ry, stride=step), :]
            both = jnp.where(lane < LANES // 2, after, before)
            both = pltpu.roll(both, (HALO + STRIP * z) % LANES, 1)
            here = (lane >= STRIP * z) & (lane < STRIP * z + 2 * HALO)
            strip = jnp.where(here, both, strip)
        fringe_ref[pl.ds((f * (rz + 1) + rz) * ry, ry), :] = strip


def own_kernel(dims, state_ref, own_ref, near_ref):
    fields, ry, rz, tiles = dims
    size = fields * ry * tiles * rz
    start = lax.axis_index("span") * size
    even = lax.axis_index("vert") % 2 == 0
    near = jnp.where(even, 0, rz - HALO)
    for f in range(fields):
        for t in range(tiles):
            for z in range(rz):
                row = start + (f * ry * tiles + t) * rz + z
                value = state_ref[pl.ds(row, ry, stride=tiles * rz), :]
                own_ref[pl.ds(((f * tiles + t) * rz + z) * ry, ry), :] = value
    for c in range(fields * tiles):
        for k in range(HALO):
            row = pl.multiple_of((c * rz + near + k) * ry, 8)
            near_ref[pl.ds((c * HALO + k) * ry, ry), :] = own_ref[pl.ds(row, ry), :]


def weights_kernel(dims, xs, ys, yaws, trig, wgt):
    ry, tiles, nt, slots = dims
    total_y = 2 * ry
    slot = lax.axis_index("span")
    active = jnp.where(lax.axis_index("case") * slots + slot > 0, 1.0, 0.0)
    lane = lax.broadcasted_iota(jnp.int32, (8, LANES), 1)
    sub = lax.broadcasted_iota(jnp.int32, (8, LANES), 0)
    angle = jnp.full((8, LANES), yaws[slot], jnp.int32).astype(jnp.float32)
    angle = (angle - 3.5) * YAW_STEP
    cos_yaw = jnp.cos(angle)
    sin_yaw = jnp.sin(angle)
    trig[0] = cos_yaw
    trig[1] = sin_yaw
    trig[2] = 0.5 * (1.0 - jnp.cos(jnp.pi * (lane.astype(jnp.float32) + 1.0) / LANES))
    for t in range(1, tiles):
        for g in range(total_y // 8):
            acc = jnp.zeros((8, LANES), jnp.float32)
            y = slot * ry + 8 * g + sub
            for k in range(nt):
                hit = lax.rem(y - ys[slot, k] + 2 * total_y, total_y) < DISK
                hit = hit & (lane + t * LANES == xs[slot, k])
                acc = acc + jnp.where(hit, 1.0, 0.0)
            acc = acc * (active * (2.0 * THRUST))
            wgt[0, 0, t, g] = jnp.zeros((8, LANES), jnp.float32)
            wgt[0, 1, t, g] = jnp.zeros((8, LANES), jnp.float32)
            wgt[1, 0, t, g] = acc * cos_yaw
            wgt[1, 1, t, g] = acc * sin_yaw


class Cells:

    def __init__(self, dims, trig):
        self.dims = fields, ry, rz, tiles = dims
        self.ext = rz + 2 * HALO
        self.rows = self.ext + 2
        self.total_y = 2 * ry
        self.store = 2 * ROW0 + self.total_y
        self.groups = self.total_y // 8
        total_z = rz * lax.axis_size("vert")
        self.slot = lax.axis_index("span")
        vert_at = lax.axis_index("vert")
        z0 = vert_at * rz
        self.even = vert_at % 2 == 0
        self.dlo = jnp.maximum(HALO - z0, 0)
        self.dhi = jnp.minimum(HALO + total_z - z0, self.ext)
        self.gate = HALO + total_z // 2 - z0
        self.one = 1 + jnp.minimum(vert_at, 0)
        self.lane = lax.broadcasted_iota(jnp.int32, (8, LANES), 1)
        self.first_lane = self.lane == 0
        self.last_lane = self.lane == LANES - 1
        self.cos_yaw, self.sin_yaw, self.ramp = trig[0], trig[1], trig[2]

    def put(self, dst, width, f, t, z, group, value):
        start = pl.multiple_of(((f * width + t) * self.rows + z + 1) * self.store, 8)
        dst[pl.ds(start + (ROW0 + 8 * group), 8), :] = value
        if group == 0:
            dst[pl.ds(start + (ROW0 + self.total_y), 1), :] = value[0:1]
        if group == self.groups - 1:
            dst[pl.ds(start + (ROW0 - 1), 1), :] = value[7:8]

    def clear_outside(self, *refs):
        fields, rz = self.dims[0], self.dims[2]
        zero = jnp.zeros((self.store, LANES), jnp.float32)
        for ref, width in refs:
            for z in (HALO - 1, HALO + rz):

                def clear(ref=ref, width=width, z=z):
                    for c in range(fields * width):
                        ref[pl.ds((c * self.rows + z + 1) * self.store, self.store), :] = zero

                pl.when((z < self.dlo) | (z >= self.dhi))(clear)

    def stage(self, src, base, dst, width, k, wgt=None, pq=None, outs=None):
        second = k % 2 == 0
        fields, ry, rz, tiles = self.dims
        rows, store, ext, groups, one = self.rows, self.store, self.ext, self.groups, self.one
        dlo, dhi, gate = self.dlo, self.dhi, self.gate
        cos_yaw, sin_yaw, ramp = self.cos_yaw, self.sin_yaw, self.ramp
        first_lane, last_lane, sides0, sides1 = self.first_lane, self.last_lane, *self.sides

        def at(ref, f, t, g, z, dy=0):
            start = ((f * width + t % width) * rows + z + 1) * store + ROW0 + 8 * g
            start = start + dy * one if dy else pl.multiple_of(start, 8)
            return ref[pl.ds(start, 8), :]

        def beside(f, t, g, side):
            return pl.ds((((f * 2 + side) * width + t) * groups + g) * 8, 8)

        def shift(z, into, t, g):
            for f in range(fields):
                c = at(src, f, t, g, z)
                after = at(src, f, t + 1, g, z)
                before = at(src, f, t - 1, g, z)
                east = pltpu.roll(jnp.where(first_lane, after, c), LANES - 1, 1)
                west = pltpu.roll(jnp.where(last_lane, before, c), 1, 1)
                into[beside(f, t, g, 0), :] = east
                into[beside(f, t, g, 1), :] = west

        def row(z, sides, following):
            if wgt is not None:
                on = jnp.where(z < gate, 1, 0)
            for t in range(width):
                for g in range(groups):
                    shift(z + 1, following, t, g)
                    c = [at(src, f, t, g, z) for f in range(fields)]
                    gx, gy, gz, lap = [], [], [], []
                    for f in range(fields):
                        east = sides[beside(f, t, g, 0), :]
                        west = sides[beside(f, t, g, 1), :]
                        north = at(src, f, t, g, z, dy=1)
                        south = at(src, f, t, g, z, dy=-1)
                        upper = at(src, f, t, g, z + 1)
                        lower = at(src, f, t, g, z - 1)
                        gx.append(east - west)
                        gy.append(north - south)
                        gz.append(upper - lower)
                        around = ((east + west) + (north + south)) + (upper + lower)
                        lap.append(around - 6.0 * c[f])
                    speed = c[1] + HALF * U_MEAN
                    strain = gx[1] * gx[1] + gy[2] * gy[2] + gz[3] * gz[3]
                    strain = strain + gy[1] * gy[1] + gz[1] * gz[1] + 4.0 * HALF * HALF
                    viscous = VISC * (strain * lax.rsqrt(strain))
                    rate = [
                        viscous * lap[f] - (speed * gx[f] + c[2] * gy[f] + c[3] * gz[f])
                        for f in range(fields)
                    ]
                    rate[0] = rate[0] - HALF * HALF * (gx[1] + gy[2] + gz[3])
                    rate[1] = rate[1] - gx[0]
                    rate[2] = rate[2] - gy[0]
                    rate[3] = rate[3] - gz[0]
                    if wgt is not None and t > 0:
                        normal = speed * cos_yaw + c[2] * sin_yaw
                        thrust = normal * jnp.abs(normal)
                        rate[1] = rate[1] - thrust * wgt[on, 0, t, g]
                        rate[2] = rate[2] - thrust * wgt[on, 1, t, g]
                    for f in range(fields):
                        if second:
                            new = 0.5 * ((at(base, f, t, g, z) + c[f]) + rate[f])
                            if pq is not None and t == 0:
                                start = pl.multiple_of((f * 2 * rows + z + 1) * store, 8)
                                new = new + ramp * (pq[pl.ds(start + (ROW0 + 8 * g), 8), :] - new)
                        else:
                            new = c[f] + rate[f]
                        if outs is not None:
                            out = outs[0] if g < groups // 2 else outs[1]
                            start = ((f * tiles + t) * rz + z - HALO) * ry + 8 * (g % (groups // 2))
                            new = new * (1.0 / SCALES[f])
                            out[pl.ds(pl.multiple_of(start, 8), 8), :] = new
                        else:
                            self.put(dst, width, f, t, z, g, new)

        first = jnp.maximum(k, dlo)
        count = jnp.minimum(ext - k, dhi) - first
        first = first - jnp.where(dhi < ext, count & 1, 0)
        for t in range(width):
            for g in range(groups):
                shift(first, sides0, t, g)

        def pair(i, carry):
            z = first + 2 * i
            row(z, sides0, sides1)
            row(z + 1, sides1, sides0)
            return carry

        lax.fori_loop(0, (count + 1) // 2, pair, 0)


def scale_of(f):
    return jnp.where(f == 0, SCALES[0], SCALES[1])


def first_kernel(
    dims, trig, wgt, own, got_near, got_far, out_own, out_got, in_own, in_near, in_far,
    q, m, sides0, sides1,
):
    fields, ry, rz, tiles = dims
    cells = Cells(dims, trig)
    cells.sides = sides0, sides1
    put = cells.put

    def fill(parts):
        def one_field(f, carry):
            for src, held, taken, half, z_dst, count in parts:
                for t in range(tiles):
                    for k in range(count):
                        row = pl.multiple_of(((f * tiles + t) * held + taken + k) * ry, 8)
                        for g in range(ry // 8):
                            value = scale_of(f) * src[pl.ds(row + 8 * g, 8), :]
                            put(q, tiles, f, t, z_dst + k, half * (ry // 8) + g, value)
            return carry

        lax.fori_loop(0, fields, one_field, 0)

    def pick(a, b):
        return jnp.where(cells.even, a, b)

    above = HALO + rz
    rest = rz - HALO
    fill(
        (
            (own, rz, 0, 0, HALO, rz),
            (in_own, rz, pick(0, rest), 0, pick(above, 0), HALO),
            (out_own, HALO, 0, 0, pick(0, above), HALO),
        )
    )
    fill(
        (
            (got_near, HALO, 0, 1, HALO + pick(0, rest), HALO),
            (got_far, rest, 0, 1, HALO + pick(HALO, 0), rest),
            (out_got, HALO, 0, 1, pick(0, above), HALO),
            (in_near, HALO, pick(0, rest), 1, pick(above + rest, 0), HALO - rest),
            (in_far, rest, 0, 1, pick(above, HALO - rest), rest),
        )
    )
    cells.clear_outside((q, tiles), (m, tiles))
    cells.stage(q, None, m, tiles, 1, wgt)
    cells.stage(m, q, q, tiles, 2, wgt)


def rest_kernel(
    dims, trig, wgt, q_in, p_own, p_out, p_in, mine_ref, send_ref, q, m, pq, pm, sides0, sides1
):
    del q_in
    fields, ry, rz, tiles = dims
    cells = Cells(dims, trig)
    cells.sides = sides0, sides1
    put = cells.put

    def fill_fringe(parts):
        def one_field(f, carry):
            for src, taken, half, z_dst, count in parts:
                base = (half * fields + f) * (rz + 1)
                strip = scale_of(f) * src[pl.ds(pl.multiple_of((base + rz) * ry, 8), ry), :]
                for k in range(count):
                    z = taken + k
                    row = pl.multiple_of((base + z) * ry, 8)
                    put(pq, 2, f, 0, z_dst + k, half, scale_of(f) * src[pl.ds(row, ry), :])
                    value = pltpu.roll(strip, 2 * LANES - HALO - STRIP * z, 1)
                    put(pq, 2, f, 1, z_dst + k, half, value)
            return carry

        lax.fori_loop(0, fields, one_field, 0)

    def pick(a, b):
        return jnp.where(cells.even, a, b)

    above = HALO + rz
    rest = rz - HALO
    for half in range(2):
        fill_fringe(
            (
                (p_own, 0, half, HALO, rz),
                (p_out, pick(rest, 0), half, pick(0, above), HALO),
                (p_in, pick(0, rest), half, pick(above, 0), HALO),
            )
        )
    cells.clear_outside((pq, 2), (pm, 2), (m, tiles))
    for step in range(STEPS):
        k = 2 * step + 1
        cells.stage(pq, None, pm, 2, k)
        cells.stage(pm, pq, pq, 2, k + 1)
        if step == 0:

            def relax(z, carry):
                for f in range(fields):
                    for g in range(cells.groups):
                        row = (f * tiles * cells.rows + z + 1) * cells.store + ROW0 + 8 * g
                        source = (f * 2 * cells.rows + z + 1) * cells.store + ROW0 + 8 * g
                        value = q[pl.ds(pl.multiple_of(row, 8), 8), :]
                        value = value + cells.ramp * (pq[pl.ds(pl.multiple_of(source, 8), 8), :] - value)
                        put(q, tiles, f, 0, z, g, value)
                return carry

            low = jnp.maximum(k + 1, cells.dlo)
            lax.fori_loop(low, jnp.minimum(cells.ext - k - 1, cells.dhi), relax, 0)
        else:
            last = (mine_ref, send_ref) if step == STEPS - 1 else None
            cells.stage(q, None, m, tiles, k, wgt)
            cells.stage(m, q, q, tiles, k + 1, wgt, pq, last)


def place_kernel(dims, other, *refs):
    fields, ry, rz, tiles = dims
    src, out_ref, block, sems = refs[0], refs[-3], refs[-2], refs[-1]
    size = ry * tiles * rz
    slot = lax.axis_index("span")
    slot = 1 - slot if other else slot
    copies = []
    for f in range(fields):
        for y in range(ry):
            for t in range(tiles):
                value = src[pl.ds((f * tiles + t) * rz * ry + y, rz, stride=ry), :]
                block[pl.ds(((f * ry + y) * tiles + t) * rz, rz), :] = value
        start = pl.multiple_of((slot * fields + f) * size, 8)
        part = block.at[pl.ds(f * size, size)]
        copies.append(pltpu.make_async_copy(part, out_ref.at[pl.ds(start, size)], sems.at[f]))
        copies[-1].start()
    for copy in copies:
        copy.wait()


def swaps(size):
    inner = [(i, i ^ 1) for i in range(size)]
    outer = [(i, i + 1 if i % 2 else i - 1) for i in range(size)]
    outer = [(i, j) for i, j in outer if 0 <= j < size]
    return inner, outer


def spread(value, axis):
    size = lax.axis_size(axis)
    at = lax.axis_index(axis)
    gap = size // 2
    while gap:
        pairs = [(i, i + gap) for i in range(0, size, 2 * gap)]
        moved = lax.ppermute(value, axis, pairs)
        value = jnp.where(at % (2 * gap) == gap, moved, value)
        gap //= 2
    return value


def body(state, turbine_x, turbine_y, yaw_index):
    slots, fields, ry, rz, x = state.shape
    tiles = x // LANES
    nt = turbine_x.shape[1]
    count = fields * ry * tiles * rz
    near_count = count // rz * HALO
    fringe_count = fields * (rz + 1) * ry
    dims = (fields, ry, rz, tiles)
    inner, outer = swaps(lax.axis_size("vert"))
    across = [(0, 1), (1, 0)]
    smem = pl.BlockSpec(memory_space=pltpu.SMEM)
    vmem = pl.BlockSpec(memory_space=pltpu.VMEM)
    hbm = pl.BlockSpec(memory_space=pl.ANY)
    whole = flat(state)

    def rows_of(n):
        return jax.ShapeDtypeStruct((n, LANES), jnp.float32)

    def block_of(n):
        return pltpu.VMEM((n, LANES), jnp.float32)

    small = pltpu.CompilerParams(vmem_limit_bytes=8 << 20)
    away_near, away_far = pl.pallas_call(
        functools.partial(away_kernel, dims),
        out_shape=[rows_of(near_count), rows_of(count - near_count)],
        in_specs=[vmem],
        out_specs=[vmem] * 2,
        compiler_params=small,
        name="away",
    )(whole)
    fringe = pl.pallas_call(
        functools.partial(fringe_kernel, dims),
        out_shape=rows_of(fringe_count),
        in_specs=[vmem],
        out_specs=vmem,
        compiler_params=small,
        name="fringe",
    )(whole)
    got_near = lax.ppermute(away_near, "span", across)
    got_far = lax.ppermute(away_far, "span", across)
    own, near = pl.pallas_call(
        functools.partial(own_kernel, dims),
        out_shape=[rows_of(count), rows_of(near_count)],
        in_specs=[vmem],
        out_specs=[vmem] * 2,
        compiler_params=small,
        name="own",
    )(whole)
    out_own = lax.ppermute(near, "vert", outer)
    in_own = lax.ppermute(own, "vert", inner)
    fringe = spread(fringe, "case")
    fringe_got = lax.ppermute(fringe, "span", across)
    out_got = lax.ppermute(got_near, "vert", outer)
    in_near = lax.ppermute(got_near, "vert", inner)
    in_far = lax.ppermute(got_far, "vert", inner)
    fringes = [jnp.concatenate([fringe, fringe_got])]
    for pairs in (outer, inner):
        fringes.append(lax.ppermute(fringes[0], "vert", pairs))
    ext = rz + 2 * HALO
    store = 2 * ROW0 + 2 * ry
    size = fields * (ext + 2) * store
    weights = (2, 2, tiles, 2 * ry // 8, 8, LANES)
    sides = [block_of(fields * 2 * tiles * 2 * ry)] * 2
    large = pltpu.CompilerParams(vmem_limit_bytes=20 << 20)
    trig, wgt = pl.pallas_call(
        functools.partial(weights_kernel, (ry, tiles, nt, slots)),
        out_shape=[
            jax.ShapeDtypeStruct((3, 8, LANES), jnp.float32),
            jax.ShapeDtypeStruct(weights, jnp.float32),
        ],
        in_specs=[smem] * 3,
        out_specs=[vmem, vmem],
        compiler_params=small,
        name="weights",
    )(turbine_x, turbine_y, yaw_index)
    q = pl.pallas_call(
        functools.partial(first_kernel, dims),
        out_shape=rows_of(size * tiles),
        in_specs=[vmem] * 10,
        out_specs=vmem,
        scratch_shapes=[block_of(size * tiles)] + sides,
        compiler_params=large,
        name="first",
    )(trig, wgt, own, got_near, got_far, out_own, out_got, in_own, in_near, in_far)
    mine, send, _ = pl.pallas_call(
        functools.partial(rest_kernel, dims),
        out_shape=[rows_of(count)] * 2 + [rows_of(size * tiles)],
        in_specs=[vmem] * 6,
        out_specs=[vmem] * 3,
        scratch_shapes=[block_of(size * tiles)] + [block_of(size * 2)] * 2 + sides,
        input_output_aliases={2: 2},
        compiler_params=large,
        name="rest",
    )(trig, wgt, q, *fringes)
    back = lax.ppermute(send, "span", across)

    def place(other, block, *earlier):
        return pl.pallas_call(
            functools.partial(place_kernel, dims, other),
            out_shape=rows_of(slots * count),
            in_specs=[vmem] + [hbm] * len(earlier),
            out_specs=hbm,
            scratch_shapes=[block_of(count), pltpu.SemaphoreType.DMA((fields,))],
            input_output_aliases={1: 0} if earlier else {},
            compiler_params=pltpu.CompilerParams(vmem_limit_bytes=8 << 20),
            name="place",
        )(block, *earlier)

    return unflat(place(True, back, place(False, mine)), state.shape)


def extended_2(shard, sides, width):
    for axis, dim in sides:
        size, length = (lax.axis_size(axis), shard.shape[dim])
        up = [(i, (i + 1) % size) for i in range(size)]
        down = [(j, i) for i, j in up]
        last = lax.slice_in_dim(shard, length - width, length, axis=dim)
        leading = lax.slice_in_dim(shard, 0, width, axis=dim)
        before = lax.ppermute(last, axis, up)
        after = lax.ppermute(leading, axis, down)
        shard = jnp.concatenate([before, shard, after], axis=dim)
    return shard


def entering(part, axis, combine, identity):
    place = lax.axis_index(axis)
    gathered = jax.tree.map(lambda a: lax.all_gather(a, axis), part)
    state = jax.tree.map(lambda a, e: jnp.zeros_like(a) + jnp.asarray(e, a.dtype), part, identity)

    def one(step, state):
        return combine(
            state, jax.tree.map(lambda a: lax.dynamic_index_in_dim(a, step, 0, False), gathered)
        )

    return lax.fori_loop(0, place, one, state)


def tendency(center, east, west, north, south, upper, lower, weight, cos_yaw, sin_yaw):
    grad_x = (east - west) * 0.5
    grad_y = (north - south) * 0.5
    grad_z = (upper - lower) * 0.5
    laplace = east + west + north + south + upper + lower - 6.0 * center
    vel_u = center[..., 1, :, :, :]
    vel_v = center[..., 2, :, :, :]
    vel_w = center[..., 3, :, :, :]
    dux = grad_x[..., 1, :, :, :]
    dvy = grad_y[..., 2, :, :, :]
    dwz = grad_z[..., 3, :, :, :]
    duy = grad_y[..., 1, :, :, :]
    duz = grad_z[..., 1, :, :, :]
    strain = dux * dux + dvy * dvy + dwz * dwz + duy * duy + duz * duz
    viscous = VISC * jnp.sqrt(1.0 + strain)
    speed = U_MEAN + vel_u
    flow = -(
        jnp.expand_dims(speed, -4) * grad_x
        + jnp.expand_dims(vel_v, -4) * grad_y
        + jnp.expand_dims(vel_w, -4) * grad_z
    )
    flow = flow + jnp.expand_dims(viscous, -4) * laplace
    normal = speed * cos_yaw + vel_v * sin_yaw
    thrust = THRUST * normal * jnp.abs(normal) * weight
    extra = jnp.stack(
        [
            -(dux + dvy + dwz),
            -grad_x[..., 0, :, :, :] - thrust * cos_yaw,
            -grad_y[..., 0, :, :, :] - thrust * sin_yaw,
            -grad_z[..., 0, :, :, :],
        ],
        axis=-4,
    )
    return flow + extra


def extended(fields):
    padded = extended_2(fields, (("span", 2), ("vert", 3)), 1)
    vert_at = lax.axis_index("vert")
    bottom = jnp.where(vert_at == 0, 0.0, padded[:, :, :, :1, :])
    summit = jnp.where(vert_at == lax.axis_size("vert") - 1, 0.0, padded[:, :, :, -1:, :])
    padded = jnp.concatenate([bottom, padded[:, :, :, 1:-1, :], summit], axis=3)
    return padded


def stencil(fields, padded, weight, cos_yaw, sin_yaw):
    east = jnp.roll(fields, -1, axis=4)
    west = jnp.roll(fields, 1, axis=4)
    north = padded[:, :, 2:, 1:-1, :]
    south = padded[:, :, :-2, 1:-1, :]
    upper = padded[:, :, 1:-1, 2:, :]
    lower = padded[:, :, 1:-1, :-2, :]
    return tendency(fields, east, west, north, south, upper, lower, weight, cos_yaw, sin_yaw)


def rate(fields, weight, cos_yaw, sin_yaw):
    return stencil(fields, extended(fields), weight, cos_yaw, sin_yaw)


def make_weight(turbine_x, turbine_y, along_y, along_z, total_y, total_z, active, length):
    along_x = jnp.arange(length, dtype=jnp.int32)
    hit_x = (along_x[None, None, :] == turbine_x[:, :, None]).astype(jnp.float32)
    hit_y = ((along_y[None, None, :] - turbine_y[:, :, None]) % total_y < DISK).astype(jnp.float32)
    plane = jnp.einsum("dky,dkx->dyx", hit_y, hit_x, precision=lax.Precision.HIGHEST)
    lower_half = (along_z < total_z // 2).astype(jnp.float32)
    return plane[:, :, None, :] * lower_half[None, None, :, None] * active[:, None, None, None]


def first_held(earlier, later):
    keep = earlier[1] > 0.0
    return (jnp.where(keep, earlier[0], later[0]), jnp.maximum(earlier[1], later[1]))


def body_general(state, turbine_x, turbine_y, yaw_index):
    slots = state.shape[0]
    rows_y = state.shape[2]
    rows_z = state.shape[3]
    total_y = rows_y * lax.axis_size("span")
    total_z = rows_z * lax.axis_size("vert")
    domain = lax.axis_index("case") * slots + jnp.arange(slots, dtype=jnp.int32)
    active = (domain > 0).astype(jnp.float32)
    along_y = lax.axis_index("span") * rows_y + jnp.arange(rows_y, dtype=jnp.int32)
    along_z = lax.axis_index("vert") * rows_z + jnp.arange(rows_z, dtype=jnp.int32)
    weight = make_weight(turbine_x, turbine_y, along_y, along_z, total_y, total_z, active, state.shape[4])
    angle = (yaw_index.astype(jnp.float32) - 3.5) * YAW_STEP
    cos_yaw = jnp.cos(angle)[:, None, None, None]
    sin_yaw = jnp.sin(angle)[:, None, None, None]
    width = state.shape[4] // 4
    ramp = 0.5 * (1.0 - jnp.cos(jnp.pi * (jnp.arange(width, dtype=jnp.float32) + 1.0) / width))
    case_at = lax.axis_index("case")
    for _ in range(STEPS):
        first = rate(state, weight, cos_yaw, sin_yaw)
        middle = state + TIME_STEP * first
        second = rate(middle, weight, cos_yaw, sin_yaw)
        state = state + 0.5 * TIME_STEP * (first + second)
        front = state[..., :width]
        own_fringe = front[0]
        marker = jnp.ones((), jnp.float32)
        blank = (jnp.zeros_like(own_fringe), jnp.zeros((), jnp.float32))
        passed = entering((own_fringe, marker), "case", first_held, blank)
        source = jnp.where(case_at == 0, own_fringe, passed[0])
        front = front + ramp * (source[None] - front)
        state = jnp.concatenate([front, state[..., width:]], axis=4)
    return state


def body_any(state, turbine_x, turbine_y, yaw_index):
    slots, _, ry, rz, x = state.shape
    fits = lax.axis_size("span") == 2 and slots == 2 and lax.axis_size("vert") % 2 == 0
    fits = fits and ry == 8 and rz % 8 == 0 and x == 4 * LANES
    chosen = body if fits else body_general
    return chosen(state, turbine_x, turbine_y, yaw_index)


def solution(mesh):
    return jax.shard_map(
        body_any,
        mesh=mesh,
        in_specs=(
            P("case", None, "span", "vert", None),
            P("case", None),
            P("case", None),
            P("case"),
        ),
        out_specs=P("case", None, "span", "vert", None),
        check_vma=False,
    )
```

```python
import functools

import jax
import jax.numpy as jnp
from jax import lax
from jax.experimental import pallas as pl
from jax.experimental.pallas import tpu as pltpu
from jax.sharding import PartitionSpec as P


STEPS = 3
DISK = 8
LANES = 128
HALO = 2 * STEPS

U_MEAN = 1.0
VISC = 0.04
THRUST = 0.75
TIME_STEP = 0.1
YAW_STEP = 0.15
HALF = 0.5 * TIME_STEP
SCALES = (HALF * HALF, HALF, HALF, HALF)

ROW0 = 8
STRIP = 16


def flat(blocks):
    _, z, x = blocks.shape[-3:]
    a = blocks.reshape(-1, z, x // LANES, LANES)
    return jnp.swapaxes(a, 1, 2).reshape(-1, LANES)


def unflat(rows, shape):
    _, z, x = shape[-3:]
    a = rows.reshape(-1, x // LANES, z, LANES)
    return jnp.swapaxes(a, 1, 2).reshape(shape)


def away_kernel(dims, state_ref, near_ref, far_ref):
    fields, ry, rz, tiles = dims
    part = ry * tiles * rz
    slot = 1 - lax.axis_index("span")
    even = lax.axis_index("vert") % 2 == 0
    near = jnp.where(even, 0, rz - HALO)
    far = jnp.where(even, HALO, 0)
    for f in range(fields):
        base = (slot * fields + f) * part
        for ref, low, count in ((near_ref, near, HALO), (far_ref, far, rz - HALO)):
            for t in range(tiles):
                for k in range(count):
                    value = state_ref[pl.ds(base + t * rz + low + k, ry, stride=tiles * rz), :]
                    ref[pl.ds(((f * tiles + t) * count + k) * ry, ry), :] = value


def fringe_kernel(dims, held_ref, fringe_ref):
    fields, ry, rz, tiles = dims
    step = tiles * rz
    lane = lax.broadcasted_iota(jnp.int32, (ry, LANES), 1)
    for f in range(fields):
        base = f * ry * step
        strip = jnp.zeros((ry, LANES), jnp.float32)
        for z in range(rz):
            place = f * (rz + 1) + z
            row = base + z
            fringe_ref[pl.ds(place * ry, ry), :] = held_ref[pl.ds(row, ry, stride=step), :]
            after = held_ref[pl.ds(row + rz, ry, stride=step), :]
            before = held_ref[pl.ds(row + (tiles - 1) * rz, ry, stride=step), :]
            both = jnp.where(lane < LANES // 2, after, before)
            both = pltpu.roll(both, (HALO + STRIP * z) % LANES, 1)
            here = (lane >= STRIP * z) & (lane < STRIP * z + 2 * HALO)
            strip = jnp.where(here, both, strip)
        fringe_ref[pl.ds((f * (rz + 1) + rz) * ry, ry), :] = strip


def own_kernel(dims, state_ref, own_ref, near_ref):
    fields, ry, rz, tiles = dims
    size = fields * ry * tiles * rz
    start = lax.axis_index("span") * size
    even = lax.axis_index("vert") % 2 == 0
    near = jnp.where(even, 0, rz - HALO)
    for f in range(fields):
        for t in range(tiles):
            for z in range(rz):
                row = start + (f * ry * tiles + t) * rz + z
                value = state_ref[pl.ds(row, ry, stride=tiles * rz), :]
                own_ref[pl.ds(((f * tiles + t) * rz + z) * ry, ry), :] = value
    for c in range(fields * tiles):
        for k in range(HALO):
            row = pl.multiple_of((c * rz + near + k) * ry, 8)
            near_ref[pl.ds((c * HALO + k) * ry, ry), :] = own_ref[pl.ds(row, ry), :]


def weights_kernel(dims, xs, ys, yaws, trig, wgt):
    ry, tiles, nt, slots = dims
    total_y = 2 * ry
    slot = lax.axis_index("span")
    active = jnp.where(lax.axis_index("case") * slots + slot > 0, 1.0, 0.0)
    lane = lax.broadcasted_iota(jnp.int32, (8, LANES), 1)
    sub = lax.broadcasted_iota(jnp.int32, (8, LANES), 0)
    angle = jnp.full((8, LANES), yaws[slot], jnp.int32).astype(jnp.float32)
    angle = (angle - 3.5) * YAW_STEP
    cos_yaw = jnp.cos(angle)
    sin_yaw = jnp.sin(angle)
    trig[0] = cos_yaw
    trig[1] = sin_yaw
    trig[2] = 0.5 * (1.0 - jnp.cos(jnp.pi * (lane.astype(jnp.float32) + 1.0) / LANES))
    for t in range(1, tiles):
        for g in range(total_y // 8):
            acc = jnp.zeros((8, LANES), jnp.float32)
            y = slot * ry + 8 * g + sub
            for k in range(nt):
                hit = lax.rem(y - ys[slot, k] + 2 * total_y, total_y) < DISK
                hit = hit & (lane + t * LANES == xs[slot, k])
                acc = acc + jnp.where(hit, 1.0, 0.0)
            acc = acc * (active * (2.0 * THRUST))
            wgt[0, 0, t, g] = jnp.zeros((8, LANES), jnp.float32)
            wgt[0, 1, t, g] = jnp.zeros((8, LANES), jnp.float32)
            wgt[1, 0, t, g] = acc * cos_yaw
            wgt[1, 1, t, g] = acc * sin_yaw


class Cells:

    def __init__(self, dims, trig):
        self.dims = fields, ry, rz, tiles = dims
        self.ext = rz + 2 * HALO
        self.rows = self.ext + 2
        self.total_y = 2 * ry
        self.store = 2 * ROW0 + self.total_y
        self.groups = self.total_y // 8
        total_z = rz * lax.axis_size("vert")
        self.slot = lax.axis_index("span")
        vert_at = lax.axis_index("vert")
        z0 = vert_at * rz
        self.even = vert_at % 2 == 0
        self.dlo = jnp.maximum(HALO - z0, 0)
        self.dhi = jnp.minimum(HALO + total_z - z0, self.ext)
        self.gate = HALO + total_z // 2 - z0
        self.one = 1 + jnp.minimum(vert_at, 0)
        self.lane = lax.broadcasted_iota(jnp.int32, (8, LANES), 1)
        self.first_lane = self.lane == 0
        self.last_lane = self.lane == LANES - 1
        if trig is not None:
            self.cos_yaw, self.sin_yaw, self.ramp = trig[0], trig[1], trig[2]

    def put(self, dst, width, f, t, z, group, value):
        start = pl.multiple_of(((f * width + t) * self.rows + z + 1) * self.store, 8)
        dst[pl.ds(start + (ROW0 + 8 * group), 8), :] = value
        if group == 0:
            dst[pl.ds(start + (ROW0 + self.total_y), 1), :] = value[0:1]
        if group == self.groups - 1:
            dst[pl.ds(start + (ROW0 - 1), 1), :] = value[7:8]

    def clear_outside(self, *refs):
        fields, rz = self.dims[0], self.dims[2]
        zero = jnp.zeros((self.store, LANES), jnp.float32)
        for ref, width in refs:
            for z in (HALO - 1, HALO + rz):

                def clear(ref=ref, width=width, z=z):
                    for c in range(fields * width):
                        ref[pl.ds((c * self.rows + z + 1) * self.store, self.store), :] = zero

                pl.when((z < self.dlo) | (z >= self.dhi))(clear)

    def stage(self, src, base, dst, width, k, wgt=None, pq=None, out=None, chosen=None):
        second = k % 2 == 0
        fields, ry, rz, tiles = self.dims
        rows, store, ext, groups, one = self.rows, self.store, self.ext, self.groups, self.one
        dlo, dhi, gate = self.dlo, self.dhi, self.gate
        cos_yaw, sin_yaw, ramp = self.cos_yaw, self.sin_yaw, self.ramp
        chosen = range(groups) if chosen is None else chosen
        first_lane, last_lane, sides0, sides1 = self.first_lane, self.last_lane, *self.sides

        def at(ref, f, t, g, z, dy=0):
            start = ((f * width + t % width) * rows + z + 1) * store + ROW0 + 8 * g
            start = start + dy * one if dy else pl.multiple_of(start, 8)
            return ref[pl.ds(start, 8), :]

        def beside(f, t, g, side):
            return pl.ds((((f * 2 + side) * width + t) * groups + g) * 8, 8)

        def shift(z, into, t, g):
            for f in range(fields):
                c = at(src, f, t, g, z)
                after = at(src, f, t + 1, g, z)
                before = at(src, f, t - 1, g, z)
                east = pltpu.roll(jnp.where(first_lane, after, c), LANES - 1, 1)
                west = pltpu.roll(jnp.where(last_lane, before, c), 1, 1)
                into[beside(f, t, g, 0), :] = east
                into[beside(f, t, g, 1), :] = west

        def row(z, sides, following):
            if wgt is not None:
                on = jnp.where(z < gate, 1, 0)
            for t in range(width):
                for g in chosen:
                    shift(z + 1, following, t, g)
                    c = [at(src, f, t, g, z) for f in range(fields)]
                    gx, gy, gz, lap = [], [], [], []
                    for f in range(fields):
                        east = sides[beside(f, t, g, 0), :]
                        west = sides[beside(f, t, g, 1), :]
                        north = at(src, f, t, g, z, dy=1)
                        south = at(src, f, t, g, z, dy=-1)
                        upper = at(src, f, t, g, z + 1)
                        lower = at(src, f, t, g, z - 1)
                        gx.append(east - west)
                        gy.append(north - south)
                        gz.append(upper - lower)
                        around = ((east + west) + (north + south)) + (upper + lower)
                        lap.append(around - 6.0 * c[f])
                    speed = c[1] + HALF * U_MEAN
                    strain = gx[1] * gx[1] + gy[2] * gy[2] + gz[3] * gz[3]
                    strain = strain + gy[1] * gy[1] + gz[1] * gz[1] + 4.0 * HALF * HALF
                    viscous = VISC * (strain * lax.rsqrt(strain))
                    rate = [
                        viscous * lap[f] - (speed * gx[f] + c[2] * gy[f] + c[3] * gz[f])
                        for f in range(fields)
                    ]
                    rate[0] = rate[0] - HALF * HALF * (gx[1] + gy[2] + gz[3])
                    rate[1] = rate[1] - gx[0]
                    rate[2] = rate[2] - gy[0]
                    rate[3] = rate[3] - gz[0]
                    if wgt is not None and t > 0:
                        normal = speed * cos_yaw + c[2] * sin_yaw
                        thrust = normal * jnp.abs(normal)
                        rate[1] = rate[1] - thrust * wgt[on, 0, t, g]
                        rate[2] = rate[2] - thrust * wgt[on, 1, t, g]
                    for f in range(fields):
                        if second:
                            new = 0.5 * ((at(base, f, t, g, z) + c[f]) + rate[f])
                            if pq is not None and t == 0:
                                start = pl.multiple_of((f * 2 * rows + z + 1) * store, 8)
                                new = new + ramp * (pq[pl.ds(start + (ROW0 + 8 * g), 8), :] - new)
                        else:
                            new = c[f] + rate[f]
                        if out is not None:
                            start = ((f * tiles + t) * rz + z - HALO) * ry + 8 * (g % (groups // 2))
                            new = new * (1.0 / SCALES[f])
                            out[pl.ds(pl.multiple_of(start, 8), 8), :] = new
                        else:
                            self.put(dst, width, f, t, z, g, new)

        first = jnp.maximum(k, dlo)
        count = jnp.minimum(ext - k, dhi) - first
        first = first - jnp.where(dhi < ext, count & 1, 0)
        for t in range(width):
            for g in chosen:
                shift(first, sides0, t, g)

        def pair(i, carry):
            z = first + 2 * i
            row(z, sides0, sides1)
            row(z + 1, sides1, sides0)
            return carry

        lax.fori_loop(0, (count + 1) // 2, pair, 0)


def scale_of(f):
    return jnp.where(f == 0, SCALES[0], SCALES[1])


def fill_rows(cells, q, parts):
    fields, ry, _, tiles = cells.dims

    def one_field(f, carry):
        for src, held, taken, half, z_dst, count in parts:
            for t in range(tiles):
                for k in range(count):
                    row = pl.multiple_of(((f * tiles + t) * held + taken + k) * ry, 8)
                    for g in range(ry // 8):
                        value = scale_of(f) * src[pl.ds(row + 8 * g, 8), :]
                        cells.put(q, tiles, f, t, z_dst + k, half * (ry // 8) + g, value)
        return carry

    lax.fori_loop(0, fields, one_field, 0)


def fill_kernel(dims, own, got_near, q):
    cells = Cells(dims, None)
    rz = dims[2]
    rest = rz - HALO
    near = HALO + jnp.where(cells.even, 0, rest)
    fill_rows(cells, q, ((own, rz, 0, 0, HALO, rz), (got_near, HALO, 0, 1, near, HALO)))


def first_kernel(
    dims, trig, wgt, q_in, got_far, out_own, out_got, in_own, in_near, in_far, q, m, sides0, sides1
):
    del q_in
    _, _, rz, tiles = dims
    cells = Cells(dims, trig)
    cells.sides = sides0, sides1

    def pick(a, b):
        return jnp.where(cells.even, a, b)

    above = HALO + rz
    rest = rz - HALO
    fill_rows(
        cells,
        q,
        (
            (in_own, rz, pick(0, rest), 0, pick(above, 0), HALO),
            (out_own, HALO, 0, 0, pick(0, above), HALO),
            (got_far, rest, 0, 1, HALO + pick(HALO, 0), rest),
            (out_got, HALO, 0, 1, pick(0, above), HALO),
            (in_near, HALO, pick(0, rest), 1, pick(above + rest, 0), HALO - rest),
            (in_far, rest, 0, 1, pick(above, HALO - rest), rest),
        ),
    )
    cells.clear_outside((q, tiles), (m, tiles))
    cells.stage(q, None, m, tiles, 1, wgt)
    cells.stage(m, q, q, tiles, 2, wgt)


def rest_kernel(
    dims, trig, wgt, q_in, p_own, p_out, p_in, send_ref, q, m, pq, pm, sides0, sides1
):
    del q_in
    fields, ry, rz, tiles = dims
    cells = Cells(dims, trig)
    cells.sides = sides0, sides1
    put = cells.put

    def fill_fringe(parts):
        def one_field(f, carry):
            for src, taken, half, z_dst, count in parts:
                base = (half * fields + f) * (rz + 1)
                strip = scale_of(f) * src[pl.ds(pl.multiple_of((base + rz) * ry, 8), ry), :]
                for k in range(count):
                    z = taken + k
                    row = pl.multiple_of((base + z) * ry, 8)
                    put(pq, 2, f, 0, z_dst + k, half, scale_of(f) * src[pl.ds(row, ry), :])
                    value = pltpu.roll(strip, 2 * LANES - HALO - STRIP * z, 1)
                    put(pq, 2, f, 1, z_dst + k, half, value)
            return carry

        lax.fori_loop(0, fields, one_field, 0)

    def pick(a, b):
        return jnp.where(cells.even, a, b)

    above = HALO + rz
    rest = rz - HALO
    for half in range(2):
        fill_fringe(
            (
                (p_own, 0, half, HALO, rz),
                (p_out, pick(rest, 0), half, pick(0, above), HALO),
                (p_in, pick(0, rest), half, pick(above, 0), HALO),
            )
        )
    cells.clear_outside((pq, 2), (pm, 2), (m, tiles))
    for step in range(STEPS):
        k = 2 * step + 1
        cells.stage(pq, None, pm, 2, k)
        cells.stage(pm, pq, pq, 2, k + 1)
        if step == 0:

            def relax(z, carry):
                for f in range(fields):
                    for g in range(cells.groups):
                        row = (f * tiles * cells.rows + z + 1) * cells.store + ROW0 + 8 * g
                        source = (f * 2 * cells.rows + z + 1) * cells.store + ROW0 + 8 * g
                        value = q[pl.ds(pl.multiple_of(row, 8), 8), :]
                        value = value + cells.ramp * (pq[pl.ds(pl.multiple_of(source, 8), 8), :] - value)
                        put(q, tiles, f, 0, z, g, value)
                return carry

            low = jnp.maximum(k + 1, cells.dlo)
            lax.fori_loop(low, jnp.minimum(cells.ext - k - 1, cells.dhi), relax, 0)
        else:
            cells.stage(q, None, m, tiles, k, wgt)
            if step < STEPS - 1:
                cells.stage(m, q, q, tiles, k + 1, wgt, pq)
            else:
                other_half = range(cells.groups // 2, cells.groups)
                cells.stage(m, q, None, tiles, k + 1, wgt, pq, send_ref, other_half)


def last_kernel(dims, trig, wgt, q, m, pq, mine_ref, sides0, sides1):
    cells = Cells(dims, trig)
    cells.sides = sides0, sides1
    cells.stage(m, q, None, dims[3], HALO, wgt, pq, mine_ref, range(cells.groups // 2))


def place_kernel(dims, other, *refs):
    fields, ry, rz, tiles = dims
    src, out_ref, block, sems = refs[0], refs[-3], refs[-2], refs[-1]
    size = ry * tiles * rz
    slot = lax.axis_index("span")
    slot = 1 - slot if other else slot
    copies = []
    for f in range(fields):
        for y in range(ry):
            for t in range(tiles):
                value = src[pl.ds((f * tiles + t) * rz * ry + y, rz, stride=ry), :]
                block[pl.ds(((f * ry + y) * tiles + t) * rz, rz), :] = value
        start = pl.multiple_of((slot * fields + f) * size, 8)
        part = block.at[pl.ds(f * size, size)]
        copies.append(pltpu.make_async_copy(part, out_ref.at[pl.ds(start, size)], sems.at[f]))
        copies[-1].start()
    for copy in copies:
        copy.wait()


def swaps(size):
    inner = [(i, i ^ 1) for i in range(size)]
    outer = [(i, i + 1 if i % 2 else i - 1) for i in range(size)]
    outer = [(i, j) for i, j in outer if 0 <= j < size]
    return inner, outer


def spread(value, axis):
    size = lax.axis_size(axis)
    at = lax.axis_index(axis)
    gap = size // 2
    while gap:
        pairs = [(i, i + gap) for i in range(0, size, 2 * gap)]
        moved = lax.ppermute(value, axis, pairs)
        value = jnp.where(at % (2 * gap) == gap, moved, value)
        gap //= 2
    return value


def body(state, turbine_x, turbine_y, yaw_index):
    slots, fields, ry, rz, x = state.shape
    tiles = x // LANES
    nt = turbine_x.shape[1]
    count = fields * ry * tiles * rz
    near_count = count // rz * HALO
    fringe_count = fields * (rz + 1) * ry
    dims = (fields, ry, rz, tiles)
    inner, outer = swaps(lax.axis_size("vert"))
    across = [(0, 1), (1, 0)]
    smem = pl.BlockSpec(memory_space=pltpu.SMEM)
    vmem = pl.BlockSpec(memory_space=pltpu.VMEM)
    hbm = pl.BlockSpec(memory_space=pl.ANY)
    whole = flat(state)

    def rows_of(n):
        return jax.ShapeDtypeStruct((n, LANES), jnp.float32)

    def block_of(n):
        return pltpu.VMEM((n, LANES), jnp.float32)

    small = pltpu.CompilerParams(vmem_limit_bytes=8 << 20)
    away_near, away_far = pl.pallas_call(
        functools.partial(away_kernel, dims),
        out_shape=[rows_of(near_count), rows_of(count - near_count)],
        in_specs=[vmem],
        out_specs=[vmem] * 2,
        compiler_params=small,
        name="away",
    )(whole)
    fringe = pl.pallas_call(
        functools.partial(fringe_kernel, dims),
        out_shape=rows_of(fringe_count),
        in_specs=[vmem],
        out_specs=vmem,
        compiler_params=small,
        name="fringe",
    )(whole)
    got_near = lax.ppermute(away_near, "span", across)
    got_far = lax.ppermute(away_far, "span", across)
    own, near = pl.pallas_call(
        functools.partial(own_kernel, dims),
        out_shape=[rows_of(count), rows_of(near_count)],
        in_specs=[vmem],
        out_specs=[vmem] * 2,
        compiler_params=small,
        name="own",
    )(whole)
    out_own = lax.ppermute(near, "vert", outer)
    in_own = lax.ppermute(own, "vert", inner)
    fringe = spread(fringe, "case")
    fringe_got = lax.ppermute(fringe, "span", across)
    out_got = lax.ppermute(got_near, "vert", outer)
    in_near = lax.ppermute(got_near, "vert", inner)
    in_far = lax.ppermute(got_far, "vert", inner)
    fringes = [jnp.concatenate([fringe, fringe_got])]
    for pairs in (outer, inner):
        fringes.append(lax.ppermute(fringes[0], "vert", pairs))
    ext = rz + 2 * HALO
    store = 2 * ROW0 + 2 * ry
    size = fields * (ext + 2) * store
    weights = (2, 2, tiles, 2 * ry // 8, 8, LANES)
    sides = [block_of(fields * 2 * tiles * 2 * ry)] * 2
    large = pltpu.CompilerParams(vmem_limit_bytes=20 << 20)
    trig, wgt = pl.pallas_call(
        functools.partial(weights_kernel, (ry, tiles, nt, slots)),
        out_shape=[
            jax.ShapeDtypeStruct((3, 8, LANES), jnp.float32),
            jax.ShapeDtypeStruct(weights, jnp.float32),
        ],
        in_specs=[smem] * 3,
        out_specs=[vmem, vmem],
        compiler_params=small,
        name="weights",
    )(turbine_x, turbine_y, yaw_index)
    q = pl.pallas_call(
        functools.partial(fill_kernel, dims),
        out_shape=rows_of(size * tiles),
        in_specs=[vmem] * 2,
        out_specs=vmem,
        compiler_params=small,
        name="fill",
    )(own, got_near)
    q = pl.pallas_call(
        functools.partial(first_kernel, dims),
        out_shape=rows_of(size * tiles),
        in_specs=[vmem] * 9,
        out_specs=vmem,
        scratch_shapes=[block_of(size * tiles)] + sides,
        input_output_aliases={2: 0},
        compiler_params=large,
        name="first",
    )(trig, wgt, q, got_far, out_own, out_got, in_own, in_near, in_far)
    send, q, m, pq = pl.pallas_call(
        functools.partial(rest_kernel, dims),
        out_shape=[rows_of(count)] + [rows_of(size * w) for w in (tiles, tiles, 2)],
        in_specs=[vmem] * 6,
        out_specs=[vmem] * 4,
        scratch_shapes=[block_of(size * 2)] + sides,
        input_output_aliases={2: 1},
        compiler_params=large,
        name="rest",
    )(trig, wgt, q, *fringes)
    back = lax.ppermute(send, "span", across)
    mine = pl.pallas_call(
        functools.partial(last_kernel, dims),
        out_shape=rows_of(count),
        in_specs=[vmem] * 5,
        out_specs=vmem,
        scratch_shapes=sides,
        compiler_params=large,
        name="last",
    )(trig, wgt, q, m, pq)

    def place(other, block, *earlier):
        return pl.pallas_call(
            functools.partial(place_kernel, dims, other),
            out_shape=rows_of(slots * count),
            in_specs=[vmem] + [hbm] * len(earlier),
            out_specs=hbm,
            scratch_shapes=[block_of(count), pltpu.SemaphoreType.DMA((fields,))],
            input_output_aliases={1: 0} if earlier else {},
            compiler_params=pltpu.CompilerParams(vmem_limit_bytes=8 << 20),
            name="place",
        )(block, *earlier)

    return unflat(place(True, back, place(False, mine)), state.shape)


def extended_2(shard, sides, width):
    for axis, dim in sides:
        size, length = (lax.axis_size(axis), shard.shape[dim])
        up = [(i, (i + 1) % size) for i in range(size)]
        down = [(j, i) for i, j in up]
        last = lax.slice_in_dim(shard, length - width, length, axis=dim)
        leading = lax.slice_in_dim(shard, 0, width, axis=dim)
        before = lax.ppermute(last, axis, up)
        after = lax.ppermute(leading, axis, down)
        shard = jnp.concatenate([before, shard, after], axis=dim)
    return shard


def entering(part, axis, combine, identity):
    place = lax.axis_index(axis)
    gathered = jax.tree.map(lambda a: lax.all_gather(a, axis), part)
    state = jax.tree.map(lambda a, e: jnp.zeros_like(a) + jnp.asarray(e, a.dtype), part, identity)

    def one(step, state):
        return combine(
            state, jax.tree.map(lambda a: lax.dynamic_index_in_dim(a, step, 0, False), gathered)
        )

    return lax.fori_loop(0, place, one, state)


def tendency(center, east, west, north, south, upper, lower, weight, cos_yaw, sin_yaw):
    grad_x = (east - west) * 0.5
    grad_y = (north - south) * 0.5
    grad_z = (upper - lower) * 0.5
    laplace = east + west + north + south + upper + lower - 6.0 * center
    vel_u = center[..., 1, :, :, :]
    vel_v = center[..., 2, :, :, :]
    vel_w = center[..., 3, :, :, :]
    dux = grad_x[..., 1, :, :, :]
    dvy = grad_y[..., 2, :, :, :]
    dwz = grad_z[..., 3, :, :, :]
    duy = grad_y[..., 1, :, :, :]
    duz = grad_z[..., 1, :, :, :]
    strain = dux * dux + dvy * dvy + dwz * dwz + duy * duy + duz * duz
    viscous = VISC * jnp.sqrt(1.0 + strain)
    speed = U_MEAN + vel_u
    flow = -(
        jnp.expand_dims(speed, -4) * grad_x
        + jnp.expand_dims(vel_v, -4) * grad_y
        + jnp.expand_dims(vel_w, -4) * grad_z
    )
    flow = flow + jnp.expand_dims(viscous, -4) * laplace
    normal = speed * cos_yaw + vel_v * sin_yaw
    thrust = THRUST * normal * jnp.abs(normal) * weight
    extra = jnp.stack(
        [
            -(dux + dvy + dwz),
            -grad_x[..., 0, :, :, :] - thrust * cos_yaw,
            -grad_y[..., 0, :, :, :] - thrust * sin_yaw,
            -grad_z[..., 0, :, :, :],
        ],
        axis=-4,
    )
    return flow + extra


def extended(fields):
    padded = extended_2(fields, (("span", 2), ("vert", 3)), 1)
    vert_at = lax.axis_index("vert")
    bottom = jnp.where(vert_at == 0, 0.0, padded[:, :, :, :1, :])
    summit = jnp.where(vert_at == lax.axis_size("vert") - 1, 0.0, padded[:, :, :, -1:, :])
    padded = jnp.concatenate([bottom, padded[:, :, :, 1:-1, :], summit], axis=3)
    return padded


def stencil(fields, padded, weight, cos_yaw, sin_yaw):
    east = jnp.roll(fields, -1, axis=4)
    west = jnp.roll(fields, 1, axis=4)
    north = padded[:, :, 2:, 1:-1, :]
    south = padded[:, :, :-2, 1:-1, :]
    upper = padded[:, :, 1:-1, 2:, :]
    lower = padded[:, :, 1:-1, :-2, :]
    return tendency(fields, east, west, north, south, upper, lower, weight, cos_yaw, sin_yaw)


def rate(fields, weight, cos_yaw, sin_yaw):
    return stencil(fields, extended(fields), weight, cos_yaw, sin_yaw)


def make_weight(turbine_x, turbine_y, along_y, along_z, total_y, total_z, active, length):
    along_x = jnp.arange(length, dtype=jnp.int32)
    hit_x = (along_x[None, None, :] == turbine_x[:, :, None]).astype(jnp.float32)
    hit_y = ((along_y[None, None, :] - turbine_y[:, :, None]) % total_y < DISK).astype(jnp.float32)
    plane = jnp.einsum("dky,dkx->dyx", hit_y, hit_x, precision=lax.Precision.HIGHEST)
    lower_half = (along_z < total_z // 2).astype(jnp.float32)
    return plane[:, :, None, :] * lower_half[None, None, :, None] * active[:, None, None, None]


def first_held(earlier, later):
    keep = earlier[1] > 0.0
    return (jnp.where(keep, earlier[0], later[0]), jnp.maximum(earlier[1], later[1]))


def body_general(state, turbine_x, turbine_y, yaw_index):
    slots = state.shape[0]
    rows_y = state.shape[2]
    rows_z = state.shape[3]
    total_y = rows_y * lax.axis_size("span")
    total_z = rows_z * lax.axis_size("vert")
    domain = lax.axis_index("case") * slots + jnp.arange(slots, dtype=jnp.int32)
    active = (domain > 0).astype(jnp.float32)
    along_y = lax.axis_index("span") * rows_y + jnp.arange(rows_y, dtype=jnp.int32)
    along_z = lax.axis_index("vert") * rows_z + jnp.arange(rows_z, dtype=jnp.int32)
    weight = make_weight(turbine_x, turbine_y, along_y, along_z, total_y, total_z, active, state.shape[4])
    angle = (yaw_index.astype(jnp.float32) - 3.5) * YAW_STEP
    cos_yaw = jnp.cos(angle)[:, None, None, None]
    sin_yaw = jnp.sin(angle)[:, None, None, None]
    width = state.shape[4] // 4
    ramp = 0.5 * (1.0 - jnp.cos(jnp.pi * (jnp.arange(width, dtype=jnp.float32) + 1.0) / width))
    case_at = lax.axis_index("case")
    for _ in range(STEPS):
        first = rate(state, weight, cos_yaw, sin_yaw)
        middle = state + TIME_STEP * first
        second = rate(middle, weight, cos_yaw, sin_yaw)
        state = state + 0.5 * TIME_STEP * (first + second)
        front = state[..., :width]
        own_fringe = front[0]
        marker = jnp.ones((), jnp.float32)
        blank = (jnp.zeros_like(own_fringe), jnp.zeros((), jnp.float32))
        passed = entering((own_fringe, marker), "case", first_held, blank)
        source = jnp.where(case_at == 0, own_fringe, passed[0])
        front = front + ramp * (source[None] - front)
        state = jnp.concatenate([front, state[..., width:]], axis=4)
    return state


def body_any(state, turbine_x, turbine_y, yaw_index):
    slots, _, ry, rz, x = state.shape
    fits = lax.axis_size("span") == 2 and slots == 2 and lax.axis_size("vert") % 2 == 0
    fits = fits and ry == 8 and rz % 8 == 0 and x == 4 * LANES
    chosen = body if fits else body_general
    return chosen(state, turbine_x, turbine_y, yaw_index)


def solution(mesh):
    return jax.shard_map(
        body_any,
        mesh=mesh,
        in_specs=(
            P("case", None, "span", "vert", None),
            P("case", None),
            P("case", None),
            P("case"),
        ),
        out_specs=P("case", None, "span", "vert", None),
        check_vma=False,
    )
```

```python
import functools

import jax
import jax.numpy as jnp
from jax import lax
from jax.experimental import pallas as pl
from jax.experimental.pallas import tpu as pltpu
from jax.sharding import PartitionSpec as P


STEPS = 3
DISK = 8
LANES = 128
HALO = 2 * STEPS

U_MEAN = 1.0
VISC = 0.04
THRUST = 0.75
TIME_STEP = 0.1
YAW_STEP = 0.15
HALF = 0.5 * TIME_STEP
SCALES = (HALF * HALF, HALF, HALF, HALF)

ROW0 = 8
STRIP = 16


def flat(blocks):
    _, z, x = blocks.shape[-3:]
    a = blocks.reshape(-1, z, x // LANES, LANES)
    return jnp.swapaxes(a, 1, 2).reshape(-1, LANES)


def unflat(rows, shape):
    _, z, x = shape[-3:]
    a = rows.reshape(-1, x // LANES, z, LANES)
    return jnp.swapaxes(a, 1, 2).reshape(shape)


def away_kernel(dims, state_ref, near_ref, far_ref):
    fields, ry, rz, tiles = dims
    part = ry * tiles * rz
    slot = 1 - lax.axis_index("span")
    even = lax.axis_index("vert") % 2 == 0
    near = jnp.where(even, 0, rz - HALO)
    far = jnp.where(even, HALO, 0)
    for f in range(fields):
        base = (slot * fields + f) * part
        for ref, low, count in ((near_ref, near, HALO), (far_ref, far, rz - HALO)):
            for t in range(tiles):
                for k in range(count):
                    value = state_ref[pl.ds(base + t * rz + low + k, ry, stride=tiles * rz), :]
                    ref[pl.ds(((f * tiles + t) * count + k) * ry, ry), :] = value


def fringe_kernel(dims, held_ref, fringe_ref):
    fields, ry, rz, tiles = dims
    step = tiles * rz
    lane = lax.broadcasted_iota(jnp.int32, (ry, LANES), 1)
    for f in range(fields):
        base = f * ry * step
        strip = jnp.zeros((ry, LANES), jnp.float32)
        for z in range(rz):
            place = f * (rz + 1) + z
            row = base + z
            fringe_ref[pl.ds(place * ry, ry), :] = held_ref[pl.ds(row, ry, stride=step), :]
            after = held_ref[pl.ds(row + rz, ry, stride=step), :]
            before = held_ref[pl.ds(row + (tiles - 1) * rz, ry, stride=step), :]
            both = jnp.where(lane < LANES // 2, after, before)
            both = pltpu.roll(both, (HALO + STRIP * z) % LANES, 1)
            here = (lane >= STRIP * z) & (lane < STRIP * z + 2 * HALO)
            strip = jnp.where(here, both, strip)
        fringe_ref[pl.ds((f * (rz + 1) + rz) * ry, ry), :] = strip


def own_kernel(dims, state_ref, own_ref, near_ref):
    fields, ry, rz, tiles = dims
    size = fields * ry * tiles * rz
    start = lax.axis_index("span") * size
    even = lax.axis_index("vert") % 2 == 0
    near = jnp.where(even, 0, rz - HALO)
    for f in range(fields):
        for t in range(tiles):
            for z in range(rz):
                row = start + (f * ry * tiles + t) * rz + z
                value = state_ref[pl.ds(row, ry, stride=tiles * rz), :]
                own_ref[pl.ds(((f * tiles + t) * rz + z) * ry, ry), :] = value
    for c in range(fields * tiles):
        for k in range(HALO):
            row = pl.multiple_of((c * rz + near + k) * ry, 8)
            near_ref[pl.ds((c * HALO + k) * ry, ry), :] = own_ref[pl.ds(row, ry), :]


def weights_kernel(dims, xs, ys, yaws, trig, wgt):
    ry, tiles, nt, slots = dims
    total_y = 2 * ry
    slot = lax.axis_index("span")
    active = jnp.where(lax.axis_index("case") * slots + slot > 0, 1.0, 0.0)
    lane = lax.broadcasted_iota(jnp.int32, (8, LANES), 1)
    sub = lax.broadcasted_iota(jnp.int32, (8, LANES), 0)
    angle = jnp.full((8, LANES), yaws[slot], jnp.int32).astype(jnp.float32)
    angle = (angle - 3.5) * YAW_STEP
    cos_yaw = jnp.cos(angle)
    sin_yaw = jnp.sin(angle)
    trig[0] = cos_yaw
    trig[1] = sin_yaw
    trig[2] = 0.5 * (1.0 - jnp.cos(jnp.pi * (lane.astype(jnp.float32) + 1.0) / LANES))
    for t in range(1, tiles):
        for g in range(total_y // 8):
            acc = jnp.zeros((8, LANES), jnp.float32)
            y = slot * ry + 8 * g + sub
            for k in range(nt):
                hit = lax.rem(y - ys[slot, k] + 2 * total_y, total_y) < DISK
                hit = hit & (lane + t * LANES == xs[slot, k])
                acc = acc + jnp.where(hit, 1.0, 0.0)
            acc = acc * (active * (2.0 * THRUST))
            wgt[0, 0, t, g] = jnp.zeros((8, LANES), jnp.float32)
            wgt[0, 1, t, g] = jnp.zeros((8, LANES), jnp.float32)
            wgt[1, 0, t, g] = acc * cos_yaw
            wgt[1, 1, t, g] = acc * sin_yaw


class Cells:

    def __init__(self, dims, trig):
        self.dims = fields, ry, rz, tiles = dims
        self.ext = rz + 2 * HALO
        self.rows = self.ext + 2
        self.total_y = 2 * ry
        self.store = 2 * ROW0 + self.total_y
        self.groups = self.total_y // 8
        total_z = rz * lax.axis_size("vert")
        self.slot = lax.axis_index("span")
        vert_at = lax.axis_index("vert")
        z0 = vert_at * rz
        self.even = vert_at % 2 == 0
        self.dlo = jnp.maximum(HALO - z0, 0)
        self.dhi = jnp.minimum(HALO + total_z - z0, self.ext)
        self.gate = HALO + total_z // 2 - z0
        self.one = 1 + jnp.minimum(vert_at, 0)
        self.lane = lax.broadcasted_iota(jnp.int32, (8, LANES), 1)
        self.first_lane = self.lane == 0
        self.last_lane = self.lane == LANES - 1
        if trig is not None:
            self.cos_yaw, self.sin_yaw, self.ramp = trig[0], trig[1], trig[2]

    def put(self, dst, width, f, t, z, group, value):
        start = pl.multiple_of(((f * width + t) * self.rows + z + 1) * self.store, 8)
        dst[pl.ds(start + (ROW0 + 8 * group), 8), :] = value
        if group == 0:
            dst[pl.ds(start + (ROW0 + self.total_y), 1), :] = value[0:1]
        if group == self.groups - 1:
            dst[pl.ds(start + (ROW0 - 1), 1), :] = value[7:8]

    def clear_outside(self, *refs):
        fields, rz = self.dims[0], self.dims[2]
        zero = jnp.zeros((self.store, LANES), jnp.float32)
        for ref, width in refs:
            for z in (HALO - 1, HALO + rz):

                def clear(ref=ref, width=width, z=z):
                    for c in range(fields * width):
                        ref[pl.ds((c * self.rows + z + 1) * self.store, self.store), :] = zero

                pl.when((z < self.dlo) | (z >= self.dhi))(clear)

    def stage(self, src, base, dst, width, k, wgt=None, pq=None, out=None, chosen=None, lo=0, hi=None, held=None):
        second = k % 2 == 0
        fields, ry, _, tiles = self.dims
        rows, store, ext, groups, one = self.rows, self.store, self.ext, self.groups, self.one
        dlo, dhi, gate = self.dlo, self.dhi, self.gate
        cos_yaw, sin_yaw, ramp = self.cos_yaw, self.sin_yaw, self.ramp
        chosen = range(groups) if chosen is None else chosen
        first_lane, last_lane, sides0, sides1 = self.first_lane, self.last_lane, *self.sides

        def at(ref, f, t, g, z, dy=0):
            start = ((f * width + t % width) * rows + z + 1) * store + ROW0 + 8 * g
            start = start + dy * one if dy else pl.multiple_of(start, 8)
            return ref[pl.ds(start, 8), :]

        def beside(f, t, g, side):
            return pl.ds((((f * 2 + side) * width + t) * groups + g) * 8, 8)

        def shift(z, into, t, g):
            for f in range(fields):
                c = at(src, f, t, g, z)
                after = at(src, f, t + 1, g, z)
                before = at(src, f, t - 1, g, z)
                east = pltpu.roll(jnp.where(first_lane, after, c), LANES - 1, 1)
                west = pltpu.roll(jnp.where(last_lane, before, c), 1, 1)
                into[beside(f, t, g, 0), :] = east
                into[beside(f, t, g, 1), :] = west

        def row(z, sides, following):
            if wgt is not None:
                on = jnp.where(z < gate, 1, 0)
            for t in range(width):
                for g in chosen:
                    shift(z + 1, following, t, g)
                    c = [at(src, f, t, g, z) for f in range(fields)]
                    gx, gy, gz, lap = [], [], [], []
                    for f in range(fields):
                        east = sides[beside(f, t, g, 0), :]
                        west = sides[beside(f, t, g, 1), :]
                        north = at(src, f, t, g, z, dy=1)
                        south = at(src, f, t, g, z, dy=-1)
                        upper = at(src, f, t, g, z + 1)
                        lower = at(src, f, t, g, z - 1)
                        gx.append(east - west)
                        gy.append(north - south)
                        gz.append(upper - lower)
                        around = ((east + west) + (north + south)) + (upper + lower)
                        lap.append(around - 6.0 * c[f])
                    speed = c[1] + HALF * U_MEAN
                    strain = gx[1] * gx[1] + gy[2] * gy[2] + gz[3] * gz[3]
                    strain = strain + gy[1] * gy[1] + gz[1] * gz[1] + 4.0 * HALF * HALF
                    viscous = VISC * (strain * lax.rsqrt(strain))
                    rate = [
                        viscous * lap[f] - (speed * gx[f] + c[2] * gy[f] + c[3] * gz[f])
                        for f in range(fields)
                    ]
                    rate[0] = rate[0] - HALF * HALF * (gx[1] + gy[2] + gz[3])
                    rate[1] = rate[1] - gx[0]
                    rate[2] = rate[2] - gy[0]
                    rate[3] = rate[3] - gz[0]
                    if wgt is not None and t > 0:
                        normal = speed * cos_yaw + c[2] * sin_yaw
                        thrust = normal * jnp.abs(normal)
                        rate[1] = rate[1] - thrust * wgt[on, 0, t, g]
                        rate[2] = rate[2] - thrust * wgt[on, 1, t, g]
                    for f in range(fields):
                        if second:
                            new = 0.5 * ((at(base, f, t, g, z) + c[f]) + rate[f])
                            if pq is not None and t == 0:
                                start = pl.multiple_of((f * 2 * rows + z + 1) * store, 8)
                                new = new + ramp * (pq[pl.ds(start + (ROW0 + 8 * g), 8), :] - new)
                        else:
                            new = c[f] + rate[f]
                        if out is not None:
                            start = (f * tiles + t) * held[1] + z - HALO - held[0]
                            start = start * ry + 8 * (g % (groups // 2))
                            new = new * (1.0 / SCALES[f])
                            out[pl.ds(pl.multiple_of(start, 8), 8), :] = new
                        else:
                            self.put(dst, width, f, t, z, g, new)

        first = jnp.maximum(max(k, lo), dlo)
        count = jnp.minimum(min(ext - k, ext if hi is None else hi), dhi) - first
        first = first - jnp.where(dhi < ext, count & 1, 0)
        for t in range(width):
            for g in chosen:
                shift(first, sides0, t, g)

        def pair(i, carry):
            z = first + 2 * i
            row(z, sides0, sides1)
            row(z + 1, sides1, sides0)
            return carry

        lax.fori_loop(0, (count + 1) // 2, pair, 0)


def scale_of(f):
    return jnp.where(f == 0, SCALES[0], SCALES[1])


def fill_rows(cells, q, parts):
    fields, ry, _, tiles = cells.dims

    def one_field(f, carry):
        for src, held, taken, half, z_dst, count in parts:
            for t in range(tiles):
                for k in range(count):
                    row = pl.multiple_of(((f * tiles + t) * held + taken + k) * ry, 8)
                    for g in range(ry // 8):
                        value = scale_of(f) * src[pl.ds(row + 8 * g, 8), :]
                        cells.put(q, tiles, f, t, z_dst + k, half * (ry // 8) + g, value)
        return carry

    lax.fori_loop(0, fields, one_field, 0)


def fill_kernel(dims, own, got_near, q):
    cells = Cells(dims, None)
    rz = dims[2]
    rest = rz - HALO
    near = HALO + jnp.where(cells.even, 0, rest)
    fill_rows(cells, q, ((own, rz, 0, 0, HALO, rz), (got_near, HALO, 0, 1, near, HALO)))


def early_kernel(dims, trig, wgt, q_in, got_far, q, m, sides0, sides1):
    del q_in
    rz, tiles = dims[2:]
    rest = rz - HALO
    cells = Cells(dims, trig)
    cells.sides = sides0, sides1
    fill_rows(cells, q, ((got_far, rest, 0, 1, HALO + jnp.where(cells.even, HALO, 0), rest),))
    cells.stage(q, None, m, tiles, 1, wgt, lo=HALO + 1, hi=HALO + rz - 1)


def first_kernel(
    dims, trig, wgt, q_in, m_in, out_own, out_got, in_own, in_near, in_far, q, m, sides0, sides1
):
    del q_in, m_in
    _, _, rz, tiles = dims
    cells = Cells(dims, trig)
    cells.sides = sides0, sides1

    def pick(a, b):
        return jnp.where(cells.even, a, b)

    above = HALO + rz
    rest = rz - HALO
    fill_rows(
        cells,
        q,
        (
            (in_own, rz, pick(0, rest), 0, pick(above, 0), HALO),
            (out_own, HALO, 0, 0, pick(0, above), HALO),
            (out_got, HALO, 0, 1, pick(0, above), HALO),
            (in_near, HALO, pick(0, rest), 1, pick(above + rest, 0), HALO - rest),
            (in_far, rest, 0, 1, pick(above, HALO - rest), rest),
        ),
    )
    cells.clear_outside((q, tiles), (m, tiles))
    cells.stage(q, None, m, tiles, 1, wgt, hi=HALO + 1)
    cells.stage(q, None, m, tiles, 1, wgt, lo=HALO + rz - 1)
    cells.stage(m, q, q, tiles, 2, wgt)


def rest_kernel(
    dims, trig, wgt, q_in, p_own, p_out, p_in, send_ref, q, m, pq, pm, sides0, sides1
):
    del q_in
    fields, ry, rz, tiles = dims
    cells = Cells(dims, trig)
    cells.sides = sides0, sides1
    put = cells.put

    def fill_fringe(parts):
        def one_field(f, carry):
            for src, taken, half, z_dst, count in parts:
                base = (half * fields + f) * (rz + 1)
                strip = scale_of(f) * src[pl.ds(pl.multiple_of((base + rz) * ry, 8), ry), :]
                for k in range(count):
                    z = taken + k
                    row = pl.multiple_of((base + z) * ry, 8)
                    put(pq, 2, f, 0, z_dst + k, half, scale_of(f) * src[pl.ds(row, ry), :])
                    value = pltpu.roll(strip, 2 * LANES - HALO - STRIP * z, 1)
                    put(pq, 2, f, 1, z_dst + k, half, value)
            return carry

        lax.fori_loop(0, fields, one_field, 0)

    def pick(a, b):
        return jnp.where(cells.even, a, b)

    above = HALO + rz
    rest = rz - HALO
    for half in range(2):
        fill_fringe(
            (
                (p_own, 0, half, HALO, rz),
                (p_out, pick(rest, 0), half, pick(0, above), HALO),
                (p_in, pick(0, rest), half, pick(above, 0), HALO),
            )
        )
    cells.clear_outside((pq, 2), (pm, 2), (m, tiles))
    for step in range(STEPS):
        k = 2 * step + 1
        cells.stage(pq, None, pm, 2, k)
        cells.stage(pm, pq, pq, 2, k + 1)
        if step == 0:

            def relax(z, carry):
                for f in range(fields):
                    for g in range(cells.groups):
                        row = (f * tiles * cells.rows + z + 1) * cells.store + ROW0 + 8 * g
                        source = (f * 2 * cells.rows + z + 1) * cells.store + ROW0 + 8 * g
                        value = q[pl.ds(pl.multiple_of(row, 8), 8), :]
                        value = value + cells.ramp * (pq[pl.ds(pl.multiple_of(source, 8), 8), :] - value)
                        put(q, tiles, f, 0, z, g, value)
                return carry

            low = jnp.maximum(k + 1, cells.dlo)
            lax.fori_loop(low, jnp.minimum(cells.ext - k - 1, cells.dhi), relax, 0)
        else:
            if step < STEPS - 1:
                cells.stage(q, None, m, tiles, k, wgt)
                cells.stage(m, q, q, tiles, k + 1, wgt, pq)
            else:
                middle = HALO + rz // 2
                other_half = range(cells.groups // 2, cells.groups)
                cells.stage(q, None, m, tiles, k, wgt, hi=middle + 1)
                lower = dict(hi=middle, held=(0, rz // 2))
                cells.stage(m, q, None, tiles, k + 1, wgt, pq, send_ref, other_half, **lower)


def upper_kernel(dims, trig, wgt, q, m_in, pq, send_ref, m, sides0, sides1):
    del m_in
    rz, tiles = dims[2:]
    cells = Cells(dims, trig)
    cells.sides = sides0, sides1
    middle = HALO + rz // 2
    other_half = range(cells.groups // 2, cells.groups)
    cells.stage(q, None, m, tiles, HALO - 1, wgt, lo=middle + 1)
    upper = dict(lo=middle, held=(rz // 2, rz // 2))
    cells.stage(m, q, None, tiles, HALO, wgt, pq, send_ref, other_half, **upper)


def last_kernel(dims, trig, wgt, q, m, pq, mine_ref, sides0, sides1):
    cells = Cells(dims, trig)
    cells.sides = sides0, sides1
    own_half = range(cells.groups // 2)
    cells.stage(m, q, None, dims[3], HALO, wgt, pq, mine_ref, own_half, held=(0, dims[2]))


def place_kernel(dims, other, parts, *refs):
    fields, ry, rz, tiles = dims
    out_ref, block, sems = refs[-3:]
    size = ry * tiles * rz
    count = rz // parts
    slot = lax.axis_index("span")
    slot = 1 - slot if other else slot
    copies = []
    for f in range(fields):
        for y in range(ry):
            for t in range(tiles):
                for i in range(parts):
                    source = (f * tiles + t) * count * ry + y
                    value = refs[i][pl.ds(source, count, stride=ry), :]
                    block[pl.ds(((f * ry + y) * tiles + t) * rz + i * count, count), :] = value
        start = pl.multiple_of((slot * fields + f) * size, 8)
        part = block.at[pl.ds(f * size, size)]
        copies.append(pltpu.make_async_copy(part, out_ref.at[pl.ds(start, size)], sems.at[f]))
        copies[-1].start()
    for copy in copies:
        copy.wait()


def swaps(size):
    inner = [(i, i ^ 1) for i in range(size)]
    outer = [(i, i + 1 if i % 2 else i - 1) for i in range(size)]
    outer = [(i, j) for i, j in outer if 0 <= j < size]
    return inner, outer


def spread(value, axis):
    size = lax.axis_size(axis)
    at = lax.axis_index(axis)
    gap = size // 2
    while gap:
        pairs = [(i, i + gap) for i in range(0, size, 2 * gap)]
        moved = lax.ppermute(value, axis, pairs)
        value = jnp.where(at % (2 * gap) == gap, moved, value)
        gap //= 2
    return value


def body(state, turbine_x, turbine_y, yaw_index):
    slots, fields, ry, rz, x = state.shape
    tiles = x // LANES
    nt = turbine_x.shape[1]
    count = fields * ry * tiles * rz
    near_count = count // rz * HALO
    fringe_count = fields * (rz + 1) * ry
    dims = (fields, ry, rz, tiles)
    inner, outer = swaps(lax.axis_size("vert"))
    across = [(0, 1), (1, 0)]
    smem = pl.BlockSpec(memory_space=pltpu.SMEM)
    vmem = pl.BlockSpec(memory_space=pltpu.VMEM)
    hbm = pl.BlockSpec(memory_space=pl.ANY)
    whole = flat(state)

    def rows_of(n):
        return jax.ShapeDtypeStruct((n, LANES), jnp.float32)

    def block_of(n):
        return pltpu.VMEM((n, LANES), jnp.float32)

    small = pltpu.CompilerParams(vmem_limit_bytes=8 << 20)
    away_near, away_far = pl.pallas_call(
        functools.partial(away_kernel, dims),
        out_shape=[rows_of(near_count), rows_of(count - near_count)],
        in_specs=[vmem],
        out_specs=[vmem] * 2,
        compiler_params=small,
        name="away",
    )(whole)
    fringe = pl.pallas_call(
        functools.partial(fringe_kernel, dims),
        out_shape=rows_of(fringe_count),
        in_specs=[vmem],
        out_specs=vmem,
        compiler_params=small,
        name="fringe",
    )(whole)
    got_near = lax.ppermute(away_near, "span", across)
    got_far = lax.ppermute(away_far, "span", across)
    own, near = pl.pallas_call(
        functools.partial(own_kernel, dims),
        out_shape=[rows_of(count), rows_of(near_count)],
        in_specs=[vmem],
        out_specs=[vmem] * 2,
        compiler_params=small,
        name="own",
    )(whole)
    out_own = lax.ppermute(near, "vert", outer)
    in_own = lax.ppermute(own, "vert", inner)
    fringe = spread(fringe, "case")
    fringe_got = lax.ppermute(fringe, "span", across)
    out_got = lax.ppermute(got_near, "vert", outer)
    in_near = lax.ppermute(got_near, "vert", inner)
    in_far = lax.ppermute(got_far, "vert", inner)
    fringes = [jnp.concatenate([fringe, fringe_got])]
    for pairs in (outer, inner):
        fringes.append(lax.ppermute(fringes[0], "vert", pairs))
    ext = rz + 2 * HALO
    store = 2 * ROW0 + 2 * ry
    size = fields * (ext + 2) * store
    weights = (2, 2, tiles, 2 * ry // 8, 8, LANES)
    sides = [block_of(fields * 2 * tiles * 2 * ry)] * 2
    large = pltpu.CompilerParams(vmem_limit_bytes=20 << 20)
    trig, wgt = pl.pallas_call(
        functools.partial(weights_kernel, (ry, tiles, nt, slots)),
        out_shape=[
            jax.ShapeDtypeStruct((3, 8, LANES), jnp.float32),
            jax.ShapeDtypeStruct(weights, jnp.float32),
        ],
        in_specs=[smem] * 3,
        out_specs=[vmem, vmem],
        compiler_params=small,
        name="weights",
    )(turbine_x, turbine_y, yaw_index)
    q = pl.pallas_call(
        functools.partial(fill_kernel, dims),
        out_shape=rows_of(size * tiles),
        in_specs=[vmem] * 2,
        out_specs=vmem,
        compiler_params=small,
        name="fill",
    )(own, got_near)
    q, m = pl.pallas_call(
        functools.partial(early_kernel, dims),
        out_shape=[rows_of(size * tiles)] * 2,
        in_specs=[vmem] * 4,
        out_specs=[vmem] * 2,
        scratch_shapes=sides,
        input_output_aliases={2: 0},
        compiler_params=large,
        name="early",
    )(trig, wgt, q, got_far)
    q, m = pl.pallas_call(
        functools.partial(first_kernel, dims),
        out_shape=[rows_of(size * tiles)] * 2,
        in_specs=[vmem] * 9,
        out_specs=[vmem] * 2,
        scratch_shapes=sides,
        input_output_aliases={2: 0, 3: 1},
        compiler_params=large,
        name="first",
    )(trig, wgt, q, m, out_own, out_got, in_own, in_near, in_far)
    half_rows = rows_of(count // 2)
    send_low, q, m, pq = pl.pallas_call(
        functools.partial(rest_kernel, dims),
        out_shape=[half_rows] + [rows_of(size * w) for w in (tiles, tiles, 2)],
        in_specs=[vmem] * 6,
        out_specs=[vmem] * 4,
        scratch_shapes=[block_of(size * 2)] + sides,
        input_output_aliases={2: 1},
        compiler_params=large,
        name="rest",
    )(trig, wgt, q, *fringes)
    back_low = lax.ppermute(send_low, "span", across)
    send_high, m = pl.pallas_call(
        functools.partial(upper_kernel, dims),
        out_shape=[half_rows, rows_of(size * tiles)],
        in_specs=[vmem] * 5,
        out_specs=[vmem] * 2,
        scratch_shapes=sides,
        input_output_aliases={3: 1},
        compiler_params=large,
        name="upper",
    )(trig, wgt, q, m, pq)
    back_high = lax.ppermute(send_high, "span", across)
    mine = pl.pallas_call(
        functools.partial(last_kernel, dims),
        out_shape=rows_of(count),
        in_specs=[vmem] * 5,
        out_specs=vmem,
        scratch_shapes=sides,
        compiler_params=large,
        name="last",
    )(trig, wgt, q, m, pq)

    def place(other, blocks, *earlier):
        parts = len(blocks)
        return pl.pallas_call(
            functools.partial(place_kernel, dims, other, parts),
            out_shape=rows_of(slots * count),
            in_specs=[vmem] * parts + [hbm] * len(earlier),
            out_specs=hbm,
            scratch_shapes=[block_of(count), pltpu.SemaphoreType.DMA((fields,))],
            input_output_aliases={parts: 0} if earlier else {},
            compiler_params=small,
            name="place",
        )(*blocks, *earlier)

    return unflat(place(True, (back_low, back_high), place(False, (mine,))), state.shape)


def extended_2(shard, sides, width):
    for axis, dim in sides:
        size, length = (lax.axis_size(axis), shard.shape[dim])
        up = [(i, (i + 1) % size) for i in range(size)]
        down = [(j, i) for i, j in up]
        last = lax.slice_in_dim(shard, length - width, length, axis=dim)
        leading = lax.slice_in_dim(shard, 0, width, axis=dim)
        before = lax.ppermute(last, axis, up)
        after = lax.ppermute(leading, axis, down)
        shard = jnp.concatenate([before, shard, after], axis=dim)
    return shard


def entering(part, axis, combine, identity):
    place = lax.axis_index(axis)
    gathered = jax.tree.map(lambda a: lax.all_gather(a, axis), part)
    state = jax.tree.map(lambda a, e: jnp.zeros_like(a) + jnp.asarray(e, a.dtype), part, identity)

    def one(step, state):
        return combine(
            state, jax.tree.map(lambda a: lax.dynamic_index_in_dim(a, step, 0, False), gathered)
        )

    return lax.fori_loop(0, place, one, state)


def tendency(center, east, west, north, south, upper, lower, weight, cos_yaw, sin_yaw):
    grad_x = (east - west) * 0.5
    grad_y = (north - south) * 0.5
    grad_z = (upper - lower) * 0.5
    laplace = east + west + north + south + upper + lower - 6.0 * center
    vel_u = center[..., 1, :, :, :]
    vel_v = center[..., 2, :, :, :]
    vel_w = center[..., 3, :, :, :]
    dux = grad_x[..., 1, :, :, :]
    dvy = grad_y[..., 2, :, :, :]
    dwz = grad_z[..., 3, :, :, :]
    duy = grad_y[..., 1, :, :, :]
    duz = grad_z[..., 1, :, :, :]
    strain = dux * dux + dvy * dvy + dwz * dwz + duy * duy + duz * duz
    viscous = VISC * jnp.sqrt(1.0 + strain)
    speed = U_MEAN + vel_u
    flow = -(
        jnp.expand_dims(speed, -4) * grad_x
        + jnp.expand_dims(vel_v, -4) * grad_y
        + jnp.expand_dims(vel_w, -4) * grad_z
    )
    flow = flow + jnp.expand_dims(viscous, -4) * laplace
    normal = speed * cos_yaw + vel_v * sin_yaw
    thrust = THRUST * normal * jnp.abs(normal) * weight
    extra = jnp.stack(
        [
            -(dux + dvy + dwz),
            -grad_x[..., 0, :, :, :] - thrust * cos_yaw,
            -grad_y[..., 0, :, :, :] - thrust * sin_yaw,
            -grad_z[..., 0, :, :, :],
        ],
        axis=-4,
    )
    return flow + extra


def extended(fields):
    padded = extended_2(fields, (("span", 2), ("vert", 3)), 1)
    vert_at = lax.axis_index("vert")
    bottom = jnp.where(vert_at == 0, 0.0, padded[:, :, :, :1, :])
    summit = jnp.where(vert_at == lax.axis_size("vert") - 1, 0.0, padded[:, :, :, -1:, :])
    padded = jnp.concatenate([bottom, padded[:, :, :, 1:-1, :], summit], axis=3)
    return padded


def stencil(fields, padded, weight, cos_yaw, sin_yaw):
    east = jnp.roll(fields, -1, axis=4)
    west = jnp.roll(fields, 1, axis=4)
    north = padded[:, :, 2:, 1:-1, :]
    south = padded[:, :, :-2, 1:-1, :]
    upper = padded[:, :, 1:-1, 2:, :]
    lower = padded[:, :, 1:-1, :-2, :]
    return tendency(fields, east, west, north, south, upper, lower, weight, cos_yaw, sin_yaw)


def rate(fields, weight, cos_yaw, sin_yaw):
    return stencil(fields, extended(fields), weight, cos_yaw, sin_yaw)


def make_weight(turbine_x, turbine_y, along_y, along_z, total_y, total_z, active, length):
    along_x = jnp.arange(length, dtype=jnp.int32)
    hit_x = (along_x[None, None, :] == turbine_x[:, :, None]).astype(jnp.float32)
    hit_y = ((along_y[None, None, :] - turbine_y[:, :, None]) % total_y < DISK).astype(jnp.float32)
    plane = jnp.einsum("dky,dkx->dyx", hit_y, hit_x, precision=lax.Precision.HIGHEST)
    lower_half = (along_z < total_z // 2).astype(jnp.float32)
    return plane[:, :, None, :] * lower_half[None, None, :, None] * active[:, None, None, None]


def first_held(earlier, later):
    keep = earlier[1] > 0.0
    return (jnp.where(keep, earlier[0], later[0]), jnp.maximum(earlier[1], later[1]))


def body_general(state, turbine_x, turbine_y, yaw_index):
    slots = state.shape[0]
    rows_y = state.shape[2]
    rows_z = state.shape[3]
    total_y = rows_y * lax.axis_size("span")
    total_z = rows_z * lax.axis_size("vert")
    domain = lax.axis_index("case") * slots + jnp.arange(slots, dtype=jnp.int32)
    active = (domain > 0).astype(jnp.float32)
    along_y = lax.axis_index("span") * rows_y + jnp.arange(rows_y, dtype=jnp.int32)
    along_z = lax.axis_index("vert") * rows_z + jnp.arange(rows_z, dtype=jnp.int32)
    weight = make_weight(turbine_x, turbine_y, along_y, along_z, total_y, total_z, active, state.shape[4])
    angle = (yaw_index.astype(jnp.float32) - 3.5) * YAW_STEP
    cos_yaw = jnp.cos(angle)[:, None, None, None]
    sin_yaw = jnp.sin(angle)[:, None, None, None]
    width = state.shape[4] // 4
    ramp = 0.5 * (1.0 - jnp.cos(jnp.pi * (jnp.arange(width, dtype=jnp.float32) + 1.0) / width))
    case_at = lax.axis_index("case")
    for _ in range(STEPS):
        first = rate(state, weight, cos_yaw, sin_yaw)
        middle = state + TIME_STEP * first
        second = rate(middle, weight, cos_yaw, sin_yaw)
        state = state + 0.5 * TIME_STEP * (first + second)
        front = state[..., :width]
        own_fringe = front[0]
        marker = jnp.ones((), jnp.float32)
        blank = (jnp.zeros_like(own_fringe), jnp.zeros((), jnp.float32))
        passed = entering((own_fringe, marker), "case", first_held, blank)
        source = jnp.where(case_at == 0, own_fringe, passed[0])
        front = front + ramp * (source[None] - front)
        state = jnp.concatenate([front, state[..., width:]], axis=4)
    return state


def body_any(state, turbine_x, turbine_y, yaw_index):
    slots, _, ry, rz, x = state.shape
    fits = lax.axis_size("span") == 2 and slots == 2 and lax.axis_size("vert") % 2 == 0
    fits = fits and ry == 8 and rz % 8 == 0 and x == 4 * LANES
    chosen = body if fits else body_general
    return chosen(state, turbine_x, turbine_y, yaw_index)


def solution(mesh):
    return jax.shard_map(
        body_any,
        mesh=mesh,
        in_specs=(
            P("case", None, "span", "vert", None),
            P("case", None),
            P("case", None),
            P("case"),
        ),
        out_specs=P("case", None, "span", "vert", None),
        check_vma=False,
    )
```

```python
import functools

import jax
import jax.numpy as jnp
from jax import lax
from jax.experimental import pallas as pl
from jax.experimental.pallas import tpu as pltpu
from jax.sharding import PartitionSpec as P


STEPS = 3
DISK = 8
LANES = 128
HALO = 2 * STEPS

U_MEAN = 1.0
VISC = 0.04
THRUST = 0.75
TIME_STEP = 0.1
YAW_STEP = 0.15
HALF = 0.5 * TIME_STEP
SCALES = (HALF * HALF, HALF, HALF, HALF)

ROW0 = 8
STRIP = 16


def flat(blocks):
    _, z, x = blocks.shape[-3:]
    a = blocks.reshape(-1, z, x // LANES, LANES)
    return jnp.swapaxes(a, 1, 2).reshape(-1, LANES)


def unflat(rows, shape):
    _, z, x = shape[-3:]
    a = rows.reshape(-1, x // LANES, z, LANES)
    return jnp.swapaxes(a, 1, 2).reshape(shape)


def away_kernel(dims, state_ref, near_ref, far_ref):
    fields, ry, rz, tiles = dims
    part = ry * tiles * rz
    slot = 1 - lax.axis_index("span")
    even = lax.axis_index("vert") % 2 == 0
    near = jnp.where(even, 0, rz - HALO)
    far = jnp.where(even, HALO, 0)
    for f in range(fields):
        base = (slot * fields + f) * part
        for ref, low, count in ((near_ref, near, HALO), (far_ref, far, rz - HALO)):
            for t in range(tiles):
                for k in range(count):
                    value = state_ref[pl.ds(base + t * rz + low + k, ry, stride=tiles * rz), :]
                    ref[pl.ds(((f * tiles + t) * count + k) * ry, ry), :] = value


def fringe_kernel(dims, held_ref, fringe_ref):
    fields, ry, rz, tiles = dims
    step = tiles * rz
    lane = lax.broadcasted_iota(jnp.int32, (ry, LANES), 1)
    for f in range(fields):
        base = f * ry * step
        strip = jnp.zeros((ry, LANES), jnp.float32)
        for z in range(rz):
            place = f * (rz + 1) + z
            row = base + z
            fringe_ref[pl.ds(place * ry, ry), :] = held_ref[pl.ds(row, ry, stride=step), :]
            after = held_ref[pl.ds(row + rz, ry, stride=step), :]
            before = held_ref[pl.ds(row + (tiles - 1) * rz, ry, stride=step), :]
            both = jnp.where(lane < LANES // 2, after, before)
            both = pltpu.roll(both, (HALO + STRIP * z) % LANES, 1)
            here = (lane >= STRIP * z) & (lane < STRIP * z + 2 * HALO)
            strip = jnp.where(here, both, strip)
        fringe_ref[pl.ds((f * (rz + 1) + rz) * ry, ry), :] = strip


def own_kernel(dims, state_ref, own_ref, near_ref):
    fields, ry, rz, tiles = dims
    size = fields * ry * tiles * rz
    start = lax.axis_index("span") * size
    even = lax.axis_index("vert") % 2 == 0
    near = jnp.where(even, 0, rz - HALO)
    for f in range(fields):
        for t in range(tiles):
            for z in range(rz):
                row = start + (f * ry * tiles + t) * rz + z
                value = state_ref[pl.ds(row, ry, stride=tiles * rz), :]
                own_ref[pl.ds(((f * tiles + t) * rz + z) * ry, ry), :] = value
    for c in range(fields * tiles):
        for k in range(HALO):
            row = pl.multiple_of((c * rz + near + k) * ry, 8)
            near_ref[pl.ds((c * HALO + k) * ry, ry), :] = own_ref[pl.ds(row, ry), :]


def weights_kernel(dims, xs, ys, yaws, trig, wgt):
    ry, tiles, nt, slots = dims
    total_y = 2 * ry
    slot = lax.axis_index("span")
    active = jnp.where(lax.axis_index("case") * slots + slot > 0, 1.0, 0.0)
    lane = lax.broadcasted_iota(jnp.int32, (8, LANES), 1)
    sub = lax.broadcasted_iota(jnp.int32, (8, LANES), 0)
    angle = jnp.full((8, LANES), yaws[slot], jnp.int32).astype(jnp.float32)
    angle = (angle - 3.5) * YAW_STEP
    cos_yaw = jnp.cos(angle)
    sin_yaw = jnp.sin(angle)
    trig[0] = cos_yaw
    trig[1] = sin_yaw
    trig[2] = 0.5 * (1.0 - jnp.cos(jnp.pi * (lane.astype(jnp.float32) + 1.0) / LANES))
    for t in range(1, tiles):
        for g in range(total_y // 8):
            acc = jnp.zeros((8, LANES), jnp.float32)
            y = slot * ry + 8 * g + sub
            for k in range(nt):
                hit = lax.rem(y - ys[slot, k] + 2 * total_y, total_y) < DISK
                hit = hit & (lane + t * LANES == xs[slot, k])
                acc = acc + jnp.where(hit, 1.0, 0.0)
            acc = acc * (active * (2.0 * THRUST))
            wgt[0, 0, t, g] = jnp.zeros((8, LANES), jnp.float32)
            wgt[0, 1, t, g] = jnp.zeros((8, LANES), jnp.float32)
            wgt[1, 0, t, g] = acc * cos_yaw
            wgt[1, 1, t, g] = acc * sin_yaw


class Cells:

    def __init__(self, dims, trig):
        self.dims = fields, ry, rz, tiles = dims
        self.ext = rz + 2 * HALO
        self.rows = self.ext + 2
        self.total_y = 2 * ry
        self.store = 2 * ROW0 + self.total_y
        self.groups = self.total_y // 8
        total_z = rz * lax.axis_size("vert")
        self.slot = lax.axis_index("span")
        vert_at = lax.axis_index("vert")
        z0 = vert_at * rz
        self.even = vert_at % 2 == 0
        self.dlo = jnp.maximum(HALO - z0, 0)
        self.dhi = jnp.minimum(HALO + total_z - z0, self.ext)
        self.gate = HALO + total_z // 2 - z0
        self.one = 1 + jnp.minimum(vert_at, 0)
        self.lane = lax.broadcasted_iota(jnp.int32, (8, LANES), 1)
        self.first_lane = self.lane == 0
        self.last_lane = self.lane == LANES - 1
        if trig is not None:
            self.cos_yaw, self.sin_yaw, self.ramp = trig[0], trig[1], trig[2]

    def put(self, dst, width, f, t, z, group, value):
        start = pl.multiple_of(((f * width + t) * self.rows + z + 1) * self.store, 8)
        dst[pl.ds(start + (ROW0 + 8 * group), 8), :] = value
        if group == 0:
            dst[pl.ds(start + (ROW0 + self.total_y), 1), :] = value[0:1]
        if group == self.groups - 1:
            dst[pl.ds(start + (ROW0 - 1), 1), :] = value[7:8]

    def clear_outside(self, *refs):
        fields, rz = self.dims[0], self.dims[2]
        zero = jnp.zeros((self.store, LANES), jnp.float32)
        for ref, width in refs:
            for z in (HALO - 1, HALO + rz):

                def clear(ref=ref, width=width, z=z):
                    for c in range(fields * width):
                        ref[pl.ds((c * self.rows + z + 1) * self.store, self.store), :] = zero

                pl.when((z < self.dlo) | (z >= self.dhi))(clear)

    def stage(self, src, base, dst, width, k, wgt=None, pq=None, out=None, chosen=None, lo=0, hi=None, held=None):
        second = k % 2 == 0
        fields, ry, _, tiles = self.dims
        rows, store, ext, groups, one = self.rows, self.store, self.ext, self.groups, self.one
        dlo, dhi, gate = self.dlo, self.dhi, self.gate
        cos_yaw, sin_yaw, ramp = self.cos_yaw, self.sin_yaw, self.ramp
        chosen = range(groups) if chosen is None else chosen
        first_lane, last_lane, sides0, sides1 = self.first_lane, self.last_lane, *self.sides

        def at(ref, f, t, g, z, dy=0):
            start = ((f * width + t % width) * rows + z + 1) * store + ROW0 + 8 * g
            start = start + dy * one if dy else pl.multiple_of(start, 8)
            return ref[pl.ds(start, 8), :]

        def beside(f, t, g, side):
            return pl.ds((((f * 2 + side) * width + t) * groups + g) * 8, 8)

        def shift(z, into, t, g):
            for f in range(fields):
                c = at(src, f, t, g, z)
                after = at(src, f, t + 1, g, z)
                before = at(src, f, t - 1, g, z)
                east = pltpu.roll(jnp.where(first_lane, after, c), LANES - 1, 1)
                west = pltpu.roll(jnp.where(last_lane, before, c), 1, 1)
                into[beside(f, t, g, 0), :] = east
                into[beside(f, t, g, 1), :] = west

        def row(z, sides, following):
            if wgt is not None:
                on = jnp.where(z < gate, 1, 0)
            for t in range(width):
                for g in chosen:
                    shift(z + 1, following, t, g)
                    c = [at(src, f, t, g, z) for f in range(fields)]
                    gx, gy, gz, lap = [], [], [], []
                    for f in range(fields):
                        east = sides[beside(f, t, g, 0), :]
                        west = sides[beside(f, t, g, 1), :]
                        north = at(src, f, t, g, z, dy=1)
                        south = at(src, f, t, g, z, dy=-1)
                        upper = at(src, f, t, g, z + 1)
                        lower = at(src, f, t, g, z - 1)
                        gx.append(east - west)
                        gy.append(north - south)
                        gz.append(upper - lower)
                        around = ((east + west) + (north + south)) + (upper + lower)
                        lap.append(around - 6.0 * c[f])
                    speed = c[1] + HALF * U_MEAN
                    strain = gx[1] * gx[1] + gy[2] * gy[2] + gz[3] * gz[3]
                    strain = strain + gy[1] * gy[1] + gz[1] * gz[1] + 4.0 * HALF * HALF
                    viscous = VISC * (strain * lax.rsqrt(strain))
                    rate = [
                        viscous * lap[f] - (speed * gx[f] + c[2] * gy[f] + c[3] * gz[f])
                        for f in range(fields)
                    ]
                    rate[0] = rate[0] - HALF * HALF * (gx[1] + gy[2] + gz[3])
                    rate[1] = rate[1] - gx[0]
                    rate[2] = rate[2] - gy[0]
                    rate[3] = rate[3] - gz[0]
                    if wgt is not None and t > 0:
                        normal = speed * cos_yaw + c[2] * sin_yaw
                        thrust = normal * jnp.abs(normal)
                        rate[1] = rate[1] - thrust * wgt[on, 0, t, g]
                        rate[2] = rate[2] - thrust * wgt[on, 1, t, g]
                    for f in range(fields):
                        if second:
                            new = 0.5 * ((at(base, f, t, g, z) + c[f]) + rate[f])
                            if pq is not None and t == 0:
                                start = pl.multiple_of((f * 2 * rows + z + 1) * store, 8)
                                new = new + ramp * (pq[pl.ds(start + (ROW0 + 8 * g), 8), :] - new)
                        else:
                            new = c[f] + rate[f]
                        if out is not None:
                            start = (f * tiles + t) * held[1] + z - HALO - held[0]
                            start = start * ry + 8 * (g % (groups // 2))
                            new = new * (1.0 / SCALES[f])
                            out[pl.ds(pl.multiple_of(start, 8), 8), :] = new
                        else:
                            self.put(dst, width, f, t, z, g, new)

        first = jnp.maximum(jnp.maximum(k, lo), dlo)
        count = jnp.minimum(jnp.minimum(ext - k, ext if hi is None else hi), dhi) - first
        first = first - jnp.where(dhi < ext, count & 1, 0)
        for t in range(width):
            for g in chosen:
                shift(first, sides0, t, g)

        def pair(i, carry):
            z = first + 2 * i
            row(z, sides0, sides1)
            row(z + 1, sides1, sides0)
            return carry

        lax.fori_loop(0, (count + 1) // 2, pair, 0)


def scale_of(f):
    return jnp.where(f == 0, SCALES[0], SCALES[1])


def fill_rows(cells, q, parts):
    fields, ry, _, tiles = cells.dims

    def one_field(f, carry):
        for src, held, taken, half, z_dst, count in parts:
            for t in range(tiles):
                for k in range(count):
                    row = pl.multiple_of(((f * tiles + t) * held + taken + k) * ry, 8)
                    for g in range(ry // 8):
                        value = scale_of(f) * src[pl.ds(row + 8 * g, 8), :]
                        cells.put(q, tiles, f, t, z_dst + k, half * (ry // 8) + g, value)
        return carry

    lax.fori_loop(0, fields, one_field, 0)


def fill_kernel(dims, own, got_near, q):
    cells = Cells(dims, None)
    rz = dims[2]
    rest = rz - HALO
    near = HALO + jnp.where(cells.even, 0, rest)
    fill_rows(cells, q, ((own, rz, 0, 0, HALO, rz), (got_near, HALO, 0, 1, near, HALO)))


def early_kernel(
    dims, trig, wgt, q_in, got_far, in_own, in_near, in_far, q, m, sides0, sides1
):
    del q_in
    rz, tiles = dims[2:]
    cells = Cells(dims, trig)
    cells.sides = sides0, sides1

    def pick(a, b):
        return jnp.where(cells.even, a, b)

    above = HALO + rz
    rest = rz - HALO
    fill_rows(
        cells,
        q,
        (
            (got_far, rest, 0, 1, HALO + pick(HALO, 0), rest),
            (in_own, rz, pick(0, rest), 0, pick(above, 0), HALO),
            (in_near, HALO, pick(0, rest), 1, pick(above + rest, 0), HALO - rest),
            (in_far, rest, 0, 1, pick(above, HALO - rest), rest),
        ),
    )
    last = HALO + above - 1
    cells.stage(q, None, m, tiles, 1, wgt, lo=pick(HALO + 1, 1), hi=pick(last, above - 1))


def first_kernel(dims, trig, wgt, q_in, m_in, out_own, out_got, q, m, sides0, sides1):
    del q_in, m_in
    rz, tiles = dims[2:]
    cells = Cells(dims, trig)
    cells.sides = sides0, sides1

    def pick(a, b):
        return jnp.where(cells.even, a, b)

    above = HALO + rz
    side = pick(0, above)
    fill_rows(cells, q, ((out_own, HALO, 0, 0, side, HALO), (out_got, HALO, 0, 1, side, HALO)))
    cells.clear_outside((q, tiles), (m, tiles))
    last = HALO + above - 1
    cells.stage(q, None, m, tiles, 1, wgt, lo=pick(1, above - 1), hi=pick(HALO + 1, last))
    cells.stage(m, q, q, tiles, 2, wgt)


def rest_kernel(
    dims, trig, wgt, q_in, p_own, p_out, p_in, send_ref, q, m, pq, pm, sides0, sides1
):
    del q_in
    fields, ry, rz, tiles = dims
    cells = Cells(dims, trig)
    cells.sides = sides0, sides1
    put = cells.put

    def fill_fringe(parts):
        def one_field(f, carry):
            for src, taken, half, z_dst, count in parts:
                base = (half * fields + f) * (rz + 1)
                strip = scale_of(f) * src[pl.ds(pl.multiple_of((base + rz) * ry, 8), ry), :]
                for k in range(count):
                    z = taken + k
                    row = pl.multiple_of((base + z) * ry, 8)
                    put(pq, 2, f, 0, z_dst + k, half, scale_of(f) * src[pl.ds(row, ry), :])
                    value = pltpu.roll(strip, 2 * LANES - HALO - STRIP * z, 1)
                    put(pq, 2, f, 1, z_dst + k, half, value)
            return carry

        lax.fori_loop(0, fields, one_field, 0)

    def pick(a, b):
        return jnp.where(cells.even, a, b)

    above = HALO + rz
    rest = rz - HALO
    for half in range(2):
        fill_fringe(
            (
                (p_own, 0, half, HALO, rz),
                (p_out, pick(rest, 0), half, pick(0, above), HALO),
                (p_in, pick(0, rest), half, pick(above, 0), HALO),
            )
        )
    cells.clear_outside((pq, 2), (pm, 2), (m, tiles))
    for step in range(STEPS):
        k = 2 * step + 1
        cells.stage(pq, None, pm, 2, k)
        cells.stage(pm, pq, pq, 2, k + 1)
        if step == 0:

            def relax(z, carry):
                for f in range(fields):
                    for g in range(cells.groups):
                        row = (f * tiles * cells.rows + z + 1) * cells.store + ROW0 + 8 * g
                        source = (f * 2 * cells.rows + z + 1) * cells.store + ROW0 + 8 * g
                        value = q[pl.ds(pl.multiple_of(row, 8), 8), :]
                        value = value + cells.ramp * (pq[pl.ds(pl.multiple_of(source, 8), 8), :] - value)
                        put(q, tiles, f, 0, z, g, value)
                return carry

            low = jnp.maximum(k + 1, cells.dlo)
            lax.fori_loop(low, jnp.minimum(cells.ext - k - 1, cells.dhi), relax, 0)
        else:
            if step < STEPS - 1:
                cells.stage(q, None, m, tiles, k, wgt)
                cells.stage(m, q, q, tiles, k + 1, wgt, pq)
            else:
                middle = HALO + rz // 2
                other_half = range(cells.groups // 2, cells.groups)
                cells.stage(q, None, m, tiles, k, wgt, hi=middle + 1)
                lower = dict(hi=middle, held=(0, rz // 2))
                cells.stage(m, q, None, tiles, k + 1, wgt, pq, send_ref, other_half, **lower)


def upper_kernel(dims, trig, wgt, q, m_in, pq, send_ref, m, sides0, sides1):
    del m_in
    rz, tiles = dims[2:]
    cells = Cells(dims, trig)
    cells.sides = sides0, sides1
    middle = HALO + rz // 2
    other_half = range(cells.groups // 2, cells.groups)
    cells.stage(q, None, m, tiles, HALO - 1, wgt, lo=middle + 1)
    upper = dict(lo=middle, held=(rz // 2, rz // 2))
    cells.stage(m, q, None, tiles, HALO, wgt, pq, send_ref, other_half, **upper)


def last_kernel(dims, trig, wgt, q, m, pq, mine_ref, sides0, sides1):
    cells = Cells(dims, trig)
    cells.sides = sides0, sides1
    own_half = range(cells.groups // 2)
    cells.stage(m, q, None, dims[3], HALO, wgt, pq, mine_ref, own_half, held=(0, dims[2]))


def place_kernel(dims, other, parts, *refs):
    fields, ry, rz, tiles = dims
    out_ref, block, sems = refs[-3:]
    size = ry * tiles * rz
    count = rz // parts
    slot = lax.axis_index("span")
    slot = 1 - slot if other else slot
    copies = []
    for f in range(fields):
        for y in range(ry):
            for t in range(tiles):
                for i in range(parts):
                    source = (f * tiles + t) * count * ry + y
                    value = refs[i][pl.ds(source, count, stride=ry), :]
                    block[pl.ds(((f * ry + y) * tiles + t) * rz + i * count, count), :] = value
        start = pl.multiple_of((slot * fields + f) * size, 8)
        part = block.at[pl.ds(f * size, size)]
        copies.append(pltpu.make_async_copy(part, out_ref.at[pl.ds(start, size)], sems.at[f]))
        copies[-1].start()
    for copy in copies:
        copy.wait()


def swaps(size):
    inner = [(i, i ^ 1) for i in range(size)]
    outer = [(i, i + 1 if i % 2 else i - 1) for i in range(size)]
    outer = [(i, j) for i, j in outer if 0 <= j < size]
    return inner, outer


def spread(value, axis):
    size = lax.axis_size(axis)
    at = lax.axis_index(axis)
    gap = size // 2
    while gap:
        pairs = [(i, i + gap) for i in range(0, size, 2 * gap)]
        moved = lax.ppermute(value, axis, pairs)
        value = jnp.where(at % (2 * gap) == gap, moved, value)
        gap //= 2
    return value


def body(state, turbine_x, turbine_y, yaw_index):
    slots, fields, ry, rz, x = state.shape
    tiles = x // LANES
    nt = turbine_x.shape[1]
    count = fields * ry * tiles * rz
    near_count = count // rz * HALO
    fringe_count = fields * (rz + 1) * ry
    dims = (fields, ry, rz, tiles)
    inner, outer = swaps(lax.axis_size("vert"))
    across = [(0, 1), (1, 0)]
    smem = pl.BlockSpec(memory_space=pltpu.SMEM)
    vmem = pl.BlockSpec(memory_space=pltpu.VMEM)
    hbm = pl.BlockSpec(memory_space=pl.ANY)
    whole = flat(state)

    def rows_of(n):
        return jax.ShapeDtypeStruct((n, LANES), jnp.float32)

    def block_of(n):
        return pltpu.VMEM((n, LANES), jnp.float32)

    small = pltpu.CompilerParams(vmem_limit_bytes=8 << 20)
    away_near, away_far = pl.pallas_call(
        functools.partial(away_kernel, dims),
        out_shape=[rows_of(near_count), rows_of(count - near_count)],
        in_specs=[vmem],
        out_specs=[vmem] * 2,
        compiler_params=small,
        name="away",
    )(whole)
    fringe = pl.pallas_call(
        functools.partial(fringe_kernel, dims),
        out_shape=rows_of(fringe_count),
        in_specs=[vmem],
        out_specs=vmem,
        compiler_params=small,
        name="fringe",
    )(whole)
    got_near = lax.ppermute(away_near, "span", across)
    got_far = lax.ppermute(away_far, "span", across)
    own, near = pl.pallas_call(
        functools.partial(own_kernel, dims),
        out_shape=[rows_of(count), rows_of(near_count)],
        in_specs=[vmem],
        out_specs=[vmem] * 2,
        compiler_params=small,
        name="own",
    )(whole)
    out_own = lax.ppermute(near, "vert", outer)
    in_own = lax.ppermute(own, "vert", inner)
    fringe = spread(fringe, "case")
    fringe_got = lax.ppermute(fringe, "span", across)
    out_got = lax.ppermute(got_near, "vert", outer)
    in_near = lax.ppermute(got_near, "vert", inner)
    in_far = lax.ppermute(got_far, "vert", inner)
    fringes = [jnp.concatenate([fringe, fringe_got])]
    for pairs in (outer, inner):
        fringes.append(lax.ppermute(fringes[0], "vert", pairs))
    ext = rz + 2 * HALO
    store = 2 * ROW0 + 2 * ry
    size = fields * (ext + 2) * store
    weights = (2, 2, tiles, 2 * ry // 8, 8, LANES)
    sides = [block_of(fields * 2 * tiles * 2 * ry)] * 2
    large = pltpu.CompilerParams(vmem_limit_bytes=20 << 20)
    trig, wgt = pl.pallas_call(
        functools.partial(weights_kernel, (ry, tiles, nt, slots)),
        out_shape=[
            jax.ShapeDtypeStruct((3, 8, LANES), jnp.float32),
            jax.ShapeDtypeStruct(weights, jnp.float32),
        ],
        in_specs=[smem] * 3,
        out_specs=[vmem, vmem],
        compiler_params=small,
        name="weights",
    )(turbine_x, turbine_y, yaw_index)
    q = pl.pallas_call(
        functools.partial(fill_kernel, dims),
        out_shape=rows_of(size * tiles),
        in_specs=[vmem] * 2,
        out_specs=vmem,
        compiler_params=small,
        name="fill",
    )(own, got_near)
    q, m = pl.pallas_call(
        functools.partial(early_kernel, dims),
        out_shape=[rows_of(size * tiles)] * 2,
        in_specs=[vmem] * 7,
        out_specs=[vmem] * 2,
        scratch_shapes=sides,
        input_output_aliases={2: 0},
        compiler_params=large,
        name="early",
    )(trig, wgt, q, got_far, in_own, in_near, in_far)
    q, m = pl.pallas_call(
        functools.partial(first_kernel, dims),
        out_shape=[rows_of(size * tiles)] * 2,
        in_specs=[vmem] * 6,
        out_specs=[vmem] * 2,
        scratch_shapes=sides,
        input_output_aliases={2: 0, 3: 1},
        compiler_params=large,
        name="first",
    )(trig, wgt, q, m, out_own, out_got)
    half_rows = rows_of(count // 2)
    send_low, q, m, pq = pl.pallas_call(
        functools.partial(rest_kernel, dims),
        out_shape=[half_rows] + [rows_of(size * w) for w in (tiles, tiles, 2)],
        in_specs=[vmem] * 6,
        out_specs=[vmem] * 4,
        scratch_shapes=[block_of(size * 2)] + sides,
        input_output_aliases={2: 1},
        compiler_params=large,
        name="rest",
    )(trig, wgt, q, *fringes)
    back_low = lax.ppermute(send_low, "span", across)
    send_high, m = pl.pallas_call(
        functools.partial(upper_kernel, dims),
        out_shape=[half_rows, rows_of(size * tiles)],
        in_specs=[vmem] * 5,
        out_specs=[vmem] * 2,
        scratch_shapes=sides,
        input_output_aliases={3: 1},
        compiler_params=large,
        name="upper",
    )(trig, wgt, q, m, pq)
    back_high = lax.ppermute(send_high, "span", across)
    mine = pl.pallas_call(
        functools.partial(last_kernel, dims),
        out_shape=rows_of(count),
        in_specs=[vmem] * 5,
        out_specs=vmem,
        scratch_shapes=sides,
        compiler_params=large,
        name="last",
    )(trig, wgt, q, m, pq)

    def place(other, blocks, *earlier):
        parts = len(blocks)
        return pl.pallas_call(
            functools.partial(place_kernel, dims, other, parts),
            out_shape=rows_of(slots * count),
            in_specs=[vmem] * parts + [hbm] * len(earlier),
            out_specs=hbm,
            scratch_shapes=[block_of(count), pltpu.SemaphoreType.DMA((fields,))],
            input_output_aliases={parts: 0} if earlier else {},
            compiler_params=small,
            name="place",
        )(*blocks, *earlier)

    return unflat(place(True, (back_low, back_high), place(False, (mine,))), state.shape)


def extended_2(shard, sides, width):
    for axis, dim in sides:
        size, length = (lax.axis_size(axis), shard.shape[dim])
        up = [(i, (i + 1) % size) for i in range(size)]
        down = [(j, i) for i, j in up]
        last = lax.slice_in_dim(shard, length - width, length, axis=dim)
        leading = lax.slice_in_dim(shard, 0, width, axis=dim)
        before = lax.ppermute(last, axis, up)
        after = lax.ppermute(leading, axis, down)
        shard = jnp.concatenate([before, shard, after], axis=dim)
    return shard


def entering(part, axis, combine, identity):
    place = lax.axis_index(axis)
    gathered = jax.tree.map(lambda a: lax.all_gather(a, axis), part)
    state = jax.tree.map(lambda a, e: jnp.zeros_like(a) + jnp.asarray(e, a.dtype), part, identity)

    def one(step, state):
        return combine(
            state, jax.tree.map(lambda a: lax.dynamic_index_in_dim(a, step, 0, False), gathered)
        )

    return lax.fori_loop(0, place, one, state)


def tendency(center, east, west, north, south, upper, lower, weight, cos_yaw, sin_yaw):
    grad_x = (east - west) * 0.5
    grad_y = (north - south) * 0.5
    grad_z = (upper - lower) * 0.5
    laplace = east + west + north + south + upper + lower - 6.0 * center
    vel_u = center[..., 1, :, :, :]
    vel_v = center[..., 2, :, :, :]
    vel_w = center[..., 3, :, :, :]
    dux = grad_x[..., 1, :, :, :]
    dvy = grad_y[..., 2, :, :, :]
    dwz = grad_z[..., 3, :, :, :]
    duy = grad_y[..., 1, :, :, :]
    duz = grad_z[..., 1, :, :, :]
    strain = dux * dux + dvy * dvy + dwz * dwz + duy * duy + duz * duz
    viscous = VISC * jnp.sqrt(1.0 + strain)
    speed = U_MEAN + vel_u
    flow = -(
        jnp.expand_dims(speed, -4) * grad_x
        + jnp.expand_dims(vel_v, -4) * grad_y
        + jnp.expand_dims(vel_w, -4) * grad_z
    )
    flow = flow + jnp.expand_dims(viscous, -4) * laplace
    normal = speed * cos_yaw + vel_v * sin_yaw
    thrust = THRUST * normal * jnp.abs(normal) * weight
    extra = jnp.stack(
        [
            -(dux + dvy + dwz),
            -grad_x[..., 0, :, :, :] - thrust * cos_yaw,
            -grad_y[..., 0, :, :, :] - thrust * sin_yaw,
            -grad_z[..., 0, :, :, :],
        ],
        axis=-4,
    )
    return flow + extra


def extended(fields):
    padded = extended_2(fields, (("span", 2), ("vert", 3)), 1)
    vert_at = lax.axis_index("vert")
    bottom = jnp.where(vert_at == 0, 0.0, padded[:, :, :, :1, :])
    summit = jnp.where(vert_at == lax.axis_size("vert") - 1, 0.0, padded[:, :, :, -1:, :])
    padded = jnp.concatenate([bottom, padded[:, :, :, 1:-1, :], summit], axis=3)
    return padded


def stencil(fields, padded, weight, cos_yaw, sin_yaw):
    east = jnp.roll(fields, -1, axis=4)
    west = jnp.roll(fields, 1, axis=4)
    north = padded[:, :, 2:, 1:-1, :]
    south = padded[:, :, :-2, 1:-1, :]
    upper = padded[:, :, 1:-1, 2:, :]
    lower = padded[:, :, 1:-1, :-2, :]
    return tendency(fields, east, west, north, south, upper, lower, weight, cos_yaw, sin_yaw)


def rate(fields, weight, cos_yaw, sin_yaw):
    return stencil(fields, extended(fields), weight, cos_yaw, sin_yaw)


def make_weight(turbine_x, turbine_y, along_y, along_z, total_y, total_z, active, length):
    along_x = jnp.arange(length, dtype=jnp.int32)
    hit_x = (along_x[None, None, :] == turbine_x[:, :, None]).astype(jnp.float32)
    hit_y = ((along_y[None, None, :] - turbine_y[:, :, None]) % total_y < DISK).astype(jnp.float32)
    plane = jnp.einsum("dky,dkx->dyx", hit_y, hit_x, precision=lax.Precision.HIGHEST)
    lower_half = (along_z < total_z // 2).astype(jnp.float32)
    return plane[:, :, None, :] * lower_half[None, None, :, None] * active[:, None, None, None]


def first_held(earlier, later):
    keep = earlier[1] > 0.0
    return (jnp.where(keep, earlier[0], later[0]), jnp.maximum(earlier[1], later[1]))


def body_general(state, turbine_x, turbine_y, yaw_index):
    slots = state.shape[0]
    rows_y = state.shape[2]
    rows_z = state.shape[3]
    total_y = rows_y * lax.axis_size("span")
    total_z = rows_z * lax.axis_size("vert")
    domain = lax.axis_index("case") * slots + jnp.arange(slots, dtype=jnp.int32)
    active = (domain > 0).astype(jnp.float32)
    along_y = lax.axis_index("span") * rows_y + jnp.arange(rows_y, dtype=jnp.int32)
    along_z = lax.axis_index("vert") * rows_z + jnp.arange(rows_z, dtype=jnp.int32)
    weight = make_weight(turbine_x, turbine_y, along_y, along_z, total_y, total_z, active, state.shape[4])
    angle = (yaw_index.astype(jnp.float32) - 3.5) * YAW_STEP
    cos_yaw = jnp.cos(angle)[:, None, None, None]
    sin_yaw = jnp.sin(angle)[:, None, None, None]
    width = state.shape[4] // 4
    ramp = 0.5 * (1.0 - jnp.cos(jnp.pi * (jnp.arange(width, dtype=jnp.float32) + 1.0) / width))
    case_at = lax.axis_index("case")
    for _ in range(STEPS):
        first = rate(state, weight, cos_yaw, sin_yaw)
        middle = state + TIME_STEP * first
        second = rate(middle, weight, cos_yaw, sin_yaw)
        state = state + 0.5 * TIME_STEP * (first + second)
        front = state[..., :width]
        own_fringe = front[0]
        marker = jnp.ones((), jnp.float32)
        blank = (jnp.zeros_like(own_fringe), jnp.zeros((), jnp.float32))
        passed = entering((own_fringe, marker), "case", first_held, blank)
        source = jnp.where(case_at == 0, own_fringe, passed[0])
        front = front + ramp * (source[None] - front)
        state = jnp.concatenate([front, state[..., width:]], axis=4)
    return state


def body_any(state, turbine_x, turbine_y, yaw_index):
    slots, _, ry, rz, x = state.shape
    fits = lax.axis_size("span") == 2 and slots == 2 and lax.axis_size("vert") % 2 == 0
    fits = fits and ry == 8 and rz % 8 == 0 and x == 4 * LANES
    chosen = body if fits else body_general
    return chosen(state, turbine_x, turbine_y, yaw_index)


def solution(mesh):
    return jax.shard_map(
        body_any,
        mesh=mesh,
        in_specs=(
            P("case", None, "span", "vert", None),
            P("case", None),
            P("case", None),
            P("case"),
        ),
        out_specs=P("case", None, "span", "vert", None),
        check_vma=False,
    )
```
